32 devices in a mesh: dp: 2 (over y), mp: 4 (over x, core), tensor: 4 (over z).
Axes of the slice: x: 2, y: 2, z: 4, core: 2. Of those that a mesh axis runs over, the one named last changes fastest.
Arguments:
- tokens: bfloat16 [4096, 2048], P(('dp', 'mp', 'tensor')), may hold values from -6 to 6
- norm_gain: float32 [2048], replicated, may hold values from 0.1 to 1.9
- w_proj: bfloat16 [4, 2048, 2048], P(None, 'mp', 'tensor'), may hold values from -0.125 to 0.125
- w_beta: bfloat16 [2048, 16], P('mp', 'tensor'), may hold values from -0.125 to 0.125
- conv_weight: float32 [3, 4, 4, 4, 128], P(None, None, 'tensor', 'mp'), may hold values from -3 to 3
- out_gain: float32 [128], replicated, may hold values from 0.1 to 1.9
- w_out: bfloat16 [2048, 2048], P('tensor', 'mp'), may hold values from -0.25 to 0.25
- mlp_gain: float32 [2048], replicated, may hold values from 0.1 to 1.9
- w_in: bfloat16 [2, 2048, 5632], P(None, 'mp', 'tensor'), may hold values from -0.125 to 0.125
- w_down: bfloat16 [5632, 2048], P('tensor', 'mp'), may hold values from -0.078125 to 0.078125
- cotangent: bfloat16 [4096, 2048], P(('dp', 'mp', 'tensor')), may hold values from -6 to 6
- starts: int32 [2, 8], P('dp'), may hold values from 0 to 2047, as said below
- lengths: int32 [2], P('dp'), may hold values from 1024 to 2048
Outputs:
- output: bfloat16 [4096, 2048], P(('dp', 'mp', 'tensor'))
- d_tokens: float32 [4096, 2048], P(('dp', 'mp', 'tensor'))
- g_norm_gain: float32 [2048], replicated
- g_proj: float32 [4, 2048, 2048], P(None, 'mp', 'tensor')
- g_beta: float32 [2048, 16], P('mp', 'tensor')
- g_conv: float32 [3, 4, 4, 4, 128], P(None, None, 'tensor', 'mp')
- g_out_gain: float32 [128], replicated
- g_out: float32 [2048, 2048], P('tensor', 'mp')
- g_mlp_gain: float32 [2048], replicated
- g_in: float32 [2, 2048, 5632], P(None, 'mp', 'tensor')
- g_down: float32 [5632, 2048], P('tensor', 'mp')
- state_norm: float32 [], replicated
The draws below stay inside these ranges and needn't reach their ends.
Inputs may be any that keep to these rules, and one draw needn't show every extreme that they name: `starts`: row s rises strictly from 0 and lists where the 8 documents of sequence s begin.
All inputs are finite; a program needn't handle non-finite values.
Results may differ from the reference program's by a relative error of at most 0.014.
Values may be sent and summed in bfloat16 or wider, within the bound.
No kernel may reach another device: no remote copies, remote signals or barrier semaphores. Data moves between devices by JAX's collectives and lax.ppermute only.
A program may use at most 256 MiB of HBM per device.

```python
import jax
import jax.numpy as jnp
from jax import lax

D = 2048
HEADS = 16
DK = 128
FF = 5632
KCONV = 4
BLOCK = 64
LENGTH = 2048
NDOCS = 8
SEQS = 2
TOKENS = 4096
N_MP = 4
N_TENSOR = 4


def draw_starts(key, part):
    row_keys = jax.random.split(jax.random.fold_in(key, 17), SEQS)

    def one_row(row_key):
        chosen = jax.random.permutation(row_key, LENGTH - 2)[:NDOCS - 1] + 1
        return jnp.sort(chosen).astype(jnp.int32)
    inner = jax.vmap(one_row)(row_keys)
    row_ids = jnp.arange(SEQS, dtype=jnp.int32)[:, None]
    col_ids = jnp.arange(NDOCS - 1, dtype=jnp.int32)[None, :]
    inner = jnp.where((row_ids == 0) & (col_ids == NDOCS - 2), LENGTH - 1, inner)
    return jnp.concatenate([jnp.zeros((SEQS, 1), jnp.int32), inner], axis=1).astype(jnp.int32)


def block_scale(rng, extent, cuts, smallest, top_value):
    def one(axis_at, blocks):
        steps = jax.random.uniform(jax.random.fold_in(jax.random.fold_in(rng, 6), axis_at), (blocks,), jnp.float32, smallest / len(cuts), top_value / len(cuts))
        return jnp.repeat(jnp.exp(steps), extent[axis_at] // blocks).reshape((-1,) + (1,) * (len(extent) - axis_at - 1))

    loudness = one(*cuts[0])
    for cut in cuts[1:]:
        loudness = loudness * one(*cut)
    return loudness


def normal_values(key, dims, scale, bound, cuts=(), kind=jnp.bfloat16):
    drawn = scale * jax.random.normal(key, dims, jnp.float32)
    if cuts:
        drawn = drawn * block_scale(key, dims, cuts, -0.22, 0.18)
    return jnp.clip(drawn, -bound, bound).astype(kind)


def setup_inputs(seed: int = 0) -> dict:
    seeds = jax.random.split(jax.random.key(seed), 14)
    tokens = normal_values(seeds[0], (TOKENS, D), 1.0, 6.0, ((0, 32),))
    norm_gain = jnp.clip(1.0 + 0.18 * jax.random.normal(seeds[1], (D,), jnp.float32), 0.1, 1.9)
    w_proj = normal_values(seeds[2], (4, D, D), D ** -0.5, 0.125, ((1, 4), (2, 4)))
    w_beta = normal_values(seeds[3], (D, HEADS), D ** -0.5, 0.125, ((0, 4), (1, 4)))
    conv_weight = normal_values(seeds[4], (3, KCONV, N_TENSOR, N_MP, HEADS // (N_TENSOR * N_MP) * DK), KCONV ** -0.5, 3.0, ((2, 4), (3, 4)), jnp.float32)
    out_gain = jnp.clip(1.0 + 0.18 * jax.random.normal(seeds[5], (DK,), jnp.float32), 0.1, 1.9)
    w_out = normal_values(seeds[6], (D, D), (D // 4) ** -0.5, 0.25, ((0, 4), (1, 4)))
    mlp_gain = jnp.clip(1.0 + 0.18 * jax.random.normal(seeds[7], (D,), jnp.float32), 0.1, 1.9)
    w_in = normal_values(seeds[8], (2, D, FF), D ** -0.5, 0.125, ((1, 4), (2, 4)))
    w_down = normal_values(seeds[9], (FF, D), FF ** -0.5, 0.078125, ((0, 4), (1, 4)))
    cotangent = normal_values(seeds[10], (TOKENS, D), 1.0, 6.0, ((0, 32),))
    starts = draw_starts(jax.random.fold_in(seeds[13], 71), 0)
    lengths = jax.random.randint(seeds[12], (SEQS,), LENGTH // 2, LENGTH + 1).astype(jnp.int32)
    return {"tokens": tokens, "norm_gain": norm_gain, "w_proj": w_proj, "w_beta": w_beta, "conv_weight": conv_weight, "out_gain": out_gain, "w_out": w_out, "mlp_gain": mlp_gain, "w_in": w_in, "w_down": w_down, "cotangent": cotangent, "starts": starts, "lengths": lengths}


@jax.custom_vjp
def low(v):
    return lax.optimization_barrier(v.astype(jnp.bfloat16)).astype(jnp.float32)

@jax.custom_vjp
def low_back(v):
    return v

def low_keep(v):
    return (low(v), None)

def low_pass(kept, grad):
    return (grad,)

def back_keep(v):
    return (v, None)

def back_low(kept, grad):
    return (low(grad),)
low.defvjp(low_keep, low_pass)
low_back.defvjp(back_keep, back_low)

def rms_rows(values, epsilon):
    return values * lax.rsqrt(lax.optimization_barrier(jnp.mean(values * values, axis=-1, keepdims=True)) + epsilon)

def short_conv(values, taps, doc_ids):
    taps_count = taps.shape[0]
    summed = values * taps[taps_count - 1]
    for offset in range(1, taps_count):
        shifted = jnp.concatenate([jnp.zeros((offset, values.shape[1]), jnp.float32), values[:-offset]], axis=0)
        prior_doc = jnp.concatenate([jnp.full((offset,), -1, jnp.int32), doc_ids[:-offset]])
        summed = summed + jnp.where((prior_doc == doc_ids)[:, None], shifted, 0.0) * taps[taps_count - 1 - offset]
    return summed

def block_delta(query, key_vec, value, beta, doc_ids):
    highest = lax.Precision.HIGHEST
    seq_len = query.shape[0]
    width = BLOCK
    count = seq_len // width
    q_blocks = query.reshape(count, width, -1)
    k_blocks = key_vec.reshape(count, width, -1)
    v_blocks = value.reshape(count, width, -1)
    b_blocks = beta.reshape(count, width)
    d_blocks = doc_ids.reshape(count, width)
    prior_doc = jnp.concatenate([jnp.full((1,), -1, jnp.int32), doc_ids[width - 1:-1:width]])
    keep_rows = (d_blocks == prior_doc[:, None]).astype(jnp.float32)
    same_doc = d_blocks[:, :, None] == d_blocks[:, None, :]
    row_ids = lax.broadcasted_iota(jnp.int32, (width, width), 0)
    col_ids = lax.broadcasted_iota(jnp.int32, (width, width), 1)
    strict_mask = same_doc & (row_ids > col_ids)[None]
    upto_mask = same_doc & (row_ids >= col_ids)[None]
    gram_mat = jnp.einsum('mik,mjk->mij', k_blocks, k_blocks, precision=highest)
    neg_mat = jnp.where(strict_mask, -b_blocks[:, :, None] * gram_mat, 0.0)
    inverse = jnp.eye(width, dtype=jnp.float32)[None] + neg_mat
    power_mat = neg_mat
    for rounds in range(width.bit_length() - 2):
        power_mat = jnp.einsum('mij,mjk->mik', power_mat, power_mat, precision=highest)
        inverse = inverse + jnp.einsum('mij,mjk->mik', inverse, power_mat, precision=highest)
    w_mat = jnp.einsum('mij,mjk->mik', inverse, (b_blocks * keep_rows)[:, :, None] * k_blocks, precision=highest)
    u_mat = jnp.einsum('mij,mjk->mik', inverse, b_blocks[:, :, None] * v_blocks, precision=highest)
    scores = jnp.where(upto_mask, jnp.einsum('mik,mjk->mij', q_blocks, k_blocks, precision=highest), 0.0)
    last_doc = (d_blocks == d_blocks[:, -1:]).astype(jnp.float32)

    def advance(state, pieces):
        w_part, u_part, q_part, s_part, k_part, keep_part, last_part = pieces
        pseudo = u_part - jnp.dot(w_part, state, precision=highest)
        result = keep_part[:, None] * jnp.dot(q_part, state, precision=highest) + jnp.dot(s_part, pseudo, precision=highest)
        new_state = keep_part[-1] * state + jnp.dot((k_part * last_part[:, None]).T, pseudo, precision=highest)
        return (new_state, (result, jnp.sqrt(jnp.sum(new_state * new_state) + 1e-12)))
    start_state = jnp.zeros((k_blocks.shape[2], v_blocks.shape[2]), jnp.float32)
    final_state, (results, norm_list) = lax.scan(jax.checkpoint(advance), start_state, (w_mat, u_mat, q_blocks, scores, k_blocks, keep_rows, last_doc))
    return (results.reshape(seq_len, -1), jnp.sum(norm_list))

def head_piece(pieces, beta_logit, conv_flat, gain_row, doc_ids, valid):
    seq_len = pieces.shape[1]
    head_count = beta_logit.shape[1]
    conv_q = short_conv(pieces[0], conv_flat[0], doc_ids)
    conv_k = short_conv(pieces[1], conv_flat[1], doc_ids)
    conv_v = short_conv(pieces[2], conv_flat[2], doc_ids)
    query = jax.nn.silu(conv_q).reshape(seq_len, head_count, -1)
    query = query * lax.rsqrt(lax.optimization_barrier(jnp.sum(query * query, axis=-1, keepdims=True)) + 1e-06)
    key_rows = jax.nn.silu(conv_k).reshape(seq_len, head_count, -1)
    key_rows = key_rows * lax.rsqrt(lax.optimization_barrier(jnp.sum(key_rows * key_rows, axis=-1, keepdims=True)) + 1e-06)
    values = jax.nn.silu(conv_v).reshape(seq_len, head_count, -1)
    beta_rows = jax.nn.sigmoid(beta_logit) * valid[:, None]
    mixed_out, norm_sums = jax.vmap(block_delta, in_axes=(1, 1, 1, 1, None), out_axes=(1, 0))(query, key_rows, values, beta_rows, doc_ids)
    gate_rows = pieces[3].reshape(seq_len, head_count, -1)
    mixed = rms_rows(mixed_out, 1e-05) * gain_row * jax.nn.silu(gate_rows) * valid[:, None, None]
    return (mixed.reshape(seq_len, -1), jnp.sum(norm_sums))

def layer(inputs, norm_gain, w_proj, w_beta, conv_flat, out_gain, w_out, mlp_gain, w_in, w_down, doc_ids, valid):
    highest = lax.Precision.HIGHEST
    normed = low(rms_rows(inputs, 1e-05) * norm_gain)
    projected = low_back(low(jnp.einsum('nd,sdc->snc', normed, w_proj, precision=highest)))
    beta_logit = low_back(low(jnp.dot(normed, w_beta, precision=highest)))
    mixed, norm_total = head_piece(projected, beta_logit, conv_flat, out_gain, doc_ids, valid)
    mixed = low_back(low(mixed))
    branch = low_back(jnp.dot(mixed, w_out, precision=highest))
    middle = inputs + branch
    normed_two = low(rms_rows(middle, 1e-05) * mlp_gain)
    gate_up = jnp.einsum('nd,sdf->snf', normed_two, w_in, precision=highest)
    gate_val = low_back(gate_up[0])
    up_val = low_back(gate_up[1])
    hidden = low(jax.nn.silu(gate_val) * up_val)
    return (middle + jnp.dot(hidden, w_down, precision=highest), norm_total)

def reference(tokens, norm_gain, w_proj, w_beta, conv_weight, out_gain, w_out, mlp_gain, w_in, w_down, cotangent, starts, lengths):
    params = (norm_gain.astype(jnp.float32), w_proj.astype(jnp.float32), w_beta.astype(jnp.float32), conv_weight.astype(jnp.float32).reshape(3, KCONV, D), out_gain.astype(jnp.float32), w_out.astype(jnp.float32), mlp_gain.astype(jnp.float32), w_in.astype(jnp.float32), w_down.astype(jnp.float32))
    seq_inputs = tokens.astype(jnp.float32).reshape(SEQS, LENGTH, D)
    seq_cot = cotangent.astype(jnp.float32).reshape(SEQS, LENGTH, D)
    places = jnp.arange(LENGTH, dtype=jnp.int32)

    def per_sequence(carried, seq_items):
        seq_in, seq_grad, seq_starts, seq_length = seq_items
        doc_ids = lax.optimization_barrier(jnp.sum((seq_starts[:, None] <= places[None, :]).astype(jnp.int32), axis=0)) - 1
        valid = (places < seq_length).astype(jnp.float32)

        def run(inputs, gain_a, proj_a, beta_a, conv_a, gain_b, out_a, gain_c, in_a, down_a):
            return layer(inputs, gain_a, proj_a, beta_a, conv_a, gain_b, out_a, gain_c, in_a, down_a, doc_ids, valid)
        result, backward, norm_total = jax.vjp(run, seq_in, *params, has_aux=True)
        grads = backward(seq_grad)
        summed = tuple((old + new for old, new in zip(carried[0], grads[1:])))
        return ((summed, carried[1] + norm_total), (result.astype(jnp.bfloat16), grads[0]))
    zero_grads = tuple((jnp.zeros_like(item) for item in params))
    (grad_sums, norm_sum), (outputs, input_grads) = lax.scan(per_sequence, (zero_grads, jnp.zeros((), jnp.float32)), (seq_inputs, seq_cot, starts, lengths))
    state_norm = norm_sum / (HEADS * SEQS * (LENGTH // BLOCK))
    return (outputs.reshape(TOKENS, D), input_grads.reshape(TOKENS, D), grad_sums[0], grad_sums[1], grad_sums[2], grad_sums[3].reshape(conv_weight.shape), grad_sums[4], grad_sums[5], grad_sums[6], grad_sums[7], grad_sums[8], state_norm)
```

```python
import jax
import jax.numpy as jnp
from jax import lax
from jax.experimental import pallas as pl
from jax.experimental.pallas import tpu as pltpu
from jax.sharding import PartitionSpec as P

HEADS = 16


def shortened(value):

    def short(part):
        return part.astype(jnp.bfloat16) if part.dtype == jnp.float32 else part

    return jax.tree.map(short, value)


def rms_rows(values, epsilon):
    return values * lax.rsqrt(jnp.mean(values * values, axis=-1, keepdims=True) + epsilon)


def scaled_norm(values, gain_row):
    return rms_rows(values, 1e-05) * gain_row


BLOCK = 64
PAIR = 2 * BLOCK
LANES = 128
f32 = jnp.float32
bf16 = jnp.bfloat16


def halves(a):
    hi = a.astype(bf16)
    return hi, (a - hi.astype(f32)).astype(bf16)


def product(a, b, dims):
    return lax.dot_general(a, b, (dims, ((), ())), preferred_element_type=f32)


def close_dot(a, b, dims=((1,), (0,))):
    a_hi, a_lo = a if isinstance(a, tuple) else halves(a)
    b_hi, b_lo = b if isinstance(b, tuple) else halves(b)
    return product(a_hi, b_hi, dims) + (product(a_hi, b_lo, dims) + product(a_lo, b_hi, dims))


NN = ((1,), (0,))
NT = ((1,), (1,))
TN = ((0,), (0,))


def doc_start(places, starts_ref):
    found = jnp.zeros_like(places)
    for j in range(1, starts_ref.shape[0]):
        begin = starts_ref[j]
        found = jnp.where(places >= begin, begin, found)
    return found


def place_rows(base, rows, width=LANES):
    return base + lax.broadcasted_iota(jnp.int32, (rows, width), 0)


def pair_masks(base, begins):
    rows = lax.broadcasted_iota(jnp.int32, (PAIR, PAIR), 0)
    cols = lax.broadcasted_iota(jnp.int32, (PAIR, PAIR), 1)
    heads = (rows // BLOCK) * BLOCK
    lower = jnp.maximum(begins - base, heads)
    upto = (cols >= lower) & (cols <= rows)
    strict = (cols >= lower) & (cols < rows)
    keep = begins < base + heads
    return upto, strict, keep, (rows == cols).astype(f32)


def forward_body(starts_ref, length_ref, x_ref, before_ref, logit_ref, taps_ref, gain_ref,
                 mixed_ref, norm_ref, conv_ref, wu_ref, t_ref, a_ref, c_ref, m_ref, s_ref, o_ref,
                 state_ref, square_ref):
    step = pl.program_id(0)
    rows = x_ref.shape[1]
    base = step * rows

    @pl.when(step == 0)
    def _():
        state_ref[...] = jnp.zeros_like(state_ref)

    places = place_rows(base, rows)
    begins = doc_start(places, starts_ref)
    since = places - begins
    valid = (places < length_ref[0]).astype(f32)
    parts = []
    for p in range(3):
        now = x_ref[p].astype(f32)
        tall = jnp.concatenate([before_ref[p].astype(f32), now], axis=0)
        lead = tall.shape[0] - rows
        summed = now * taps_ref[p, 3:4, :]
        for j in range(1, 4):
            moved = pltpu.roll(tall, j, 0)[lead:]
            summed = summed + jnp.where(since >= j, moved, 0.0) * taps_ref[p, 3 - j:4 - j, :]
        conv_ref[p] = summed
        act = summed * jax.nn.sigmoid(summed)
        if p < 2:
            act = act * lax.rsqrt(jnp.sum(act * act, axis=1, keepdims=True) + 1e-06)
        parts.append(act)
    beta = jax.nn.sigmoid(logit_ref[...].astype(f32)) * valid
    gates = x_ref[3].astype(f32)
    gates = gates * jax.nn.sigmoid(gates) * valid * gain_ref[...]
    pairs = rows // PAIR
    blocks = []
    for g in range(pairs):
        at = slice(g * PAIR, (g + 1) * PAIR)
        start = base + g * PAIR
        q, k, v, b = parts[0][at], parts[1][at], parts[2][at], beta[at]
        upto, strict, keep, eye = pair_masks(start, begins[at])
        kb = b * k
        k_two = halves(k)
        neg = jnp.where(strict, -close_dot(kb, k_two, NT), 0.0)
        inverse = eye + neg
        power = neg
        for _ in range(BLOCK.bit_length() - 2):
            power_two = halves(power)
            power = close_dot(power_two, power_two)
            inverse = inverse + close_dot(inverse, power)
        wu = close_dot(inverse, jnp.concatenate([jnp.where(keep, kb, 0.0), b * v], axis=1))
        wu_two = halves(wu)
        scores = jnp.where(upto, close_dot(q, k_two, NT), 0.0)
        cd = close_dot(scores, wu_two)
        c = jnp.where(keep, q, 0.0) - cd[:, :LANES]
        wu_ref[at] = wu
        t_ref[at] = inverse
        a_ref[at] = scores
        c_ref[at] = c
        for h in range(2):
            inner = slice(h * BLOCK, (h + 1) * BLOCK)
            first = start + h * BLOCK
            final = doc_start(first + BLOCK - 1, starts_ref)
            tail = place_rows(first, BLOCK) >= final
            k_last = jnp.where(tail, k[inner], 0.0)
            mb = close_dot(k_last, (wu_two[0][inner], wu_two[1][inner]), TN)
            kept = jnp.where(final < first, 1.0, 0.0)
            m = kept * eye - mb[:, :LANES]
            m_ref[g * 2 + h] = m
            blocks.append((halves(m), mb[:, LANES:], c[inner], cd[inner, LANES:]))
    state = state_ref[...]
    results = []
    for n, (m_two, addend, c, d) in enumerate(blocks):
        s_ref[n] = state
        s_two = halves(state)
        results.append(close_dot(c, s_two) + d)
        state = close_dot(m_two, s_two) + addend
        square_ref[pl.ds(step * len(blocks) + n, 1), :] = jnp.sum(state * state, axis=0, keepdims=True)
    state_ref[...] = state
    result = jnp.concatenate(results, axis=0)
    o_ref[...] = result
    unit = result * lax.rsqrt(jnp.mean(result * result, axis=1, keepdims=True) + 1e-05)
    mixed_ref[...] = (unit * gates).astype(bf16)

    @pl.when(step == pl.num_programs(0) - 1)
    def _():
        sizes = jnp.sqrt(jnp.sum(square_ref[...], axis=1, keepdims=True) + 1e-12)
        norm_ref[...] = jnp.broadcast_to(jnp.sum(sizes, axis=0, keepdims=True), norm_ref.shape)


def backward_body(starts_ref, length_ref, x_ref, logit_ref, taps_ref, gain_ref, grad_ref,
                  conv_ref, wu_ref, t_ref, a_ref, c_ref, m_ref, s_ref, o_ref,
                  dx_ref, dlogit_ref, dtaps_ref, dgain_ref, dstate_ref, after_ref):
    step = pl.program_id(0)
    rows = x_ref.shape[1]
    base = (pl.num_programs(0) - 1 - step) * rows

    @pl.when(step == 0)
    def _():
        dstate_ref[...] = jnp.zeros_like(dstate_ref)
        after_ref[...] = jnp.zeros_like(after_ref)
        dtaps_ref[...] = jnp.zeros_like(dtaps_ref)
        dgain_ref[...] = jnp.zeros_like(dgain_ref)

    lead = after_ref.shape[1]
    places_tall = place_rows(base, rows + lead)
    begins_tall = doc_start(places_tall, starts_ref)
    since_tall = places_tall - begins_tall
    places, begins = places_tall[:rows], begins_tall[:rows]
    valid = (places < length_ref[0]).astype(f32)
    gain = gain_ref[...]
    gate = x_ref[3].astype(f32)
    gate_sig = jax.nn.sigmoid(gate)
    gate_act = gate * gate_sig
    o = o_ref[...]
    r = lax.rsqrt(jnp.mean(o * o, axis=1, keepdims=True) + 1e-05)
    unit = o * r
    grad = grad_ref[...].astype(f32) * valid
    gu = grad * unit
    dgain_ref[0:1, :] += jnp.sum(gu * gate_act, axis=0, keepdims=True)
    dx_ref[3] = (gu * gain * (gate_sig * (1.0 + gate * (1.0 - gate_sig)))).astype(bf16)
    dunit = grad * gain * gate_act
    d_o = r * (dunit - unit * jnp.mean(dunit * unit, axis=1, keepdims=True))
    convs, sigs, acts, scales, units = [], [], [], [], []
    for p in range(3):
        conv = conv_ref[p]
        sig = jax.nn.sigmoid(conv)
        act = conv * sig
        convs.append(conv)
        sigs.append(sig)
        if p < 2:
            scale = lax.rsqrt(jnp.sum(act * act, axis=1, keepdims=True) + 1e-06)
            scales.append(scale)
            units.append(act * scale)
        else:
            units.append(act)
    logit_sig = jax.nn.sigmoid(logit_ref[...].astype(f32))
    beta = logit_sig * valid
    pairs = rows // PAIR
    do_two = halves(d_o)
    pieces = [None] * (2 * pairs)
    for n in range(2 * pairs):
        inner = slice(n * BLOCK, (n + 1) * BLOCK)
        pieces[n] = close_dot(c_ref[inner, :], (do_two[0][inner], do_two[1][inner]), TN)
    dstate = dstate_ref[...]
    dstates = [None] * (2 * pairs)
    for n in reversed(range(2 * pairs)):
        d_two = halves(dstate)
        dstates[n] = d_two
        dstate = close_dot(m_ref[n], d_two, TN) + pieces[n]
    dstate_ref[...] = dstate
    grads = [[], [], []]
    dbetas = []
    for g in range(pairs):
        at = slice(g * PAIR, (g + 1) * PAIR)
        start = base + g * PAIR
        q, k, v, b = units[0][at], units[1][at], units[2][at], beta[at]
        upto, strict, keep, eye = pair_masks(start, begins[at])
        wu = wu_ref[at, :]
        wu_two = halves(wu)
        a_two = halves(a_ref[at, :])
        k_two = halves(k)
        do_pair = (do_two[0][at], do_two[1][at])
        p_rows, dp_rows, dq_rows, dk_rows, dw_rows = [], [], [], [], []
        later = close_dot(a_two, do_pair, TN)
        for h in range(2):
            n = g * 2 + h
            inner = slice(h * BLOCK, (h + 1) * BLOCK)
            first = start + h * BLOCK
            final = doc_start(first + BLOCK - 1, starts_ref)
            tail = place_rows(first, BLOCK) >= final
            s_two = halves(s_ref[n])
            ds_two = dstates[n]
            wu_in = (wu_two[0][inner, :LANES], wu_two[1][inner, :LANES])
            p = wu[inner, LANES:] - close_dot(wu_in, s_two)
            p_two = halves(p)
            k_last = jnp.where(tail, k[inner], 0.0)
            dp = later[inner] + close_dot(k_last, ds_two)
            dp_two = halves(dp)
            p_rows.append(p_two)
            dp_rows.append(dp)
            do_in = (do_pair[0][inner], do_pair[1][inner])
            dq_rows.append(close_dot(do_in, s_two, NT))
            dk_rows.append(jnp.where(tail, close_dot(p_two, ds_two, NT), 0.0))
            dw_rows.append(-close_dot(dp_two, s_two, NT))
        p_two = tuple(jnp.concatenate([p_rows[0][i], p_rows[1][i]], axis=0) for i in range(2))
        dp = jnp.concatenate(dp_rows, axis=0)
        da_two = halves(jnp.where(upto, close_dot(do_pair, p_two, NT), 0.0))
        q_two = halves(q)
        dq = jnp.where(keep, jnp.concatenate(dq_rows, axis=0), 0.0) + close_dot(da_two, k_two)
        dk = jnp.concatenate(dk_rows, axis=0) + close_dot(da_two, q_two, TN)
        dwu = jnp.concatenate([jnp.concatenate(dw_rows, axis=0), dp], axis=1)
        dbkv = close_dot(t_ref[at, :], dwu, TN)
        dl_two = halves(jnp.where(strict, -close_dot(dbkv, wu_two, NT), 0.0))
        dkb = close_dot(dl_two, k_two) + jnp.where(keep, dbkv[:, :LANES], 0.0)
        dbv = dbkv[:, LANES:]
        dk = dk + b * dkb + close_dot(dl_two, b * k, TN)
        grads[0].append(dq)
        grads[1].append(dk)
        grads[2].append(b * dbv)
        dbetas.append(jnp.sum(k * dkb + v * dbv, axis=1, keepdims=True))
    dbeta = jnp.concatenate(dbetas, axis=0)
    dlogit_ref[...] = dbeta * (beta * (1.0 - logit_sig))[:, :1]
    for p in range(3):
        dact = jnp.concatenate(grads[p], axis=0)
        if p < 2:
            dact = scales[p] * (dact - units[p] * jnp.sum(dact * units[p], axis=1, keepdims=True))
        dconv = dact * (sigs[p] * (1.0 + convs[p] * (1.0 - sigs[p])))
        tall = jnp.concatenate([dconv, after_ref[p]], axis=0)
        after_ref[p] = dconv[:lead]
        x = x_ref[p].astype(f32)
        dx = dconv * taps_ref[p, 3:4, :]
        dtaps_ref[p, 3:4, :] += jnp.sum(dconv * x, axis=0, keepdims=True)
        for j in range(1, 4):
            moved = pltpu.roll(jnp.where(since_tall >= j, tall, 0.0), rows + lead - j, 0)[:rows]
            dx = dx + moved * taps_ref[p, 3 - j:4 - j, :]
            dtaps_ref[p, 3 - j:4 - j, :] += jnp.sum(moved * x, axis=0, keepdims=True)
        dx_ref[p] = dx.astype(bf16)


def head_forward(x, logit, taps, gain, starts, length, rows=256):
    count = x.shape[1]
    rows = min(rows, count)
    steps = count // rows
    per = rows // BLOCK
    whole = lambda shape: pl.BlockSpec(shape, lambda i, *_: (0,) * len(shape))
    flat = lambda width: pl.BlockSpec((rows, width), lambda i, *_: (i, 0))
    square = pl.BlockSpec((per, LANES, LANES), lambda i, *_: (i, 0, 0))
    halo = 16
    s = jax.ShapeDtypeStruct
    outs = pl.pallas_call(
        forward_body,
        grid_spec=pltpu.PrefetchScalarGridSpec(
            num_scalar_prefetch=2,
            grid=(steps,),
            in_specs=[
                pl.BlockSpec((4, rows, LANES), lambda i, *_: (0, i, 0)),
                pl.BlockSpec((3, halo, LANES), lambda i, *_: (0, jnp.maximum(i * (rows // halo) - 1, 0), 0)),
                pl.BlockSpec((rows, 1), lambda i, *_: (i, 0)),
                whole(taps.shape),
                whole(gain.shape),
            ],
            out_specs=[
                flat(LANES),
                whole((8, LANES)),
                pl.BlockSpec((3, rows, LANES), lambda i, *_: (0, i, 0)),
                flat(2 * LANES), flat(PAIR), flat(PAIR), flat(LANES),
                square, square, flat(LANES),
            ],
            scratch_shapes=[pltpu.VMEM((LANES, LANES), f32), pltpu.VMEM((count // BLOCK, LANES), f32)],
        ),
        out_shape=[
            s((count, LANES), bf16), s((8, LANES), f32), s((3, count, LANES), f32),
            s((count, 2 * LANES), f32), s((count, PAIR), f32), s((count, PAIR), f32), s((count, LANES), f32),
            s((count // BLOCK, LANES, LANES), f32), s((count // BLOCK, LANES, LANES), f32),
            s((count, LANES), f32),
        ],
        name="head_forward",
    )(starts, length, x, x, logit, taps, gain)
    return outs[0], outs[1][0, 0], tuple(outs[2:])


def head_backward(grad, x, logit, taps, gain, starts, length, kept, rows=256):
    count = x.shape[1]
    rows = min(rows, count)
    steps = count // rows
    per = rows // BLOCK
    whole = lambda shape: pl.BlockSpec(shape, lambda i, *_: (0,) * len(shape))
    flat = lambda width: pl.BlockSpec((rows, width), lambda i, *_: (steps - 1 - i, 0))
    deep = lambda d: pl.BlockSpec((d, rows, LANES), lambda i, *_: (0, steps - 1 - i, 0))
    square = pl.BlockSpec((per, LANES, LANES), lambda i, *_: (steps - 1 - i, 0, 0))
    s = jax.ShapeDtypeStruct
    return pl.pallas_call(
        backward_body,
        grid_spec=pltpu.PrefetchScalarGridSpec(
            num_scalar_prefetch=2,
            grid=(steps,),
            in_specs=[
                deep(4), flat(1), whole(taps.shape), whole(gain.shape), flat(LANES),
                deep(3), flat(2 * LANES), flat(PAIR), flat(PAIR), flat(LANES), square, square, flat(LANES),
            ],
            out_specs=[deep(4), flat(1), whole(taps.shape), whole((8, LANES))],
            scratch_shapes=[pltpu.VMEM((LANES, LANES), f32), pltpu.VMEM((3, 8, LANES), f32)],
        ),
        out_shape=[s((4, count, LANES), bf16), s((count, 1), f32), s(taps.shape, f32), s((8, LANES), f32)],
        name="head_backward",
    )(starts, length, x, logit, taps, gain, grad, *kept)

def spread(values):
    return lax.all_gather(values, "tensor", axis=0, tiled=True)


def collect(values):
    return lax.psum_scatter(values, "tensor", scatter_dimension=0, tiled=True)


def shards(
    tokens,
    norm_gain,
    w_proj,
    w_beta,
    conv_weight,
    out_gain,
    w_out,
    mlp_gain,
    w_in,
    w_down,
    cotangent,
    starts,
    lengths,
):
    f32 = jnp.float32
    bf16 = jnp.bfloat16
    full_proj, full_beta, full_out, full_in, full_down = (
        lax.all_gather(w_proj, "mp", axis=1, tiled=True),
        lax.all_gather(w_beta, "mp", axis=0, tiled=True),
        lax.all_gather(w_out, "mp", axis=1, tiled=True),
        lax.all_gather(w_in, "mp", axis=1, tiled=True),
        lax.all_gather(w_down, "mp", axis=1, tiled=True),
    )
    inputs = tokens.astype(f32)
    normed_local, first_back = jax.vjp(scaled_norm, inputs, norm_gain)
    normed = spread(normed_local.astype(bf16))
    projected = jnp.einsum("nd,sdc->snc", normed, full_proj, preferred_element_type=f32).astype(
        bf16
    )
    beta_logit = jnp.dot(normed, full_beta, preferred_element_type=f32).astype(bf16)[None]
    heads_proj, heads_beta = (
        lax.all_to_all(projected, "mp", split_axis=2, concat_axis=1, tiled=True),
        lax.all_to_all(beta_logit, "mp", split_axis=2, concat_axis=1, tiled=True),
    )
    seq_count = starts.shape[0]
    seq_len = heads_proj.shape[1] // seq_count
    channels = heads_proj.shape[2]
    assert seq_count == 1 and channels == LANES
    conv_flat = conv_weight.reshape(3, conv_weight.shape[1], channels)
    logit = heads_beta[0].astype(f32)
    head_args = (heads_proj, logit, conv_flat, out_gain[None], starts[0], lengths)
    mixed_low, norm_total, kept = head_forward(*head_args)
    mixed_tok = lax.all_to_all(mixed_low, "mp", split_axis=0, concat_axis=1, tiled=True)
    branch = collect(jnp.dot(mixed_tok, full_out, preferred_element_type=f32))
    middle = inputs + branch
    normed_local_two, second_back = jax.vjp(scaled_norm, middle, mlp_gain)
    normed_two = spread(normed_local_two.astype(bf16))
    gate_up = jnp.einsum("nd,sdf->snf", normed_two, full_in, preferred_element_type=f32)
    gate_val = gate_up[0]
    up_val = gate_up[1]
    activated = jax.nn.silu(gate_val)
    hidden = (activated * up_val).astype(bf16)
    feed_out = collect(jnp.dot(hidden, full_down, preferred_element_type=f32))
    output = (middle + feed_out).astype(bf16)
    grad_rows_all = spread(cotangent)
    g_down = jnp.einsum("nf,nd->fd", hidden, grad_rows_all, preferred_element_type=f32)
    d_hidden = jnp.einsum("nd,fd->nf", grad_rows_all, full_down, preferred_element_type=f32)
    sigma = jax.nn.sigmoid(gate_val)
    d_gate = (d_hidden * up_val * sigma * (1.0 + gate_val * (1.0 - sigma))).astype(bf16)
    d_up = (d_hidden * activated).astype(bf16)
    d_gate_up = jnp.stack([d_gate, d_up])
    g_in = jnp.einsum("nd,snf->sdf", normed_two, d_gate_up, preferred_element_type=f32)
    d_normed_two = collect(
        jnp.einsum("snf,sdf->nd", d_gate_up, full_in, preferred_element_type=f32)
    )
    d_mid_norm, g_mlp_gain = second_back(d_normed_two)
    d_middle = cotangent.astype(f32) + d_mid_norm
    d_middle_all = spread(d_middle.astype(bf16))
    g_out = jnp.einsum("nc,nd->cd", mixed_tok, d_middle_all, preferred_element_type=f32)
    d_mixed = jnp.einsum("nd,cd->nc", d_middle_all, full_out, preferred_element_type=f32).astype(
        bf16
    )[None]
    d_mixed_heads = lax.all_to_all(d_mixed, "mp", split_axis=2, concat_axis=1, tiled=True)
    d_proj_heads, d_betas, g_conv_flat, g_out_gain = head_backward(
        d_mixed_heads[0], *head_args, kept
    )
    g_out_gain = g_out_gain[0]
    d_beta_heads = d_betas.astype(bf16)[None]
    d_proj_tok, d_beta_tok = (
        lax.all_to_all(
            shortened(d_proj_heads), "mp", split_axis=1, concat_axis=2, tiled=True
        ).astype(d_proj_heads.dtype),
        lax.all_to_all(
            shortened(d_beta_heads), "mp", split_axis=1, concat_axis=2, tiled=True
        ).astype(d_beta_heads.dtype),
    )
    g_proj = jnp.einsum("nd,snc->sdc", normed, d_proj_tok, preferred_element_type=f32)
    g_beta = jnp.einsum("nd,nh->dh", normed, d_beta_tok[0], preferred_element_type=f32)
    d_normed_part = jnp.einsum("snc,sdc->nd", d_proj_tok, full_proj, preferred_element_type=f32)
    d_normed_part = d_normed_part + jnp.einsum(
        "nh,dh->nd", d_beta_tok[0], full_beta, preferred_element_type=f32
    )
    d_normed = collect(d_normed_part)
    d_in_norm, g_norm_gain = first_back(d_normed)
    d_tokens = d_middle + d_in_norm
    g_conv = g_conv_flat.reshape(conv_weight.shape)
    rows_proj, rows_beta, rows_out, rows_in, rows_down = (
        lax.psum_scatter(g_proj, "mp", scatter_dimension=1, tiled=True),
        lax.psum_scatter(g_beta, "mp", scatter_dimension=0, tiled=True),
        lax.psum_scatter(g_out, "mp", scatter_dimension=1, tiled=True),
        lax.psum_scatter(g_in, "mp", scatter_dimension=1, tiled=True),
        lax.psum_scatter(g_down, "mp", scatter_dimension=1, tiled=True),
    )
    sum_proj, sum_beta, sum_out, sum_in, sum_down, sum_conv = lax.psum(
        (rows_proj, rows_beta, rows_out, rows_in, rows_down, g_conv), "dp"
    )
    gain_one, gain_two, gain_head, norm_all = lax.psum(
        (g_norm_gain, g_mlp_gain, g_out_gain, norm_total), ("dp", "mp", "tensor")
    )
    state_norm = norm_all / (HEADS * seq_count * lax.axis_size("dp") * (seq_len // BLOCK))
    return (
        output,
        d_tokens,
        gain_one,
        sum_proj,
        sum_beta,
        sum_conv,
        gain_head,
        sum_out,
        gain_two,
        sum_in,
        sum_down,
        state_norm,
    )


def solution(mesh):
    placed = (
        P(("dp", "mp", "tensor"), None),
        P(),
        P(None, "mp", "tensor"),
        P("mp", "tensor"),
        P(None, None, "tensor", "mp", None),
        P(),
        P("tensor", "mp"),
        P(),
        P(None, "mp", "tensor"),
        P("tensor", "mp"),
        P(("dp", "mp", "tensor"), None),
        P("dp", None),
        P("dp"),
    )
    return jax.shard_map(
        shards,
        mesh=mesh,
        in_specs=placed,
        out_specs=(
            P(("dp", "mp", "tensor"), None),
            P(("dp", "mp", "tensor"), None),
            P(),
            P(None, "mp", "tensor"),
            P("mp", "tensor"),
            P(None, None, "tensor", "mp", None),
            P(),
            P("tensor", "mp"),
            P(),
            P(None, "mp", "tensor"),
            P("tensor", "mp"),
            P(),
        ),
        check_vma=False,
    )
```

```python
import jax
import jax.numpy as jnp
from jax import lax
from jax.experimental import pallas as pl
from jax.experimental.pallas import tpu as pltpu
from jax.sharding import PartitionSpec as P

BLOCK = 64
PAIR = 2 * BLOCK
LANES = 128
f32 = jnp.float32
bf16 = jnp.bfloat16


def halves(a):
    hi = a.astype(bf16)
    return hi, (a - hi.astype(f32)).astype(bf16)


def product(a, b, dims):
    return lax.dot_general(a, b, (dims, ((), ())), preferred_element_type=f32)


def close_dot(a, b, dims=((1,), (0,))):
    a_hi, a_lo = a if isinstance(a, tuple) else halves(a)
    b_hi, b_lo = b if isinstance(b, tuple) else halves(b)
    return product(a_hi, b_hi, dims) + (product(a_hi, b_lo, dims) + product(a_lo, b_hi, dims))


NN = ((1,), (0,))
NT = ((1,), (1,))
TN = ((0,), (0,))


def doc_start(places, starts_ref):
    found = jnp.zeros_like(places)
    for j in range(1, starts_ref.shape[0]):
        begin = starts_ref[j]
        found = jnp.where(places >= begin, begin, found)
    return found


def place_rows(base, rows, width=LANES):
    return base + lax.broadcasted_iota(jnp.int32, (rows, width), 0)


def pair_masks(base, begins):
    rows = lax.broadcasted_iota(jnp.int32, (PAIR, PAIR), 0)
    cols = lax.broadcasted_iota(jnp.int32, (PAIR, PAIR), 1)
    heads = (rows // BLOCK) * BLOCK
    lower = jnp.maximum(begins - base, heads)
    upto = (cols >= lower) & (cols <= rows)
    strict = (cols >= lower) & (cols < rows)
    keep = begins < base + heads
    return upto, strict, keep, (rows == cols).astype(f32)


HALO = 16


def place_of(chunk, info_ref):
    return chunk ^ info_ref[1]


def in_order(step, count, info_ref, refs, target_ref, first):
    local = place_of(step * count, info_ref)
    near = local < pl.num_programs(0) * count // 2
    for n in range(count):
        inside = (local ^ n) % count

        @pl.when(near)
        def _():
            target_ref[first + n * PAIR:first + (n + 1) * PAIR, :] = refs[0][
                pl.ds(pl.multiple_of(inside * PAIR, PAIR), PAIR), :]

        @pl.when(jnp.logical_not(near))
        def _():
            target_ref[first + n * PAIR:first + (n + 1) * PAIR, :] = refs[1][
                pl.ds(pl.multiple_of(inside * PAIR, PAIR), PAIR), :]


def out_of_order(step, count, info_ref, value, target_ref, width):
    local = place_of(step * count, info_ref)
    for n in range(count):
        inside = pl.multiple_of(((local ^ n) % count) * PAIR, PAIR)
        target_ref[pl.ds(inside, PAIR), width] = value[n * PAIR:(n + 1) * PAIR]


def column(row):
    eye = lax.broadcasted_iota(jnp.int32, (PAIR, PAIR), 0) == lax.broadcasted_iota(jnp.int32, (PAIR, PAIR), 1)
    return jnp.sum(jnp.where(eye, row, 0.0), axis=1, keepdims=True)


def columns(step, count, info_ref, ref):
    return jnp.concatenate(
        [column(ref[pl.ds(place_of(step * count + n, info_ref), 1), :]) for n in range(count)], axis=0)


def forward_body(starts_ref, info_ref, near_ref, far_ref, before_near_ref, before_far_ref, logit_ref, taps_ref,
                 gain_ref, mixed_ref, norm_ref, conv_ref, wu_ref, t_ref, a_ref, c_ref, m_ref, s_ref, o_ref,
                 state_ref, square_ref, x_ref):
    step = pl.program_id(0)
    rows = near_ref.shape[0]
    base = step * rows
    count = rows // PAIR
    half_chunks = pl.num_programs(0) * count // 2
    before = place_of(jnp.maximum(step * count - 1, 0), info_ref)

    @pl.when(before < half_chunks)
    def _():
        x_ref[:HALO, :] = before_near_ref[...]

    @pl.when(before >= half_chunks)
    def _():
        x_ref[:HALO, :] = before_far_ref[...]

    in_order(step, count, info_ref, (near_ref, far_ref), x_ref, HALO)

    @pl.when(step == 0)
    def _():
        state_ref[...] = jnp.zeros_like(state_ref)

    places = place_rows(base, rows)
    begins = doc_start(places, starts_ref)
    since = places - begins
    valid = (places < info_ref[0]).astype(f32)
    parts = []
    for p in range(3):
        tall = x_ref[:, p * LANES:(p + 1) * LANES].astype(f32)
        now = tall[HALO:]
        summed = now * taps_ref[p, 3:4, :]
        for j in range(1, 4):
            moved = pltpu.roll(tall, j, 0)[HALO:]
            summed = summed + jnp.where(since >= j, moved, 0.0) * taps_ref[p, 3 - j:4 - j, :]
        conv_ref[p] = summed
        act = summed * jax.nn.sigmoid(summed)
        if p < 2:
            act = act * lax.rsqrt(jnp.sum(act * act, axis=1, keepdims=True) + 1e-06)
        parts.append(act)
    beta = jax.nn.sigmoid(columns(step, count, info_ref, logit_ref)) * valid
    gates = x_ref[HALO:, 3 * LANES:].astype(f32)
    gates = gates * jax.nn.sigmoid(gates) * valid * gain_ref[...]
    pairs = rows // PAIR
    blocks = []
    for g in range(pairs):
        at = slice(g * PAIR, (g + 1) * PAIR)
        start = base + g * PAIR
        q, k, v, b = parts[0][at], parts[1][at], parts[2][at], beta[at]
        upto, strict, keep, eye = pair_masks(start, begins[at])
        kb = b * k
        k_two = halves(k)
        neg = jnp.where(strict, -close_dot(kb, k_two, NT), 0.0)
        inverse = eye + neg
        power = neg
        for _ in range(BLOCK.bit_length() - 2):
            power_two = halves(power)
            power = close_dot(power_two, power_two)
            inverse = inverse + close_dot(inverse, power)
        wu = close_dot(inverse, jnp.concatenate([jnp.where(keep, kb, 0.0), b * v], axis=1))
        wu_two = halves(wu)
        scores = jnp.where(upto, close_dot(q, k_two, NT), 0.0)
        cd = close_dot(scores, wu_two)
        c = jnp.where(keep, q, 0.0) - cd[:, :LANES]
        wu_ref[at] = wu
        t_ref[at] = inverse
        a_ref[at] = scores
        c_ref[at] = c
        for h in range(2):
            inner = slice(h * BLOCK, (h + 1) * BLOCK)
            first = start + h * BLOCK
            final = doc_start(first + BLOCK - 1, starts_ref)
            tail = place_rows(first, BLOCK) >= final
            k_last = jnp.where(tail, k[inner], 0.0)
            mb = close_dot(k_last, (wu_two[0][inner], wu_two[1][inner]), TN)
            kept = jnp.where(final < first, 1.0, 0.0)
            m = kept * eye - mb[:, :LANES]
            m_ref[g * 2 + h] = m
            blocks.append((halves(m), mb[:, LANES:], c[inner], cd[inner, LANES:]))
    state = state_ref[...]
    results = []
    for n, (m_two, addend, c, d) in enumerate(blocks):
        s_ref[n] = state
        s_two = halves(state)
        results.append(close_dot(c, s_two) + d)
        state = close_dot(m_two, s_two) + addend
        square_ref[pl.ds(step * len(blocks) + n, 1), :] = jnp.sum(state * state, axis=0, keepdims=True)
    state_ref[...] = state
    result = jnp.concatenate(results, axis=0)
    o_ref[...] = result
    unit = result * lax.rsqrt(jnp.mean(result * result, axis=1, keepdims=True) + 1e-05)
    out_of_order(step, count, info_ref, (unit * gates).astype(bf16), mixed_ref, slice(None))

    @pl.when(step == pl.num_programs(0) - 1)
    def _():
        sizes = jnp.sqrt(jnp.sum(square_ref[...], axis=1, keepdims=True) + 1e-12)
        norm_ref[...] = jnp.broadcast_to(jnp.sum(sizes, axis=0, keepdims=True), norm_ref.shape)


def backward_body(starts_ref, info_ref, near_ref, far_ref, logit_ref, taps_ref, gain_ref, grad_near_ref,
                  grad_far_ref, conv_ref, wu_ref, t_ref, a_ref, c_ref, m_ref, s_ref, o_ref,
                  dx_ref, dlogit_ref, dtaps_ref, dgain_ref, dstate_ref, after_ref, x_ref, grad_ref):
    step = pl.num_programs(0) - 1 - pl.program_id(0)
    rows = near_ref.shape[0]
    base = step * rows
    count = rows // PAIR
    in_order(step, count, info_ref, (near_ref, far_ref), x_ref, 0)
    in_order(step, count, info_ref, (grad_near_ref, grad_far_ref), grad_ref, 0)

    @pl.when(pl.program_id(0) == 0)
    def _():
        dstate_ref[...] = jnp.zeros_like(dstate_ref)
        after_ref[...] = jnp.zeros_like(after_ref)
        dtaps_ref[...] = jnp.zeros_like(dtaps_ref)
        dgain_ref[...] = jnp.zeros_like(dgain_ref)

    lead = after_ref.shape[1]
    places_tall = place_rows(base, rows + lead)
    begins_tall = doc_start(places_tall, starts_ref)
    since_tall = places_tall - begins_tall
    places, begins = places_tall[:rows], begins_tall[:rows]
    valid = (places < info_ref[0]).astype(f32)
    gain = gain_ref[...]
    gate = x_ref[:, 3 * LANES:].astype(f32)
    gate_sig = jax.nn.sigmoid(gate)
    gate_act = gate * gate_sig
    o = o_ref[...]
    r = lax.rsqrt(jnp.mean(o * o, axis=1, keepdims=True) + 1e-05)
    unit = o * r
    grad = grad_ref[...].astype(f32) * valid
    gu = grad * unit
    dgain_ref[0:1, :] += jnp.sum(gu * gate_act, axis=0, keepdims=True)
    dgate = (gu * gain * (gate_sig * (1.0 + gate * (1.0 - gate_sig)))).astype(bf16)
    out_of_order(step, count, info_ref, dgate, dx_ref, slice(3 * LANES, 4 * LANES))
    dunit = grad * gain * gate_act
    d_o = r * (dunit - unit * jnp.mean(dunit * unit, axis=1, keepdims=True))
    convs, sigs, acts, scales, units = [], [], [], [], []
    for p in range(3):
        conv = conv_ref[p]
        sig = jax.nn.sigmoid(conv)
        act = conv * sig
        convs.append(conv)
        sigs.append(sig)
        if p < 2:
            scale = lax.rsqrt(jnp.sum(act * act, axis=1, keepdims=True) + 1e-06)
            scales.append(scale)
            units.append(act * scale)
        else:
            units.append(act)
    logit_sig = jax.nn.sigmoid(columns(step, count, info_ref, logit_ref))
    beta = logit_sig * valid
    pairs = rows // PAIR
    do_two = halves(d_o)
    pieces = [None] * (2 * pairs)
    for n in range(2 * pairs):
        inner = slice(n * BLOCK, (n + 1) * BLOCK)
        pieces[n] = close_dot(c_ref[inner, :], (do_two[0][inner], do_two[1][inner]), TN)
    dstate = dstate_ref[...]
    dstates = [None] * (2 * pairs)
    for n in reversed(range(2 * pairs)):
        d_two = halves(dstate)
        dstates[n] = d_two
        dstate = close_dot(m_ref[n], d_two, TN) + pieces[n]
    dstate_ref[...] = dstate
    grads = [[], [], []]
    dbetas = []
    for g in range(pairs):
        at = slice(g * PAIR, (g + 1) * PAIR)
        start = base + g * PAIR
        q, k, v, b = units[0][at], units[1][at], units[2][at], beta[at]
        upto, strict, keep, eye = pair_masks(start, begins[at])
        wu = wu_ref[at, :]
        wu_two = halves(wu)
        a_two = halves(a_ref[at, :])
        k_two = halves(k)
        do_pair = (do_two[0][at], do_two[1][at])
        p_rows, dp_rows, dq_rows, dk_rows, dw_rows = [], [], [], [], []
        later = close_dot(a_two, do_pair, TN)
        for h in range(2):
            n = g * 2 + h
            inner = slice(h * BLOCK, (h + 1) * BLOCK)
            first = start + h * BLOCK
            final = doc_start(first + BLOCK - 1, starts_ref)
            tail = place_rows(first, BLOCK) >= final
            s_two = halves(s_ref[n])
            ds_two = dstates[n]
            wu_in = (wu_two[0][inner, :LANES], wu_two[1][inner, :LANES])
            p = wu[inner, LANES:] - close_dot(wu_in, s_two)
            p_two = halves(p)
            k_last = jnp.where(tail, k[inner], 0.0)
            dp = later[inner] + close_dot(k_last, ds_two)
            dp_two = halves(dp)
            p_rows.append(p_two)
            dp_rows.append(dp)
            do_in = (do_pair[0][inner], do_pair[1][inner])
            dq_rows.append(close_dot(do_in, s_two, NT))
            dk_rows.append(jnp.where(tail, close_dot(p_two, ds_two, NT), 0.0))
            dw_rows.append(-close_dot(dp_two, s_two, NT))
        p_two = tuple(jnp.concatenate([p_rows[0][i], p_rows[1][i]], axis=0) for i in range(2))
        dp = jnp.concatenate(dp_rows, axis=0)
        da_two = halves(jnp.where(upto, close_dot(do_pair, p_two, NT), 0.0))
        q_two = halves(q)
        dq = jnp.where(keep, jnp.concatenate(dq_rows, axis=0), 0.0) + close_dot(da_two, k_two)
        dk = jnp.concatenate(dk_rows, axis=0) + close_dot(da_two, q_two, TN)
        dwu = jnp.concatenate([jnp.concatenate(dw_rows, axis=0), dp], axis=1)
        dbkv = close_dot(t_ref[at, :], dwu, TN)
        dl_two = halves(jnp.where(strict, -close_dot(dbkv, wu_two, NT), 0.0))
        dkb = close_dot(dl_two, k_two) + jnp.where(keep, dbkv[:, :LANES], 0.0)
        dbv = dbkv[:, LANES:]
        dk = dk + b * dkb + close_dot(dl_two, b * k, TN)
        grads[0].append(dq)
        grads[1].append(dk)
        grads[2].append(b * dbv)
        dbetas.append(jnp.sum(k * dkb + v * dbv, axis=1, keepdims=True))
    dbeta = jnp.concatenate(dbetas, axis=0)
    dlogit = dbeta * (beta * (1.0 - logit_sig))
    eye = lax.broadcasted_iota(jnp.int32, (PAIR, PAIR), 0) == lax.broadcasted_iota(jnp.int32, (PAIR, PAIR), 1)
    for n in range(count):
        row = jnp.sum(jnp.where(eye, dlogit[n * PAIR:(n + 1) * PAIR], 0.0), axis=0, keepdims=True)
        dlogit_ref[pl.ds(place_of(step * count + n, info_ref), 1), :] = row
    for p in range(3):
        dact = jnp.concatenate(grads[p], axis=0)
        if p < 2:
            dact = scales[p] * (dact - units[p] * jnp.sum(dact * units[p], axis=1, keepdims=True))
        dconv = dact * (sigs[p] * (1.0 + convs[p] * (1.0 - sigs[p])))
        tall = jnp.concatenate([dconv, after_ref[p]], axis=0)
        after_ref[p] = dconv[:lead]
        x = x_ref[:, p * LANES:(p + 1) * LANES].astype(f32)
        dx = dconv * taps_ref[p, 3:4, :]
        dtaps_ref[p, 3:4, :] += jnp.sum(dconv * x, axis=0, keepdims=True)
        for j in range(1, 4):
            moved = pltpu.roll(jnp.where(since_tall >= j, tall, 0.0), rows + lead - j, 0)[:rows]
            dx = dx + moved * taps_ref[p, 3 - j:4 - j, :]
            dtaps_ref[p, 3 - j:4 - j, :] += jnp.sum(moved * x, axis=0, keepdims=True)
        out_of_order(step, count, info_ref, dx.astype(bf16), dx_ref, slice(p * LANES, (p + 1) * LANES))


def half_specs(rows, width, steps, order):
    count = rows // PAIR

    def pair(i, info):
        return place_of(order(i) * count, info) // count

    return [
        pl.BlockSpec((rows, width), lambda i, _, info: (jnp.minimum(pair(i, info), steps // 2 - 1), 0)),
        pl.BlockSpec((rows, width), lambda i, _, info: (jnp.maximum(pair(i, info) - steps // 2, 0), 0)),
    ]


def whole_spec(shape):
    return pl.BlockSpec(shape, lambda i, *_: (0,) * len(shape))


def head_forward(near, far, logit, taps, gain, starts, info, rows=256):
    total = 2 * near.shape[0]
    steps = total // rows
    count = rows // PAIR
    per = rows // BLOCK
    chunks = total // PAIR
    flat = lambda width: pl.BlockSpec((rows, width), lambda i, *_: (i, 0))
    square = pl.BlockSpec((per, LANES, LANES), lambda i, *_: (i, 0, 0))
    fine = PAIR // HALO

    def before(i, info):
        return place_of(jnp.maximum(i * count - 1, 0), info)

    s = jax.ShapeDtypeStruct
    outs = pl.pallas_call(
        forward_body,
        grid_spec=pltpu.PrefetchScalarGridSpec(
            num_scalar_prefetch=2,
            grid=(steps,),
            in_specs=[
                *half_specs(rows, 4 * LANES, steps, lambda i: i),
                pl.BlockSpec((HALO, 4 * LANES), lambda i, _, info: (
                    jnp.minimum(before(i, info), chunks // 2 - 1) * fine + fine - 1, 0)),
                pl.BlockSpec((HALO, 4 * LANES), lambda i, _, info: (
                    jnp.maximum(before(i, info) - chunks // 2, 0) * fine + fine - 1, 0)),
                whole_spec(logit.shape),
                whole_spec(taps.shape),
                whole_spec(gain.shape),
            ],
            out_specs=[
                pl.BlockSpec((rows, LANES), lambda i, _, info: (place_of(i * count, info) // count, 0)),
                whole_spec((8, LANES)),
                pl.BlockSpec((3, rows, LANES), lambda i, *_: (0, i, 0)),
                flat(2 * LANES), flat(PAIR), flat(PAIR), flat(LANES),
                square, square, flat(LANES),
            ],
            scratch_shapes=[
                pltpu.VMEM((LANES, LANES), f32), pltpu.VMEM((total // BLOCK, LANES), f32),
                pltpu.VMEM((rows + HALO, 4 * LANES), bf16),
            ],
        ),
        out_shape=[
            s((total, LANES), bf16), s((8, LANES), f32), s((3, total, LANES), f32),
            s((total, 2 * LANES), f32), s((total, PAIR), f32), s((total, PAIR), f32), s((total, LANES), f32),
            s((total // BLOCK, LANES, LANES), f32), s((total // BLOCK, LANES, LANES), f32),
            s((total, LANES), f32),
        ],
        name="head_forward",
    )(starts, info, near, far, near, far, logit, taps, gain)
    return outs[0], outs[1][0, 0], tuple(outs[2:])


def head_backward(grad_near, grad_far, near, far, logit, taps, gain, starts, info, kept, rows=256):
    total = 2 * near.shape[0]
    steps = total // rows
    count = rows // PAIR
    per = rows // BLOCK
    back = lambda i: steps - 1 - i
    flat = lambda width: pl.BlockSpec((rows, width), lambda i, *_: (back(i), 0))
    square = pl.BlockSpec((per, LANES, LANES), lambda i, *_: (back(i), 0, 0))
    s = jax.ShapeDtypeStruct
    return pl.pallas_call(
        backward_body,
        grid_spec=pltpu.PrefetchScalarGridSpec(
            num_scalar_prefetch=2,
            grid=(steps,),
            in_specs=[
                *half_specs(rows, 4 * LANES, steps, back),
                whole_spec(logit.shape), whole_spec(taps.shape), whole_spec(gain.shape),
                *half_specs(rows, LANES, steps, back),
                pl.BlockSpec((3, rows, LANES), lambda i, *_: (0, back(i), 0)),
                flat(2 * LANES), flat(PAIR), flat(PAIR), flat(LANES), square, square, flat(LANES),
            ],
            out_specs=[
                pl.BlockSpec((rows, 4 * LANES), lambda i, _, info: (place_of(back(i) * count, info) // count, 0)),
                whole_spec(logit.shape), whole_spec(taps.shape), whole_spec((8, LANES)),
            ],
            scratch_shapes=[
                pltpu.VMEM((LANES, LANES), f32), pltpu.VMEM((3, 8, LANES), f32),
                pltpu.VMEM((rows, 4 * LANES), bf16), pltpu.VMEM((rows, LANES), bf16),
            ],
        ),
        out_shape=[s((total, 4 * LANES), bf16), s(logit.shape, f32), s(taps.shape, f32), s((8, LANES), f32)],
        name="head_backward",
    )(starts, info, near, far, logit, taps, gain, grad_near, grad_far, *kept)


def other(value, axis, bit):
    size = lax.axis_size(axis)
    return lax.ppermute(value, axis, [(i, i ^ bit) for i in range(size)])


def after(value, *done):
    return lax.optimization_barrier((value, *done))[0]


def own_order(value, index, axis, parts=4):
    size = value.shape[axis] // parts
    return jnp.concatenate(
        [lax.dynamic_slice_in_dim(value, (p ^ index) * size, size, axis) for p in range(parts)], axis
    )


def neighbour_order(value, axis, bit, parts=4):
    size = value.shape[axis] // parts
    return jnp.concatenate(
        [lax.slice_in_dim(value, (p ^ bit) * size, ((p ^ bit) + 1) * size, axis=axis) for p in range(parts)], axis
    )


def matmul(a, b, dims=((1,), (0,))):
    return lax.dot_general(a, b, (dims, ((), ())), preferred_element_type=f32)


def norm_rows(values, gain):
    scale = lax.rsqrt(jnp.mean(values * values, axis=-1, keepdims=True) + 1e-05)
    unit = values * scale
    return unit * gain, unit, scale


def norm_back(grad, unit, scale, gain):
    pulled = grad * gain
    inner = jnp.mean(pulled * unit, axis=-1, keepdims=True)
    return scale * (pulled - unit * inner), jnp.sum(grad * unit, axis=0)


def spread(values):
    mine = [values] + [other(values, "tensor", s) for s in range(1, lax.axis_size("tensor"))]
    theirs = [neighbour_order(other(v, "mp", 1), 1, 1) for v in mine]
    return jnp.concatenate(mine + theirs, axis=0)


def collect(partial):
    ways = lax.axis_size("tensor")
    rows = partial.rows // 2
    theirs = partial(rows, 2 * rows).astype(bf16)
    back = neighbour_order(other(theirs, "mp", 1), 1, 1)
    joined = partial(0, rows) + back.astype(f32)
    piece = rows // ways
    total = joined[:piece]
    for s in range(1, ways):
        total = total + other(joined[s * piece:(s + 1) * piece].astype(bf16), "tensor", s).astype(f32)
    return total


class Rows:
    def __init__(self, rows, body):
        self.rows = rows
        self.body = body

    def __call__(self, start, stop):
        return self.body(start, stop)


def over_dp(value):
    bit = 1
    while bit < lax.axis_size("dp"):
        low = value.astype(bf16)
        value = low.astype(f32) + other(low, "dp", bit).astype(f32)
        bit *= 2
    return value


def shards(
    tokens,
    norm_gain,
    w_proj,
    w_beta,
    conv_weight,
    out_gain,
    w_out,
    mlp_gain,
    w_in,
    w_down,
    cotangent,
    starts,
    lengths,
):
    assert lax.axis_size("mp") == 4 and starts.shape[0] == 1
    m = lax.axis_index("mp")
    core = m & 1
    place = m * lax.axis_size("tensor") + lax.axis_index("tensor")
    block = w_proj.shape[1]
    near_blocks = 2 * block

    inputs = own_order(tokens, m, 1).astype(f32)
    gain_one = own_order(norm_gain, m, 0)
    gain_two = own_order(mlp_gain, m, 0)
    scaled, unit_one, scale_one = norm_rows(inputs, gain_one)
    scaled = scaled.astype(bf16)

    pieces, _, wide = w_proj.shape
    head = wide // 4
    heads = [
        lax.dynamic_slice_in_dim(w_proj, (j ^ m) * head, head, 2).transpose(1, 0, 2).reshape(block, pieces * head)
        for j in range(4)
    ]
    pair = lambda values, i, j, axis: jnp.concatenate([values[i], values[j]], axis)
    full_proj = jnp.concatenate(
        [
            pair(heads, 0, 2, 1),
            other(pair(heads, 1, 3, 1), "mp", 1),
            other(pair(heads, 2, 0, 1), "mp", 2),
            other(pair(heads, 3, 1, 1), "mp", 3),
        ],
        axis=0,
    )
    beta_rows = w_beta.T
    full_beta = own_order(
        jnp.concatenate([beta_rows] + [other(beta_rows, "mp", s) for s in range(1, 4)], axis=1), m, 0
    )
    full_beta = jnp.concatenate([full_beta[0:1], full_beta[2:3]], axis=0)

    normed = spread(scaled)
    far_out = matmul(normed, full_proj[:, pieces * head:]).astype(bf16)
    logits = matmul(full_beta, normed, ((1,), (1,))).astype(bf16)
    far = other(far_out, "mp", 2)
    far_logit = other(logits[1:2], "mp", 2)
    near = matmul(normed, full_proj[:, : pieces * head]).astype(bf16)
    chunk_rows = (-1, LANES)
    logit = jnp.concatenate([logits[0].reshape(chunk_rows), far_logit.reshape(chunk_rows)], axis=0).astype(f32)

    w_out, w_in, w_down = after((w_out, w_in, w_down), far)
    out_rows = [lax.dynamic_slice_in_dim(w_out, (j ^ m) * head, head, 0) for j in range(4)]
    full_out = jnp.concatenate(
        [
            pair(out_rows, 0, 2, 0),
            other(pair(out_rows, 1, 3, 0), "mp", 1),
            other(pair(out_rows, 2, 0, 0), "mp", 2),
            other(pair(out_rows, 3, 1, 0), "mp", 3),
        ],
        axis=1,
    )
    units = w_down.shape[0]
    half = LANES * ((units // LANES + 1) // 2)
    ours_in = lax.dynamic_slice_in_dim(w_in, core * (units - half), half, 2)
    theirs_in = lax.dynamic_slice_in_dim(w_in, (1 - core) * (units - half), half, 2)
    far_in = other(ours_in, "mp", 2)
    diag_in = other(theirs_in, "mp", 3)
    full_in = jnp.concatenate([ours_in, other(theirs_in, "mp", 1), far_in, diag_in], axis=1)
    w_down = after(w_down, far_in, diag_in)
    ours_down = lax.dynamic_slice_in_dim(w_down, core * (units - half), half, 0)
    theirs_down = lax.dynamic_slice_in_dim(w_down, (1 - core) * (units - half), half, 0)
    full_down = jnp.concatenate(
        [ours_down, other(theirs_down, "mp", 1), other(ours_down, "mp", 2), other(theirs_down, "mp", 3)], axis=1
    )
    live = (lax.broadcasted_iota(jnp.int32, (1, half), 1) >= core * (2 * half - units)).astype(f32)

    taps = conv_weight.reshape(3, conv_weight.shape[1], head)
    info = jnp.stack([lengths[0], place]).astype(jnp.int32)
    head_args = (near, far, logit, taps, out_gain[None], starts[0], info)
    mixed, norm_total, kept = head_forward(*head_args)
    count = near.shape[0]
    mixed_tok = jnp.concatenate([mixed[:count], other(mixed[count:], "mp", 2)], axis=1)
    branch = collect(Rows(count, lambda a, b: matmul(mixed_tok[a:b], full_out)))
    middle = inputs + branch
    scaled_two, unit_two, scale_two = norm_rows(middle, gain_two)
    normed_two = spread(scaled_two.astype(bf16))

    cot_own = own_order(cotangent, m, 1)
    cot_all = spread(after(cot_own, normed))
    gate = matmul(normed_two, full_in[0])
    up = matmul(normed_two, full_in[1])
    sigma = jax.nn.sigmoid(gate)
    activated = gate * sigma
    hidden = (activated * up * live).astype(bf16)
    d_hidden = matmul(cot_all, full_down, ((1,), (1,)))
    d_hidden = d_hidden * live
    d_gate = (d_hidden * up * sigma * (1.0 + gate * (1.0 - sigma))).astype(bf16)
    d_up = (d_hidden * activated).astype(bf16)
    d_normed_two = collect(
        Rows(
            count,
            lambda a, b: matmul(d_gate[a:b], full_in[0], ((1,), (1,))) + matmul(d_up[a:b], full_in[1], ((1,), (1,))),
        )
    )
    d_mid_norm, g_mlp = norm_back(d_normed_two, unit_two, scale_two, gain_two)
    d_middle = cot_own.astype(f32) + d_mid_norm
    feed = collect(Rows(count, lambda a, b: matmul(hidden[a:b], full_down)))
    output = own_order((middle + feed).astype(bf16), m, 1)

    tn = ((0,), (0,))

    def joined_units(mine, theirs, axis):
        gap = units - half
        low = jnp.where(core == 0, mine, theirs)
        high = jnp.where(core == 0, theirs, mine)
        zero = jnp.zeros_like(lax.slice_in_dim(low, 0, gap, axis=axis))
        return jnp.concatenate([low, zero], axis) + jnp.concatenate([zero, high], axis)

    def far_sum(product, lhs, rhs, axis, swap=None):
        cut = lambda v, a, b: lax.slice_in_dim(v, a, b, axis=1)
        if axis == 0:
            sent = product(cut(lhs, near_blocks, 2 * near_blocks), rhs).astype(bf16)
            held = product(cut(lhs, 0, near_blocks), rhs)
        else:
            sent = product(lhs, cut(rhs, near_blocks, 2 * near_blocks)).astype(bf16)
            held = product(lhs, cut(rhs, 0, near_blocks))
        back = other(sent, "mp", 2)
        if swap is not None:
            back = neighbour_order(back, swap, 1, 2)
        return (held + back.astype(f32)).astype(bf16)

    grad_dot = lambda a, b: matmul(a, b, tn)
    down_two = far_sum(grad_dot, hidden, cot_all, 1)
    down_mine = down_two[:, :block]
    g_down = over_dp(joined_units(down_mine, other(down_two[:, block:], "mp", 1), 0))
    in_sums = []
    for grad in (d_gate, d_up):
        in_two = far_sum(grad_dot, normed_two, grad, 0)
        in_sums.append(over_dp(joined_units(in_two[:block], other(in_two[block:], "mp", 1), 1)))
    g_in = jnp.stack(in_sums)

    d_mid_all = spread(d_middle.astype(bf16))
    d_mixed = matmul(d_mid_all, full_out, ((1,), (1,))).astype(bf16)
    d_far = other(d_mixed[:, head:], "mp", 2)
    out_two = far_sum(grad_dot, mixed_tok, d_mid_all, 1, swap=0)
    out_theirs = other(out_two[:, block:], "mp", 1)
    out_mine = out_two[:, :block]
    g_out = over_dp(
        own_order(
            jnp.concatenate([out_mine[:head], out_theirs[:head], out_mine[head:], out_theirs[head:]], axis=0), m, 0
        )
    )
    d_heads, d_logit, d_taps, g_head_gain = head_backward(d_mixed[:, :head], d_far, *head_args, kept)
    d_proj = jnp.concatenate([d_heads[:count], other(d_heads[count:], "mp", 2)], axis=1)
    d_logit = d_logit.astype(bf16)
    half_chunks = d_logit.shape[0] // 2
    d_logits = jnp.concatenate(
        [d_logit[:half_chunks].reshape(1, count), other(d_logit[half_chunks:], "mp", 2).reshape(1, count)], axis=0
    )
    d_normed = collect(
        Rows(
            count,
            lambda a, b: matmul(d_proj[a:b], full_proj, ((1,), (1,))) + matmul(d_logits[:, a:b], full_beta, tn),
        )
    )
    proj_two = far_sum(grad_dot, normed, d_proj, 0, swap=1)
    proj_mine = proj_two[:block]
    proj_theirs = other(proj_two[block:], "mp", 1)
    span = pieces * head
    g_proj = over_dp(
        jnp.concatenate(
            [proj_mine[:, :span], proj_theirs[:, :span], proj_mine[:, span:], proj_theirs[:, span:]], axis=1
        )
    )
    g_proj = jnp.concatenate(
        [
            lax.dynamic_slice_in_dim(g_proj, (h ^ m) * span, span, 1).reshape(block, pieces, head).transpose(1, 0, 2)
            for h in range(4)
        ],
        axis=2,
    )
    beta_part = matmul(d_logits, normed)
    beta_back = neighbour_order(neighbour_order(other(beta_part, "mp", 2), 0, 1, 2), 1, 1, 2)
    beta_two = beta_part + beta_back
    beta_theirs = other(beta_two[:, block:near_blocks], "mp", 1)
    beta_rows = own_order(
        jnp.concatenate([beta_two[:1, :block], beta_theirs[:1], beta_two[1:, :block], beta_theirs[1:]], axis=0), m, 0
    )
    bit = 1
    while bit < lax.axis_size("dp"):
        beta_rows = beta_rows + other(beta_rows, "dp", bit)
        d_taps = d_taps + other(d_taps, "dp", bit)
        bit *= 2
    d_in_norm, g_norm = norm_back(d_normed, unit_one, scale_one, gain_one)
    d_tokens = own_order(d_middle + d_in_norm, m, 1)
    sum_norm, sum_mlp, sum_head, norm_all = lax.psum(
        (own_order(g_norm, m, 0), own_order(g_mlp, m, 0), g_head_gain[0], norm_total), ("dp", "mp", "tensor")
    )
    ways = lax.axis_size("mp") * lax.axis_size("tensor")
    state_norm = norm_all / (ways * lax.axis_size("dp") * (2 * count // BLOCK))
    return (
        output,
        d_tokens,
        sum_norm,
        g_proj,
        beta_rows.T,
        d_taps.reshape(conv_weight.shape),
        sum_head,
        g_out,
        sum_mlp,
        g_in,
        g_down,
        state_norm,
    )


def solution(mesh):
    placed = (
        P(("dp", "mp", "tensor"), None),
        P(),
        P(None, "mp", "tensor"),
        P("mp", "tensor"),
        P(None, None, "tensor", "mp", None),
        P(),
        P("tensor", "mp"),
        P(),
        P(None, "mp", "tensor"),
        P("tensor", "mp"),
        P(("dp", "mp", "tensor"), None),
        P("dp", None),
        P("dp"),
    )
    return jax.shard_map(
        shards,
        mesh=mesh,
        in_specs=placed,
        out_specs=(
            P(("dp", "mp", "tensor"), None),
            P(("dp", "mp", "tensor"), None),
            P(),
            P(None, "mp", "tensor"),
            P("mp", "tensor"),
            P(None, None, "tensor", "mp", None),
            P(),
            P("tensor", "mp"),
            P(),
            P(None, "mp", "tensor"),
            P("tensor", "mp"),
            P(),
        ),
        check_vma=False,
    )
```

```python
import jax
import jax.numpy as jnp
from jax import lax
from jax.experimental import pallas as pl
from jax.experimental.pallas import tpu as pltpu
from jax.sharding import PartitionSpec as P

BLOCK = 64
PAIR = 2 * BLOCK
LANES = 128
f32 = jnp.float32
bf16 = jnp.bfloat16


def halves(a):
    hi = a.astype(bf16)
    return hi, (a - hi.astype(f32)).astype(bf16)


def product(a, b, dims):
    return lax.dot_general(a, b, (dims, ((), ())), preferred_element_type=f32)


def close_dot(a, b, dims=((1,), (0,))):
    a_hi, a_lo = a if isinstance(a, tuple) else halves(a)
    b_hi, b_lo = b if isinstance(b, tuple) else halves(b)
    return product(a_hi, b_hi, dims) + (product(a_hi, b_lo, dims) + product(a_lo, b_hi, dims))


NN = ((1,), (0,))
NT = ((1,), (1,))
TN = ((0,), (0,))


def doc_start(places, starts_ref):
    found = jnp.zeros_like(places)
    for j in range(1, starts_ref.shape[0]):
        begin = starts_ref[j]
        found = jnp.where(places >= begin, begin, found)
    return found


def place_rows(base, rows, width=LANES):
    return base + lax.broadcasted_iota(jnp.int32, (rows, width), 0)


def pair_masks(base, begins):
    rows = lax.broadcasted_iota(jnp.int32, (PAIR, PAIR), 0)
    cols = lax.broadcasted_iota(jnp.int32, (PAIR, PAIR), 1)
    heads = (rows // BLOCK) * BLOCK
    lower = jnp.maximum(begins - base, heads)
    upto = (cols >= lower) & (cols <= rows)
    strict = (cols >= lower) & (cols < rows)
    keep = begins < base + heads
    return upto, strict, keep, (rows == cols).astype(f32)


HALO = 16


def place_of(chunk, info_ref):
    return chunk ^ info_ref[1]


def in_order(step, count, info_ref, refs, target_ref, first):
    local = place_of(step * count, info_ref)
    near = local < pl.num_programs(0) * count // 2
    for n in range(count):
        inside = (local ^ n) % count

        @pl.when(near)
        def _():
            target_ref[first + n * PAIR:first + (n + 1) * PAIR, :] = refs[0][
                pl.ds(pl.multiple_of(inside * PAIR, PAIR), PAIR), :]

        @pl.when(jnp.logical_not(near))
        def _():
            target_ref[first + n * PAIR:first + (n + 1) * PAIR, :] = refs[1][
                pl.ds(pl.multiple_of(inside * PAIR, PAIR), PAIR), :]


def out_of_order(step, count, info_ref, value, target_ref, width):
    local = place_of(step * count, info_ref)
    for n in range(count):
        inside = pl.multiple_of(((local ^ n) % count) * PAIR, PAIR)
        target_ref[pl.ds(inside, PAIR), width] = value[n * PAIR:(n + 1) * PAIR]


def column(row):
    eye = lax.broadcasted_iota(jnp.int32, (PAIR, PAIR), 0) == lax.broadcasted_iota(jnp.int32, (PAIR, PAIR), 1)
    return jnp.sum(jnp.where(eye, row, 0.0), axis=1, keepdims=True)


def columns(step, count, info_ref, ref):
    return jnp.concatenate(
        [column(ref[pl.ds(place_of(step * count + n, info_ref), 1), :]) for n in range(count)], axis=0)


def forward_body(starts_ref, info_ref, near_ref, far_ref, before_near_ref, before_far_ref, logit_ref, taps_ref,
                 gain_ref, mixed_ref, norm_ref, conv_ref, wu_ref, t_ref, a_ref, c_ref, m_ref, s_ref, o_ref,
                 state_ref, square_ref, x_ref):
    step = pl.program_id(0)
    rows = near_ref.shape[0]
    base = step * rows
    count = rows // PAIR
    half_chunks = pl.num_programs(0) * count // 2
    before = place_of(jnp.maximum(step * count - 1, 0), info_ref)

    @pl.when(before < half_chunks)
    def _():
        x_ref[:HALO, :] = before_near_ref[...]

    @pl.when(before >= half_chunks)
    def _():
        x_ref[:HALO, :] = before_far_ref[...]

    in_order(step, count, info_ref, (near_ref, far_ref), x_ref, HALO)

    @pl.when(step == 0)
    def _():
        state_ref[...] = jnp.zeros_like(state_ref)

    places = place_rows(base, rows)
    begins = doc_start(places, starts_ref)
    since = places - begins
    valid = (places < info_ref[0]).astype(f32)
    parts = []
    for p in range(3):
        tall = x_ref[:, p * LANES:(p + 1) * LANES].astype(f32)
        now = tall[HALO:]
        summed = now * taps_ref[p, 3:4, :]
        for j in range(1, 4):
            moved = pltpu.roll(tall, j, 0)[HALO:]
            summed = summed + jnp.where(since >= j, moved, 0.0) * taps_ref[p, 3 - j:4 - j, :]
        conv_ref[p] = summed
        act = summed * jax.nn.sigmoid(summed)
        if p < 2:
            act = act * lax.rsqrt(jnp.sum(act * act, axis=1, keepdims=True) + 1e-06)
        parts.append(act)
    beta = jax.nn.sigmoid(columns(step, count, info_ref, logit_ref)) * valid
    gates = x_ref[HALO:, 3 * LANES:].astype(f32)
    gates = gates * jax.nn.sigmoid(gates) * valid * gain_ref[...]
    pairs = rows // PAIR
    blocks = []
    for g in range(pairs):
        at = slice(g * PAIR, (g + 1) * PAIR)
        start = base + g * PAIR
        q, k, v, b = parts[0][at], parts[1][at], parts[2][at], beta[at]
        upto, strict, keep, eye = pair_masks(start, begins[at])
        kb = b * k
        k_two = halves(k)
        neg = jnp.where(strict, -close_dot(kb, k_two, NT), 0.0)
        inverse = eye + neg
        power = neg
        for _ in range(BLOCK.bit_length() - 2):
            power_two = halves(power)
            power = close_dot(power_two, power_two)
            inverse = inverse + close_dot(inverse, power)
        wu = close_dot(inverse, jnp.concatenate([jnp.where(keep, kb, 0.0), b * v], axis=1))
        wu_two = halves(wu)
        scores = jnp.where(upto, close_dot(q, k_two, NT), 0.0)
        cd = close_dot(scores, wu_two)
        c = jnp.where(keep, q, 0.0) - cd[:, :LANES]
        wu_ref[at] = wu
        t_ref[at] = inverse
        a_ref[at] = scores
        c_ref[at] = c
        for h in range(2):
            inner = slice(h * BLOCK, (h + 1) * BLOCK)
            first = start + h * BLOCK
            final = doc_start(first + BLOCK - 1, starts_ref)
            tail = place_rows(first, BLOCK) >= final
            k_last = jnp.where(tail, k[inner], 0.0)
            mb = close_dot(k_last, (wu_two[0][inner], wu_two[1][inner]), TN)
            kept = jnp.where(final < first, 1.0, 0.0)
            m = kept * eye - mb[:, :LANES]
            m_ref[g * 2 + h] = m
            blocks.append((halves(m), mb[:, LANES:], c[inner], cd[inner, LANES:]))
    state = state_ref[...]
    results = []
    for n, (m_two, addend, c, d) in enumerate(blocks):
        s_ref[n] = state
        s_two = halves(state)
        results.append(close_dot(c, s_two) + d)
        state = close_dot(m_two, s_two) + addend
        square_ref[pl.ds(step * len(blocks) + n, 1), :] = jnp.sum(state * state, axis=0, keepdims=True)
    state_ref[...] = state
    result = jnp.concatenate(results, axis=0)
    o_ref[...] = result
    unit = result * lax.rsqrt(jnp.mean(result * result, axis=1, keepdims=True) + 1e-05)
    out_of_order(step, count, info_ref, (unit * gates).astype(bf16), mixed_ref, slice(None))

    @pl.when(step == pl.num_programs(0) - 1)
    def _():
        sizes = jnp.sqrt(jnp.sum(square_ref[...], axis=1, keepdims=True) + 1e-12)
        norm_ref[...] = jnp.broadcast_to(jnp.sum(sizes, axis=0, keepdims=True), norm_ref.shape)


def backward_body(starts_ref, info_ref, near_ref, far_ref, logit_ref, taps_ref, gain_ref, grad_near_ref,
                  grad_far_ref, conv_ref, wu_ref, t_ref, a_ref, c_ref, m_ref, s_ref, o_ref,
                  dx_ref, dlogit_ref, dtaps_ref, dgain_ref, dstate_ref, after_ref, x_ref, grad_ref):
    step = pl.num_programs(0) - 1 - pl.program_id(0)
    rows = near_ref.shape[0]
    base = step * rows
    count = rows // PAIR
    in_order(step, count, info_ref, (near_ref, far_ref), x_ref, 0)
    in_order(step, count, info_ref, (grad_near_ref, grad_far_ref), grad_ref, 0)

    @pl.when(pl.program_id(0) == 0)
    def _():
        dstate_ref[...] = jnp.zeros_like(dstate_ref)
        after_ref[...] = jnp.zeros_like(after_ref)
        dtaps_ref[...] = jnp.zeros_like(dtaps_ref)
        dgain_ref[...] = jnp.zeros_like(dgain_ref)

    lead = after_ref.shape[1]
    places_tall = place_rows(base, rows + lead)
    begins_tall = doc_start(places_tall, starts_ref)
    since_tall = places_tall - begins_tall
    places, begins = places_tall[:rows], begins_tall[:rows]
    valid = (places < info_ref[0]).astype(f32)
    gain = gain_ref[...]
    gate = x_ref[:, 3 * LANES:].astype(f32)
    gate_sig = jax.nn.sigmoid(gate)
    gate_act = gate * gate_sig
    o = o_ref[...]
    r = lax.rsqrt(jnp.mean(o * o, axis=1, keepdims=True) + 1e-05)
    unit = o * r
    grad = grad_ref[...].astype(f32) * valid
    gu = grad * unit
    dgain_ref[0:1, :] += jnp.sum(gu * gate_act, axis=0, keepdims=True)
    dgate = (gu * gain * (gate_sig * (1.0 + gate * (1.0 - gate_sig)))).astype(bf16)
    out_of_order(step, count, info_ref, dgate, dx_ref, slice(3 * LANES, 4 * LANES))
    dunit = grad * gain * gate_act
    d_o = r * (dunit - unit * jnp.mean(dunit * unit, axis=1, keepdims=True))
    convs, sigs, acts, scales, units = [], [], [], [], []
    for p in range(3):
        conv = conv_ref[p]
        sig = jax.nn.sigmoid(conv)
        act = conv * sig
        convs.append(conv)
        sigs.append(sig)
        if p < 2:
            scale = lax.rsqrt(jnp.sum(act * act, axis=1, keepdims=True) + 1e-06)
            scales.append(scale)
            units.append(act * scale)
        else:
            units.append(act)
    logit_sig = jax.nn.sigmoid(columns(step, count, info_ref, logit_ref))
    beta = logit_sig * valid
    pairs = rows // PAIR
    do_two = halves(d_o)
    pieces = [None] * (2 * pairs)
    for n in range(2 * pairs):
        inner = slice(n * BLOCK, (n + 1) * BLOCK)
        pieces[n] = close_dot(c_ref[inner, :], (do_two[0][inner], do_two[1][inner]), TN)
    dstate = dstate_ref[...]
    dstates = [None] * (2 * pairs)
    for n in reversed(range(2 * pairs)):
        d_two = halves(dstate)
        dstates[n] = d_two
        dstate = close_dot(m_ref[n], d_two, TN) + pieces[n]
    dstate_ref[...] = dstate
    grads = [[], [], []]
    dbetas = []
    for g in range(pairs):
        at = slice(g * PAIR, (g + 1) * PAIR)
        start = base + g * PAIR
        q, k, v, b = units[0][at], units[1][at], units[2][at], beta[at]
        upto, strict, keep, eye = pair_masks(start, begins[at])
        wu = wu_ref[at, :]
        wu_two = halves(wu)
        a_two = halves(a_ref[at, :])
        k_two = halves(k)
        do_pair = (do_two[0][at], do_two[1][at])
        p_rows, dp_rows, dq_rows, dk_rows, dw_rows = [], [], [], [], []
        later = close_dot(a_two, do_pair, TN)
        for h in range(2):
            n = g * 2 + h
            inner = slice(h * BLOCK, (h + 1) * BLOCK)
            first = start + h * BLOCK
            final = doc_start(first + BLOCK - 1, starts_ref)
            tail = place_rows(first, BLOCK) >= final
            s_two = halves(s_ref[n])
            ds_two = dstates[n]
            wu_in = (wu_two[0][inner, :LANES], wu_two[1][inner, :LANES])
            p = wu[inner, LANES:] - close_dot(wu_in, s_two)
            p_two = halves(p)
            k_last = jnp.where(tail, k[inner], 0.0)
            dp = later[inner] + close_dot(k_last, ds_two)
            dp_two = halves(dp)
            p_rows.append(p_two)
            dp_rows.append(dp)
            do_in = (do_pair[0][inner], do_pair[1][inner])
            dq_rows.append(close_dot(do_in, s_two, NT))
            dk_rows.append(jnp.where(tail, close_dot(p_two, ds_two, NT), 0.0))
            dw_rows.append(-close_dot(dp_two, s_two, NT))
        p_two = tuple(jnp.concatenate([p_rows[0][i], p_rows[1][i]], axis=0) for i in range(2))
        dp = jnp.concatenate(dp_rows, axis=0)
        da_two = halves(jnp.where(upto, close_dot(do_pair, p_two, NT), 0.0))
        q_two = halves(q)
        dq = jnp.where(keep, jnp.concatenate(dq_rows, axis=0), 0.0) + close_dot(da_two, k_two)
        dk = jnp.concatenate(dk_rows, axis=0) + close_dot(da_two, q_two, TN)
        dwu = jnp.concatenate([jnp.concatenate(dw_rows, axis=0), dp], axis=1)
        dbkv = close_dot(t_ref[at, :], dwu, TN)
        dl_two = halves(jnp.where(strict, -close_dot(dbkv, wu_two, NT), 0.0))
        dkb = close_dot(dl_two, k_two) + jnp.where(keep, dbkv[:, :LANES], 0.0)
        dbv = dbkv[:, LANES:]
        dk = dk + b * dkb + close_dot(dl_two, b * k, TN)
        grads[0].append(dq)
        grads[1].append(dk)
        grads[2].append(b * dbv)
        dbetas.append(jnp.sum(k * dkb + v * dbv, axis=1, keepdims=True))
    dbeta = jnp.concatenate(dbetas, axis=0)
    dlogit = dbeta * (beta * (1.0 - logit_sig))
    eye = lax.broadcasted_iota(jnp.int32, (PAIR, PAIR), 0) == lax.broadcasted_iota(jnp.int32, (PAIR, PAIR), 1)
    for n in range(count):
        row = jnp.sum(jnp.where(eye, dlogit[n * PAIR:(n + 1) * PAIR], 0.0), axis=0, keepdims=True)
        dlogit_ref[pl.ds(place_of(step * count + n, info_ref), 1), :] = row
    for p in range(3):
        dact = jnp.concatenate(grads[p], axis=0)
        if p < 2:
            dact = scales[p] * (dact - units[p] * jnp.sum(dact * units[p], axis=1, keepdims=True))
        dconv = dact * (sigs[p] * (1.0 + convs[p] * (1.0 - sigs[p])))
        tall = jnp.concatenate([dconv, after_ref[p]], axis=0)
        after_ref[p] = dconv[:lead]
        x = x_ref[:, p * LANES:(p + 1) * LANES].astype(f32)
        dx = dconv * taps_ref[p, 3:4, :]
        dtaps_ref[p, 3:4, :] += jnp.sum(dconv * x, axis=0, keepdims=True)
        for j in range(1, 4):
            moved = pltpu.roll(jnp.where(since_tall >= j, tall, 0.0), rows + lead - j, 0)[:rows]
            dx = dx + moved * taps_ref[p, 3 - j:4 - j, :]
            dtaps_ref[p, 3 - j:4 - j, :] += jnp.sum(moved * x, axis=0, keepdims=True)
        out_of_order(step, count, info_ref, dx.astype(bf16), dx_ref, slice(p * LANES, (p + 1) * LANES))


def half_specs(rows, width, steps, order):
    count = rows // PAIR

    def pair(i, info):
        return place_of(order(i) * count, info) // count

    return [
        pl.BlockSpec((rows, width), lambda i, _, info: (jnp.minimum(pair(i, info), steps // 2 - 1), 0)),
        pl.BlockSpec((rows, width), lambda i, _, info: (jnp.maximum(pair(i, info) - steps // 2, 0), 0)),
    ]


def whole_spec(shape):
    return pl.BlockSpec(shape, lambda i, *_: (0,) * len(shape))


def head_forward(near, far, logit, taps, gain, starts, info, rows=256):
    total = 2 * near.shape[0]
    steps = total // rows
    count = rows // PAIR
    per = rows // BLOCK
    chunks = total // PAIR
    flat = lambda width: pl.BlockSpec((rows, width), lambda i, *_: (i, 0))
    square = pl.BlockSpec((per, LANES, LANES), lambda i, *_: (i, 0, 0))
    fine = PAIR // HALO

    def before(i, info):
        return place_of(jnp.maximum(i * count - 1, 0), info)

    s = jax.ShapeDtypeStruct
    outs = pl.pallas_call(
        forward_body,
        grid_spec=pltpu.PrefetchScalarGridSpec(
            num_scalar_prefetch=2,
            grid=(steps,),
            in_specs=[
                *half_specs(rows, 4 * LANES, steps, lambda i: i),
                pl.BlockSpec((HALO, 4 * LANES), lambda i, _, info: (
                    jnp.minimum(before(i, info), chunks // 2 - 1) * fine + fine - 1, 0)),
                pl.BlockSpec((HALO, 4 * LANES), lambda i, _, info: (
                    jnp.maximum(before(i, info) - chunks // 2, 0) * fine + fine - 1, 0)),
                whole_spec(logit.shape),
                whole_spec(taps.shape),
                whole_spec(gain.shape),
            ],
            out_specs=[
                pl.BlockSpec((rows, LANES), lambda i, _, info: (place_of(i * count, info) // count, 0)),
                whole_spec((8, LANES)),
                pl.BlockSpec((3, rows, LANES), lambda i, *_: (0, i, 0)),
                flat(2 * LANES), flat(PAIR), flat(PAIR), flat(LANES),
                square, square, flat(LANES),
            ],
            scratch_shapes=[
                pltpu.VMEM((LANES, LANES), f32), pltpu.VMEM((total // BLOCK, LANES), f32),
                pltpu.VMEM((rows + HALO, 4 * LANES), bf16),
            ],
        ),
        out_shape=[
            s((total, LANES), bf16), s((8, LANES), f32), s((3, total, LANES), f32),
            s((total, 2 * LANES), f32), s((total, PAIR), f32), s((total, PAIR), f32), s((total, LANES), f32),
            s((total // BLOCK, LANES, LANES), f32), s((total // BLOCK, LANES, LANES), f32),
            s((total, LANES), f32),
        ],
        name="head_forward",
    )(starts, info, near, far, near, far, logit, taps, gain)
    return outs[0], outs[1][0, 0], tuple(outs[2:])


def head_backward(grad_near, grad_far, near, far, logit, taps, gain, starts, info, kept, rows=256):
    total = 2 * near.shape[0]
    steps = total // rows
    count = rows // PAIR
    per = rows // BLOCK
    back = lambda i: steps - 1 - i
    flat = lambda width: pl.BlockSpec((rows, width), lambda i, *_: (back(i), 0))
    square = pl.BlockSpec((per, LANES, LANES), lambda i, *_: (back(i), 0, 0))
    s = jax.ShapeDtypeStruct
    return pl.pallas_call(
        backward_body,
        grid_spec=pltpu.PrefetchScalarGridSpec(
            num_scalar_prefetch=2,
            grid=(steps,),
            in_specs=[
                *half_specs(rows, 4 * LANES, steps, back),
                whole_spec(logit.shape), whole_spec(taps.shape), whole_spec(gain.shape),
                *half_specs(rows, LANES, steps, back),
                pl.BlockSpec((3, rows, LANES), lambda i, *_: (0, back(i), 0)),
                flat(2 * LANES), flat(PAIR), flat(PAIR), flat(LANES), square, square, flat(LANES),
            ],
            out_specs=[
                pl.BlockSpec((rows, 4 * LANES), lambda i, _, info: (place_of(back(i) * count, info) // count, 0)),
                whole_spec(logit.shape), whole_spec(taps.shape), whole_spec((8, LANES)),
            ],
            scratch_shapes=[
                pltpu.VMEM((LANES, LANES), f32), pltpu.VMEM((3, 8, LANES), f32),
                pltpu.VMEM((rows, 4 * LANES), bf16), pltpu.VMEM((rows, LANES), bf16),
            ],
        ),
        out_shape=[s((total, 4 * LANES), bf16), s(logit.shape, f32), s(taps.shape, f32), s((8, LANES), f32)],
        name="head_backward",
    )(starts, info, near, far, logit, taps, gain, grad_near, grad_far, *kept)


def other(value, axis, bit):
    size = lax.axis_size(axis)
    return lax.ppermute(value, axis, [(i, i ^ bit) for i in range(size)])


def after(value, *done):
    return lax.optimization_barrier((value, *done))[0]


def own_order(value, index, axis, parts=4):
    size = value.shape[axis] // parts
    return jnp.concatenate(
        [lax.dynamic_slice_in_dim(value, (p ^ index) * size, size, axis) for p in range(parts)], axis
    )


def neighbour_order(value, axis, bit, parts=4):
    size = value.shape[axis] // parts
    return jnp.concatenate(
        [lax.slice_in_dim(value, (p ^ bit) * size, ((p ^ bit) + 1) * size, axis=axis) for p in range(parts)], axis
    )


def matmul(a, b, dims=((1,), (0,))):
    return lax.dot_general(a, b, (dims, ((), ())), preferred_element_type=f32)


def norm_rows(values, gain):
    scale = lax.rsqrt(jnp.mean(values * values, axis=-1, keepdims=True) + 1e-05)
    unit = values * scale
    return unit * gain, unit, scale


def norm_back(grad, unit, scale, gain):
    pulled = grad * gain
    inner = jnp.mean(pulled * unit, axis=-1, keepdims=True)
    return scale * (pulled - unit * inner), jnp.sum(grad * unit, axis=0)


def tensor_tree():
    return lax.axis_size("tensor") == 4


def inner_place():
    index = lax.axis_index("tensor")
    return (index == 1) | (index == 2)


def along_tensor(value, pairs):
    return lax.ppermute(value, "tensor", pairs)


def gather_tensor(value):
    if not tensor_tree():
        return [value] + [other(value, "tensor", s) for s in range(1, lax.axis_size("tensor"))]
    two = other(value, "tensor", 2)
    one = other(value, "tensor", 1)
    passed = along_tensor(two, [(2, 3), (1, 0)])
    middle = along_tensor(after(value, one), [(1, 2), (2, 1)])
    return [value, one, two, jnp.where(inner_place(), middle, passed)]


def spread(values):
    mine = gather_tensor(values)
    theirs = [neighbour_order(other(v, "mp", 1), 1, 1) for v in mine]
    return jnp.concatenate(mine + theirs, axis=0)


def partials(rows, body):
    return body(rows // 2, rows).astype(bf16), body(0, rows // 2)


def collect(parts):
    theirs, mine = parts
    ways = lax.axis_size("tensor")
    piece = mine.shape[0] // ways
    last = (ways - 1) * piece
    tail = mine[last:] + neighbour_order(other(theirs[last:], "mp", 1), 1, 1).astype(f32)
    rest = mine[:last] + neighbour_order(other(theirs[:last], "mp", 1), 1, 1).astype(f32)
    if not tensor_tree():
        joined = jnp.concatenate([rest, tail], axis=0)
        total = joined[:piece]
        for s in range(1, ways):
            total = total + other(joined[s * piece:(s + 1) * piece].astype(bf16), "tensor", s).astype(f32)
        return total
    low = tail.astype(bf16)
    passed = along_tensor(low, [(3, 2), (0, 1)])
    middle = along_tensor(low, [(1, 2), (2, 1)])
    two = other((rest[2 * piece:] + passed.astype(f32)).astype(bf16), "tensor", 2)
    one = other(rest[piece:2 * piece].astype(bf16), "tensor", 1)
    return rest[:piece] + middle.astype(f32) + one.astype(f32) + two.astype(f32)


def over_dp(value):
    bit = 1
    while bit < lax.axis_size("dp"):
        low = value.astype(bf16)
        value = low.astype(f32) + other(low, "dp", bit).astype(f32)
        bit *= 2
    return value


def over_all(value):
    for axis in ("mp", "tensor", "dp"):
        bit = 1
        while bit < lax.axis_size(axis):
            value = value + other(value, axis, bit)
            bit *= 2
    return value


def shards(
    tokens,
    norm_gain,
    w_proj,
    w_beta,
    conv_weight,
    out_gain,
    w_out,
    mlp_gain,
    w_in,
    w_down,
    cotangent,
    starts,
    lengths,
):
    assert lax.axis_size("mp") == 4 and starts.shape[0] == 1
    m = lax.axis_index("mp")
    core = m & 1
    place = m * lax.axis_size("tensor") + lax.axis_index("tensor")
    block = w_proj.shape[1]
    near_blocks = 2 * block

    inputs = own_order(tokens, m, 1).astype(f32)
    gain_one = own_order(norm_gain, m, 0)
    gain_two = own_order(mlp_gain, m, 0)
    scaled, unit_one, scale_one = norm_rows(inputs, gain_one)
    scaled = scaled.astype(bf16)

    pieces, _, wide = w_proj.shape
    head = wide // 4
    span = pieces * head
    heads = [
        lax.dynamic_slice_in_dim(w_proj, (j ^ m) * head, head, 2).transpose(1, 0, 2).reshape(block, span)
        for j in range(4)
    ]
    beta_rows = own_order(w_beta.T, m, 0)
    pair = lambda values, i, j, axis: jnp.concatenate([values[i], values[j]], axis)

    def with_beta(i, j):
        row = jnp.concatenate([beta_rows[i], beta_rows[j]])[None]
        return jnp.concatenate([pair(heads, i, j, 1), jnp.pad(row, ((0, HALO - 1), (0, 2 * span - 2 * block)))], 0)

    far_sent, across_sent, core_sent = with_beta(2, 0), with_beta(3, 1), with_beta(1, 3)
    far_got = other(far_sent, "mp", 2)
    across_got = other(across_sent, "mp", 3)
    core_got = other(core_sent, "mp", 1)
    own_pair = pair(heads, 0, 2, 1)
    normed = spread(after(scaled, far_sent, across_sent, core_sent))
    full_proj = jnp.concatenate([own_pair, core_got[:block], far_got[:block], across_got[:block]], axis=0)
    full_beta = jnp.concatenate(
        [jnp.stack([beta_rows[0], beta_rows[2]])]
        + [v[block, : 2 * block].reshape(2, block) for v in (core_got, far_got, across_got)],
        axis=1,
    )
    logits = matmul(full_beta, normed, ((1,), (1,))).astype(bf16)
    far_out = matmul(normed, full_proj[:, span:]).astype(bf16)
    count = far_out.shape[0]
    logit_rows = count // span
    far_sent = jnp.concatenate([far_out, jnp.pad(logits[1].reshape(logit_rows, span), ((0, HALO - logit_rows), (0, 0)))], 0)
    far = other(far_sent, "mp", 2)
    near = matmul(normed, full_proj[:, :span]).astype(bf16)
    chunk_rows = (-1, LANES)
    logit = jnp.concatenate(
        [logits[0].reshape(chunk_rows), far[count:count + logit_rows].reshape(chunk_rows)], axis=0
    ).astype(f32)

    units = w_down.shape[0]
    half = LANES * ((units // LANES + 1) // 2)
    ours = lambda v, axis: lax.dynamic_slice_in_dim(v, core * (units - half), half, axis)
    theirs = lambda v, axis: lax.dynamic_slice_in_dim(v, (1 - core) * (units - half), half, axis)
    live = (lax.broadcasted_iota(jnp.int32, (1, half), 1) >= core * (2 * half - units)).astype(f32)
    w_out = after(w_out, far)
    out_blocks = lambda v: [lax.dynamic_slice_in_dim(v, (j ^ m) * head, head, 0) for j in range(4)]
    out_mine, out_far = out_blocks(w_out), out_blocks(other(w_out, "mp", 2))
    w_down = after(w_down, far)
    down_far = other(w_down, "mp", 2)
    out_core = other(jnp.concatenate([pair(out_mine, 1, 3, 0), pair(out_far, 1, 3, 0)], axis=1), "mp", 1)
    full_out = jnp.concatenate(
        [pair(out_mine, 0, 2, 0), out_core[:, :block], pair(out_far, 0, 2, 0), out_core[:, block:]], axis=1
    )
    down_core = other(jnp.concatenate([theirs(w_down, 0), theirs(down_far, 0)], axis=1), "mp", 1)
    full_down = jnp.concatenate(
        [ours(w_down, 0), down_core[:, :block], ours(down_far, 0), down_core[:, block:]], axis=1
    )
    cot_own = own_order(cotangent, m, 1)
    cot_all = spread(after(cot_own, normed))

    taps = conv_weight.reshape(3, conv_weight.shape[1], head)
    info = jnp.stack([lengths[0], place]).astype(jnp.int32)
    head_args = (near, far, logit, taps, out_gain[None], starts[0], info)
    mixed, norm_total, kept = head_forward(*head_args)
    mixed_far = other(mixed[count:], "mp", 2)
    mixed_tok = jnp.concatenate([mixed[:count], mixed_far], axis=1)
    branch = collect(partials(count, lambda a, b: matmul(mixed_tok[a:b], full_out)))

    w_in = after(w_in, mixed_far)
    in_far = other(w_in, "mp", 2)
    in_core = other(theirs(w_in, 2), "mp", 1)
    in_across = other(theirs(in_far, 2), "mp", 1)
    full_in = jnp.concatenate([ours(w_in, 2), in_core, ours(in_far, 2), in_across], axis=1)

    middle = inputs + branch
    scaled_two, unit_two, scale_two = norm_rows(middle, gain_two)
    normed_two = spread(scaled_two.astype(bf16))

    gate = matmul(normed_two, full_in[0])
    up = matmul(normed_two, full_in[1])
    sigma = jax.nn.sigmoid(gate)
    activated = gate * sigma
    hidden = (activated * up * live).astype(bf16)
    d_hidden = matmul(cot_all, full_down, ((1,), (1,)))
    d_hidden = d_hidden * live
    d_gate = (d_hidden * up * sigma * (1.0 + gate * (1.0 - sigma))).astype(bf16)
    d_up = (d_hidden * activated).astype(bf16)
    d_normed_two = collect(
        partials(
            count,
            lambda a, b: matmul(d_gate[a:b], full_in[0], ((1,), (1,))) + matmul(d_up[a:b], full_in[1], ((1,), (1,))),
        )
    )
    d_mid_norm, g_mlp = norm_back(d_normed_two, unit_two, scale_two, gain_two)
    d_middle = cot_own.astype(f32) + d_mid_norm
    d_mid_all = spread(d_middle.astype(bf16))
    d_mixed = matmul(d_mid_all, full_out, ((1,), (1,))).astype(bf16)
    d_far = other(d_mixed[:, head:], "mp", 2)
    feed = collect(after(partials(count, lambda a, b: matmul(hidden[a:b], full_down)), d_mid_all))
    output = own_order((middle + feed).astype(bf16), m, 1)

    tn = ((0,), (0,))
    grad_dot = lambda a, b: matmul(a, b, tn)

    def joined_units(mine, theirs, axis):
        gap = units - half
        low = jnp.where(core == 0, mine, theirs)
        high = jnp.where(core == 0, theirs, mine)
        zero = jnp.zeros_like(lax.slice_in_dim(low, 0, gap, axis=axis))
        return jnp.concatenate([low, zero], axis) + jnp.concatenate([zero, high], axis)

    def units_grad(product, axis, *before):
        cut = lambda v, p: lax.slice_in_dim(v, p * block, (p + 1) * block, axis=axis)
        two = lambda i, j: jnp.concatenate([cut(product, i), cut(product, j)], axis)
        joined = joined_units(two(0, 2), other(two(1, 3), "mp", 1), 1 - axis)
        sent = cut(joined, 1)
        if before:
            sent = after(sent, *before)
        return over_dp(cut(joined, 0).astype(f32) + other(sent, "mp", 2).astype(f32))

    g_down = units_grad(grad_dot(hidden, cot_all).astype(bf16), 1)
    g_in = jnp.stack(
        [
            units_grad(grad_dot(normed_two, d_gate).astype(bf16), 0),
            units_grad(grad_dot(normed_two, d_up).astype(bf16), 0, d_far),
        ]
    )

    out_grad = grad_dot(mixed_tok, d_mid_all)
    out_back = neighbour_order(other(after(out_grad[:, near_blocks:].astype(bf16), d_far), "mp", 2), 0, 1, 2)
    out_two = (out_grad[:, :near_blocks] + out_back.astype(f32)).astype(bf16)
    out_theirs = other(out_two[:, block:], "mp", 1)
    out_mine = out_two[:, :block]
    g_out = over_dp(
        own_order(
            jnp.concatenate([out_mine[:head], out_theirs[:head], out_mine[head:], out_theirs[head:]], axis=0), m, 0
        )
    )
    d_heads, d_logit, d_taps, g_head_gain = head_backward(d_mixed[:, :head], d_far, *head_args, kept)
    d_logit = d_logit.astype(bf16)
    half_chunks = d_logit.shape[0] // 2
    d_sent = jnp.concatenate(
        [
            d_heads[count:],
            jnp.pad(d_logit[half_chunks:].reshape(logit_rows, span), ((0, HALO - logit_rows), (0, 0))),
        ],
        axis=0,
    )
    d_got = other(d_sent, "mp", 2)
    d_own = d_heads[:count]
    d_proj = jnp.concatenate([d_own, d_got[:count]], axis=1)
    d_logits = jnp.concatenate(
        [d_logit[:half_chunks].reshape(1, count), d_got[count:count + logit_rows].reshape(1, count)], axis=0
    )
    d_normed = collect(
        partials(
            count,
            lambda a, b: matmul(d_proj[a:b], full_proj, ((1,), (1,))) + matmul(d_logits[:, a:b], full_beta, tn),
        )
    )
    own_grad = grad_dot(normed, d_own)
    far_grad = grad_dot(normed, d_got[:count])
    own_back = other(own_grad[near_blocks:].astype(bf16), "mp", 2)
    far_back = other(after(far_grad[near_blocks:].astype(bf16), own_back), "mp", 2)

    def proj_part(held, back):
        two = (held[:near_blocks] + back.astype(f32)).astype(bf16)
        return over_dp(jnp.concatenate([two[:block], other(two[block:], "mp", 1)], axis=1))

    part_far = proj_part(far_grad, own_back)
    part_own = proj_part(own_grad, far_back)
    g_heads = [part_own[:, :span], part_own[:, span:], part_far[:, :span], part_far[:, span:]]
    g_proj = own_order(
        jnp.concatenate([v.reshape(block, pieces, head).transpose(1, 0, 2) for v in g_heads], axis=2), m, 2
    )
    beta_part = matmul(d_logits, normed)
    beta_back = neighbour_order(neighbour_order(other(beta_part, "mp", 2), 0, 1, 2), 1, 1, 2)
    beta_two = beta_part + beta_back
    beta_theirs = other(beta_two[:, block:near_blocks], "mp", 1)
    g_beta = own_order(
        jnp.concatenate([beta_two[:1, :block], beta_theirs[:1], beta_two[1:, :block], beta_theirs[1:]], axis=0), m, 0
    )
    small = jnp.concatenate([g_beta.reshape(-1, LANES), d_taps.reshape(-1, LANES)], axis=0)
    bit = 1
    while bit < lax.axis_size("dp"):
        small = small + other(small, "dp", bit)
        bit *= 2
    cut = g_beta.size // LANES
    g_beta = small[:cut].reshape(g_beta.shape)
    d_taps = small[cut:]
    d_in_norm, g_norm = norm_back(d_normed, unit_one, scale_one, gain_one)
    d_tokens = own_order(d_middle + d_in_norm, m, 1)
    row = lambda v: v.reshape(-1, LANES)
    sums = over_all(
        jnp.concatenate(
            [
                row(own_order(g_norm, m, 0)),
                row(own_order(g_mlp, m, 0)),
                g_head_gain[:1],
                jnp.full((1, LANES), norm_total),
            ],
            axis=0,
        )
    )
    lines = g_norm.shape[0] // LANES
    ways = lax.axis_size("mp") * lax.axis_size("tensor")
    state_norm = sums[2 * lines + 1, 0] / (ways * lax.axis_size("dp") * (2 * count // BLOCK))
    return (
        output,
        d_tokens,
        sums[:lines].reshape(-1),
        g_proj,
        g_beta.T,
        d_taps.reshape(conv_weight.shape),
        sums[2 * lines],
        g_out,
        sums[lines:2 * lines].reshape(-1),
        g_in,
        g_down,
        state_norm,
    )


def solution(mesh):
    placed = (
        P(("dp", "mp", "tensor"), None),
        P(),
        P(None, "mp", "tensor"),
        P("mp", "tensor"),
        P(None, None, "tensor", "mp", None),
        P(),
        P("tensor", "mp"),
        P(),
        P(None, "mp", "tensor"),
        P("tensor", "mp"),
        P(("dp", "mp", "tensor"), None),
        P("dp", None),
        P("dp"),
    )
    return jax.shard_map(
        shards,
        mesh=mesh,
        in_specs=placed,
        out_specs=(
            P(("dp", "mp", "tensor"), None),
            P(("dp", "mp", "tensor"), None),
            P(),
            P(None, "mp", "tensor"),
            P("mp", "tensor"),
            P(None, None, "tensor", "mp", None),
            P(),
            P("tensor", "mp"),
            P(),
            P(None, "mp", "tensor"),
            P("tensor", "mp"),
            P(),
        ),
        check_vma=False,
    )
```

```python
import jax
import jax.numpy as jnp
from jax import lax
from jax.experimental import pallas as pl
from jax.experimental.pallas import tpu as pltpu
from jax.sharding import PartitionSpec as P

BLOCK = 64
PAIR = 2 * BLOCK
LANES = 128
f32 = jnp.float32
bf16 = jnp.bfloat16


def halves(a):
    hi = a.astype(bf16)
    return hi, (a - hi.astype(f32)).astype(bf16)


def product(a, b, dims):
    return lax.dot_general(a, b, (dims, ((), ())), preferred_element_type=f32)


def close_dot(a, b, dims=((1,), (0,))):
    a_hi, a_lo = a if isinstance(a, tuple) else halves(a)
    b_hi, b_lo = b if isinstance(b, tuple) else halves(b)
    return product(a_hi, b_hi, dims) + (product(a_hi, b_lo, dims) + product(a_lo, b_hi, dims))


NN = ((1,), (0,))
NT = ((1,), (1,))
TN = ((0,), (0,))


def doc_start(places, starts_ref):
    found = jnp.zeros_like(places)
    for j in range(1, starts_ref.shape[0]):
        begin = starts_ref[j]
        found = jnp.where(places >= begin, begin, found)
    return found


def place_rows(base, rows, width=LANES):
    return base + lax.broadcasted_iota(jnp.int32, (rows, width), 0)


def pair_masks(base, begins):
    rows = lax.broadcasted_iota(jnp.int32, (PAIR, PAIR), 0)
    cols = lax.broadcasted_iota(jnp.int32, (PAIR, PAIR), 1)
    heads = (rows // BLOCK) * BLOCK
    lower = jnp.maximum(begins - base, heads)
    upto = (cols >= lower) & (cols <= rows)
    strict = (cols >= lower) & (cols < rows)
    keep = begins < base + heads
    return upto, strict, keep, (rows == cols).astype(f32)


HALO = 16


def place_of(chunk, info_ref):
    return chunk ^ info_ref[1]


def in_order(step, count, info_ref, refs, target_ref, first):
    local = place_of(step * count, info_ref)
    near = local < pl.num_programs(0) * count // 2
    for n in range(count):
        inside = (local ^ n) % count

        @pl.when(near)
        def _():
            target_ref[first + n * PAIR:first + (n + 1) * PAIR, :] = refs[0][
                pl.ds(pl.multiple_of(inside * PAIR, PAIR), PAIR), :]

        @pl.when(jnp.logical_not(near))
        def _():
            target_ref[first + n * PAIR:first + (n + 1) * PAIR, :] = refs[1][
                pl.ds(pl.multiple_of(inside * PAIR, PAIR), PAIR), :]


def out_of_order(step, count, info_ref, value, target_ref, width):
    local = place_of(step * count, info_ref)
    for n in range(count):
        inside = pl.multiple_of(((local ^ n) % count) * PAIR, PAIR)
        target_ref[pl.ds(inside, PAIR), width] = value[n * PAIR:(n + 1) * PAIR]


def column(row):
    eye = lax.broadcasted_iota(jnp.int32, (PAIR, PAIR), 0) == lax.broadcasted_iota(jnp.int32, (PAIR, PAIR), 1)
    return jnp.sum(jnp.where(eye, row, 0.0), axis=1, keepdims=True)


def columns(step, count, info_ref, ref):
    return jnp.concatenate(
        [column(ref[pl.ds(place_of(step * count + n, info_ref), 1), :]) for n in range(count)], axis=0)


def forward_body(starts_ref, info_ref, near_ref, far_ref, before_near_ref, before_far_ref, logit_ref, taps_ref,
                 gain_ref, mixed_ref, norm_ref, conv_ref, wu_ref, t_ref, a_ref, c_ref, m_ref, s_ref, o_ref,
                 state_ref, square_ref, x_ref):
    step = pl.program_id(0)
    rows = near_ref.shape[0]
    base = step * rows
    count = rows // PAIR
    half_chunks = pl.num_programs(0) * count // 2
    before = place_of(jnp.maximum(step * count - 1, 0), info_ref)

    @pl.when(before < half_chunks)
    def _():
        x_ref[:HALO, :] = before_near_ref[...]

    @pl.when(before >= half_chunks)
    def _():
        x_ref[:HALO, :] = before_far_ref[...]

    in_order(step, count, info_ref, (near_ref, far_ref), x_ref, HALO)

    @pl.when(step == 0)
    def _():
        state_ref[...] = jnp.zeros_like(state_ref)

    places = place_rows(base, rows)
    begins = doc_start(places, starts_ref)
    since = places - begins
    valid = (places < info_ref[0]).astype(f32)
    parts = []
    for p in range(3):
        tall = x_ref[:, p * LANES:(p + 1) * LANES].astype(f32)
        now = tall[HALO:]
        summed = now * taps_ref[p, 3:4, :]
        for j in range(1, 4):
            moved = pltpu.roll(tall, j, 0)[HALO:]
            summed = summed + jnp.where(since >= j, moved, 0.0) * taps_ref[p, 3 - j:4 - j, :]
        conv_ref[p] = summed
        act = summed * jax.nn.sigmoid(summed)
        if p < 2:
            act = act * lax.rsqrt(jnp.sum(act * act, axis=1, keepdims=True) + 1e-06)
        parts.append(act)
    beta = jax.nn.sigmoid(columns(step, count, info_ref, logit_ref)) * valid
    gates = x_ref[HALO:, 3 * LANES:].astype(f32)
    gates = gates * jax.nn.sigmoid(gates) * valid * gain_ref[...]
    pairs = rows // PAIR
    blocks = []
    for g in range(pairs):
        at = slice(g * PAIR, (g + 1) * PAIR)
        start = base + g * PAIR
        q, k, v, b = parts[0][at], parts[1][at], parts[2][at], beta[at]
        upto, strict, keep, eye = pair_masks(start, begins[at])
        kb = b * k
        k_two = halves(k)
        neg = jnp.where(strict, -close_dot(kb, k_two, NT), 0.0)
        inverse = eye + neg
        power = neg
        for _ in range(BLOCK.bit_length() - 2):
            power_two = halves(power)
            power = close_dot(power_two, power_two)
            inverse = inverse + close_dot(inverse, power)
        wu = close_dot(inverse, jnp.concatenate([jnp.where(keep, kb, 0.0), b * v], axis=1))
        wu_two = halves(wu)
        scores = jnp.where(upto, close_dot(q, k_two, NT), 0.0)
        cd = close_dot(scores, wu_two)
        c = jnp.where(keep, q, 0.0) - cd[:, :LANES]
        wu_ref[at] = wu
        t_ref[at] = inverse
        a_ref[at] = scores
        c_ref[at] = c
        for h in range(2):
            inner = slice(h * BLOCK, (h + 1) * BLOCK)
            first = start + h * BLOCK
            final = doc_start(first + BLOCK - 1, starts_ref)
            tail = place_rows(first, BLOCK) >= final
            k_last = jnp.where(tail, k[inner], 0.0)
            mb = close_dot(k_last, (wu_two[0][inner], wu_two[1][inner]), TN)
            kept = jnp.where(final < first, 1.0, 0.0)
            m = kept * eye - mb[:, :LANES]
            m_ref[g * 2 + h] = m
            blocks.append((halves(m), mb[:, LANES:], c[inner], cd[inner, LANES:]))
    state = state_ref[...]
    results = []
    for n, (m_two, addend, c, d) in enumerate(blocks):
        s_ref[n] = state
        s_two = halves(state)
        results.append(close_dot(c, s_two) + d)
        state = close_dot(m_two, s_two) + addend
        square_ref[pl.ds(step * len(blocks) + n, 1), :] = jnp.sum(state * state, axis=0, keepdims=True)
    state_ref[...] = state
    result = jnp.concatenate(results, axis=0)
    o_ref[...] = result
    unit = result * lax.rsqrt(jnp.mean(result * result, axis=1, keepdims=True) + 1e-05)
    out_of_order(step, count, info_ref, (unit * gates).astype(bf16), mixed_ref, slice(None))

    @pl.when(step == pl.num_programs(0) - 1)
    def _():
        sizes = jnp.sqrt(jnp.sum(square_ref[...], axis=1, keepdims=True) + 1e-12)
        norm_ref[...] = jnp.broadcast_to(jnp.sum(sizes, axis=0, keepdims=True), norm_ref.shape)


def backward_body(starts_ref, info_ref, near_ref, far_ref, logit_ref, taps_ref, gain_ref, grad_near_ref,
                  grad_far_ref, conv_ref, wu_ref, t_ref, a_ref, c_ref, m_ref, s_ref, o_ref,
                  dx_ref, dlogit_ref, dtaps_ref, dgain_ref, dstate_ref, after_ref, x_ref, grad_ref):
    step = pl.num_programs(0) - 1 - pl.program_id(0)
    rows = near_ref.shape[0]
    base = step * rows
    count = rows // PAIR
    in_order(step, count, info_ref, (near_ref, far_ref), x_ref, 0)
    in_order(step, count, info_ref, (grad_near_ref, grad_far_ref), grad_ref, 0)

    @pl.when(pl.program_id(0) == 0)
    def _():
        dstate_ref[...] = jnp.zeros_like(dstate_ref)
        after_ref[...] = jnp.zeros_like(after_ref)
        dtaps_ref[...] = jnp.zeros_like(dtaps_ref)
        dgain_ref[...] = jnp.zeros_like(dgain_ref)

    lead = after_ref.shape[1]
    places_tall = place_rows(base, rows + lead)
    begins_tall = doc_start(places_tall, starts_ref)
    since_tall = places_tall - begins_tall
    places, begins = places_tall[:rows], begins_tall[:rows]
    valid = (places < info_ref[0]).astype(f32)
    gain = gain_ref[...]
    gate = x_ref[:, 3 * LANES:].astype(f32)
    gate_sig = jax.nn.sigmoid(gate)
    gate_act = gate * gate_sig
    o = o_ref[...]
    r = lax.rsqrt(jnp.mean(o * o, axis=1, keepdims=True) + 1e-05)
    unit = o * r
    grad = grad_ref[...].astype(f32) * valid
    gu = grad * unit
    dgain_ref[0:1, :] += jnp.sum(gu * gate_act, axis=0, keepdims=True)
    dgate = (gu * gain * (gate_sig * (1.0 + gate * (1.0 - gate_sig)))).astype(bf16)
    out_of_order(step, count, info_ref, dgate, dx_ref, slice(3 * LANES, 4 * LANES))
    dunit = grad * gain * gate_act
    d_o = r * (dunit - unit * jnp.mean(dunit * unit, axis=1, keepdims=True))
    convs, sigs, acts, scales, units = [], [], [], [], []
    for p in range(3):
        conv = conv_ref[p]
        sig = jax.nn.sigmoid(conv)
        act = conv * sig
        convs.append(conv)
        sigs.append(sig)
        if p < 2:
            scale = lax.rsqrt(jnp.sum(act * act, axis=1, keepdims=True) + 1e-06)
            scales.append(scale)
            units.append(act * scale)
        else:
            units.append(act)
    logit_sig = jax.nn.sigmoid(columns(step, count, info_ref, logit_ref))
    beta = logit_sig * valid
    pairs = rows // PAIR
    do_two = halves(d_o)
    pieces = [None] * (2 * pairs)
    for n in range(2 * pairs):
        inner = slice(n * BLOCK, (n + 1) * BLOCK)
        pieces[n] = close_dot(c_ref[inner, :], (do_two[0][inner], do_two[1][inner]), TN)
    dstate = dstate_ref[...]
    dstates = [None] * (2 * pairs)
    for n in reversed(range(2 * pairs)):
        d_two = halves(dstate)
        dstates[n] = d_two
        dstate = close_dot(m_ref[n], d_two, TN) + pieces[n]
    dstate_ref[...] = dstate
    grads = [[], [], []]
    dbetas = []
    for g in range(pairs):
        at = slice(g * PAIR, (g + 1) * PAIR)
        start = base + g * PAIR
        q, k, v, b = units[0][at], units[1][at], units[2][at], beta[at]
        upto, strict, keep, eye = pair_masks(start, begins[at])
        wu = wu_ref[at, :]
        wu_two = halves(wu)
        a_two = halves(a_ref[at, :])
        k_two = halves(k)
        do_pair = (do_two[0][at], do_two[1][at])
        p_rows, dp_rows, dq_rows, dk_rows, dw_rows = [], [], [], [], []
        later = close_dot(a_two, do_pair, TN)
        for h in range(2):
            n = g * 2 + h
            inner = slice(h * BLOCK, (h + 1) * BLOCK)
            first = start + h * BLOCK
            final = doc_start(first + BLOCK - 1, starts_ref)
            tail = place_rows(first, BLOCK) >= final
            s_two = halves(s_ref[n])
            ds_two = dstates[n]
            wu_in = (wu_two[0][inner, :LANES], wu_two[1][inner, :LANES])
            p = wu[inner, LANES:] - close_dot(wu_in, s_two)
            p_two = halves(p)
            k_last = jnp.where(tail, k[inner], 0.0)
            dp = later[inner] + close_dot(k_last, ds_two)
            dp_two = halves(dp)
            p_rows.append(p_two)
            dp_rows.append(dp)
            do_in = (do_pair[0][inner], do_pair[1][inner])
            dq_rows.append(close_dot(do_in, s_two, NT))
            dk_rows.append(jnp.where(tail, close_dot(p_two, ds_two, NT), 0.0))
            dw_rows.append(-close_dot(dp_two, s_two, NT))
        p_two = tuple(jnp.concatenate([p_rows[0][i], p_rows[1][i]], axis=0) for i in range(2))
        dp = jnp.concatenate(dp_rows, axis=0)
        da_two = halves(jnp.where(upto, close_dot(do_pair, p_two, NT), 0.0))
        q_two = halves(q)
        dq = jnp.where(keep, jnp.concatenate(dq_rows, axis=0), 0.0) + close_dot(da_two, k_two)
        dk = jnp.concatenate(dk_rows, axis=0) + close_dot(da_two, q_two, TN)
        dwu = jnp.concatenate([jnp.concatenate(dw_rows, axis=0), dp], axis=1)
        dbkv = close_dot(t_ref[at, :], dwu, TN)
        dl_two = halves(jnp.where(strict, -close_dot(dbkv, wu_two, NT), 0.0))
        dkb = close_dot(dl_two, k_two) + jnp.where(keep, dbkv[:, :LANES], 0.0)
        dbv = dbkv[:, LANES:]
        dk = dk + b * dkb + close_dot(dl_two, b * k, TN)
        grads[0].append(dq)
        grads[1].append(dk)
        grads[2].append(b * dbv)
        dbetas.append(jnp.sum(k * dkb + v * dbv, axis=1, keepdims=True))
    dbeta = jnp.concatenate(dbetas, axis=0)
    dlogit = dbeta * (beta * (1.0 - logit_sig))
    eye = lax.broadcasted_iota(jnp.int32, (PAIR, PAIR), 0) == lax.broadcasted_iota(jnp.int32, (PAIR, PAIR), 1)
    for n in range(count):
        row = jnp.sum(jnp.where(eye, dlogit[n * PAIR:(n + 1) * PAIR], 0.0), axis=0, keepdims=True)
        dlogit_ref[pl.ds(place_of(step * count + n, info_ref), 1), :] = row
    for p in range(3):
        dact = jnp.concatenate(grads[p], axis=0)
        if p < 2:
            dact = scales[p] * (dact - units[p] * jnp.sum(dact * units[p], axis=1, keepdims=True))
        dconv = dact * (sigs[p] * (1.0 + convs[p] * (1.0 - sigs[p])))
        tall = jnp.concatenate([dconv, after_ref[p]], axis=0)
        after_ref[p] = dconv[:lead]
        x = x_ref[:, p * LANES:(p + 1) * LANES].astype(f32)
        dx = dconv * taps_ref[p, 3:4, :]
        dtaps_ref[p, 3:4, :] += jnp.sum(dconv * x, axis=0, keepdims=True)
        for j in range(1, 4):
            moved = pltpu.roll(jnp.where(since_tall >= j, tall, 0.0), rows + lead - j, 0)[:rows]
            dx = dx + moved * taps_ref[p, 3 - j:4 - j, :]
            dtaps_ref[p, 3 - j:4 - j, :] += jnp.sum(moved * x, axis=0, keepdims=True)
        out_of_order(step, count, info_ref, dx.astype(bf16), dx_ref, slice(p * LANES, (p + 1) * LANES))


def half_specs(rows, width, steps, order):
    count = rows // PAIR

    def pair(i, info):
        return place_of(order(i) * count, info) // count

    return [
        pl.BlockSpec((rows, width), lambda i, _, info: (jnp.minimum(pair(i, info), steps // 2 - 1), 0)),
        pl.BlockSpec((rows, width), lambda i, _, info: (jnp.maximum(pair(i, info) - steps // 2, 0), 0)),
    ]


def whole_spec(shape):
    return pl.BlockSpec(shape, lambda i, *_: (0,) * len(shape))


def head_forward(near, far, logit, taps, gain, starts, info, rows=256):
    total = 2 * near.shape[0]
    steps = total // rows
    count = rows // PAIR
    per = rows // BLOCK
    chunks = total // PAIR
    flat = lambda width: pl.BlockSpec((rows, width), lambda i, *_: (i, 0))
    square = pl.BlockSpec((per, LANES, LANES), lambda i, *_: (i, 0, 0))
    fine = PAIR // HALO

    def before(i, info):
        return place_of(jnp.maximum(i * count - 1, 0), info)

    s = jax.ShapeDtypeStruct
    outs = pl.pallas_call(
        forward_body,
        grid_spec=pltpu.PrefetchScalarGridSpec(
            num_scalar_prefetch=2,
            grid=(steps,),
            in_specs=[
                *half_specs(rows, 4 * LANES, steps, lambda i: i),
                pl.BlockSpec((HALO, 4 * LANES), lambda i, _, info: (
                    jnp.minimum(before(i, info), chunks // 2 - 1) * fine + fine - 1, 0)),
                pl.BlockSpec((HALO, 4 * LANES), lambda i, _, info: (
                    jnp.maximum(before(i, info) - chunks // 2, 0) * fine + fine - 1, 0)),
                whole_spec(logit.shape),
                whole_spec(taps.shape),
                whole_spec(gain.shape),
            ],
            out_specs=[
                pl.BlockSpec((rows, LANES), lambda i, _, info: (place_of(i * count, info) // count, 0)),
                whole_spec((8, LANES)),
                pl.BlockSpec((3, rows, LANES), lambda i, *_: (0, i, 0)),
                flat(2 * LANES), flat(PAIR), flat(PAIR), flat(LANES),
                square, square, flat(LANES),
            ],
            scratch_shapes=[
                pltpu.VMEM((LANES, LANES), f32), pltpu.VMEM((total // BLOCK, LANES), f32),
                pltpu.VMEM((rows + HALO, 4 * LANES), bf16),
            ],
        ),
        out_shape=[
            s((total, LANES), bf16), s((8, LANES), f32), s((3, total, LANES), f32),
            s((total, 2 * LANES), f32), s((total, PAIR), f32), s((total, PAIR), f32), s((total, LANES), f32),
            s((total // BLOCK, LANES, LANES), f32), s((total // BLOCK, LANES, LANES), f32),
            s((total, LANES), f32),
        ],
        name="head_forward",
        cost_estimate=pl.CostEstimate(flops=total * 20_000_000, transcendentals=0, bytes_accessed=total * 10_000),
    )(starts, info, near, far, near, far, logit, taps, gain)
    return outs[0], outs[1][0, 0], tuple(outs[2:])


def head_backward(grad_near, grad_far, near, far, logit, taps, gain, starts, info, kept, rows=256):
    total = 2 * near.shape[0]
    steps = total // rows
    count = rows // PAIR
    per = rows // BLOCK
    back = lambda i: steps - 1 - i
    flat = lambda width: pl.BlockSpec((rows, width), lambda i, *_: (back(i), 0))
    square = pl.BlockSpec((per, LANES, LANES), lambda i, *_: (back(i), 0, 0))
    s = jax.ShapeDtypeStruct
    return pl.pallas_call(
        backward_body,
        grid_spec=pltpu.PrefetchScalarGridSpec(
            num_scalar_prefetch=2,
            grid=(steps,),
            in_specs=[
                *half_specs(rows, 4 * LANES, steps, back),
                whole_spec(logit.shape), whole_spec(taps.shape), whole_spec(gain.shape),
                *half_specs(rows, LANES, steps, back),
                pl.BlockSpec((3, rows, LANES), lambda i, *_: (0, back(i), 0)),
                flat(2 * LANES), flat(PAIR), flat(PAIR), flat(LANES), square, square, flat(LANES),
            ],
            out_specs=[
                pl.BlockSpec((rows, 4 * LANES), lambda i, _, info: (place_of(back(i) * count, info) // count, 0)),
                whole_spec(logit.shape), whole_spec(taps.shape), whole_spec((8, LANES)),
            ],
            scratch_shapes=[
                pltpu.VMEM((LANES, LANES), f32), pltpu.VMEM((3, 8, LANES), f32),
                pltpu.VMEM((rows, 4 * LANES), bf16), pltpu.VMEM((rows, LANES), bf16),
            ],
        ),
        out_shape=[s((total, 4 * LANES), bf16), s(logit.shape, f32), s(taps.shape, f32), s((8, LANES), f32)],
        name="head_backward",
        cost_estimate=pl.CostEstimate(flops=total * 18_000_000, transcendentals=0, bytes_accessed=total * 10_000),
    )(starts, info, near, far, logit, taps, gain, grad_near, grad_far, *kept)


def other(value, axis, bit):
    size = lax.axis_size(axis)
    return lax.ppermute(value, axis, [(i, i ^ bit) for i in range(size)])


def after(value, *done):
    return lax.optimization_barrier((value, *done))[0]


def own_order(value, index, axis, parts=4):
    size = value.shape[axis] // parts
    return jnp.concatenate(
        [lax.dynamic_slice_in_dim(value, (p ^ index) * size, size, axis) for p in range(parts)], axis
    )


def neighbour_order(value, axis, bit, parts=4):
    size = value.shape[axis] // parts
    return jnp.concatenate(
        [lax.slice_in_dim(value, (p ^ bit) * size, ((p ^ bit) + 1) * size, axis=axis) for p in range(parts)], axis
    )


def matmul(a, b, dims=((1,), (0,))):
    return lax.dot_general(a, b, (dims, ((), ())), preferred_element_type=f32)


def norm_rows(values, gain):
    scale = lax.rsqrt(jnp.mean(values * values, axis=-1, keepdims=True) + 1e-05)
    unit = values * scale
    return unit * gain, unit, scale


def norm_back(grad, unit, scale, gain):
    pulled = grad * gain
    inner = jnp.mean(pulled * unit, axis=-1, keepdims=True)
    return scale * (pulled - unit * inner), jnp.sum(grad * unit, axis=0)


def tensor_tree():
    return lax.axis_size("tensor") == 4


def inner_place():
    index = lax.axis_index("tensor")
    return (index == 1) | (index == 2)


def along_tensor(value, pairs):
    return lax.ppermute(value, "tensor", pairs)


def gather_tensor(value, tree=True, before=()):
    if not tree or not tensor_tree():
        return [value] + [other(value, "tensor", s) for s in range(1, lax.axis_size("tensor"))]
    two = after(other(value, "tensor", 2), *before)
    one = other(value, "tensor", 1)
    passed = along_tensor(two, [(2, 3), (1, 0)])
    middle = along_tensor(after(value, one), [(1, 2), (2, 1)])
    return [value, one, two, jnp.where(inner_place(), middle, passed)]


def with_core(mine, theirs=()):
    came = list(theirs) + [other(v, "mp", 1) for v in mine[len(theirs):]]
    return jnp.concatenate(mine + [neighbour_order(v, 1, 1) for v in came], axis=0)


def spread(values):
    return with_core(gather_tensor(values))


def partials(rows, body):
    return body(rows // 2, rows).astype(bf16), body(0, rows // 2)


def collect_pieces(parts, before=()):
    theirs, mine = parts
    ways = lax.axis_size("tensor")
    piece = mine.shape[0] // ways
    if not tensor_tree():
        joined = mine + neighbour_order(other(theirs, "mp", 1), 1, 1).astype(f32)
        sent = [joined[s * piece:(s + 1) * piece].astype(bf16) for s in range(1, ways)]
        return joined[:piece], [other(v, "tensor", s + 1) for s, v in enumerate(sent)], sent
    last = (ways - 1) * piece
    tail = mine[last:] + neighbour_order(other(theirs[last:], "mp", 1), 1, 1).astype(f32)
    rest = mine[:last] + neighbour_order(other(theirs[:last], "mp", 1), 1, 1).astype(f32)
    low = tail.astype(bf16)
    passed = along_tensor(low, [(3, 2), (0, 1)])
    middle = along_tensor(low, [(1, 2), (2, 1)])
    sent = [(rest[2 * piece:] + passed.astype(f32)).astype(bf16), rest[piece:2 * piece].astype(bf16)]
    sent = list(after(sent, middle, *before))
    return rest[:piece], [middle, other(sent[0], "tensor", 2), other(sent[1], "tensor", 1)], sent


def added(own, received):
    for v in received:
        own = own + v.astype(f32)
    return own


def over_dp_pieces(value):
    bit = 1
    low = value.astype(bf16)
    came = other(low, "dp", bit)
    while 2 * bit < lax.axis_size("dp"):
        bit *= 2
        low = (low.astype(f32) + came.astype(f32)).astype(bf16)
        came = other(low, "dp", bit)
    return low, came


def summed(low, came):
    return low.astype(f32) + came.astype(f32)


def over_all(value):
    for axis in ("mp", "tensor"):
        if lax.axis_size(axis) == 4:
            one, two, three = [other(value, axis, bit) for bit in (1, 2, 3)]
            value = (value + one) + (two + three)
        else:
            bit = 1
            while bit < lax.axis_size(axis):
                value = value + other(value, axis, bit)
                bit *= 2
    bit = 1
    while bit < lax.axis_size("dp"):
        value = value + other(value, "dp", bit)
        bit *= 2
    return value


def shards(
    tokens,
    norm_gain,
    w_proj,
    w_beta,
    conv_weight,
    out_gain,
    w_out,
    mlp_gain,
    w_in,
    w_down,
    cotangent,
    starts,
    lengths,
):
    assert lax.axis_size("mp") == 4 and starts.shape[0] == 1
    m = lax.axis_index("mp")
    core = m & 1
    place = m * lax.axis_size("tensor") + lax.axis_index("tensor")
    block = w_proj.shape[1]
    near_blocks = 2 * block

    pieces, _, wide = w_proj.shape
    head = wide // 4
    span = pieces * head
    pair = lambda values, i, j, axis: jnp.concatenate([values[i], values[j]], axis)
    proj_got = other(w_proj, "mp", 2)
    beta_mine = w_beta.T
    beta_got = other(beta_mine, "mp", 2)
    scaled = own_order(norm_rows(tokens.astype(f32), norm_gain)[0].astype(bf16), m, 1)
    normed = spread(scaled)
    inputs = own_order(after(tokens, normed), m, 1).astype(f32)
    gain_one = own_order(norm_gain, m, 0)
    gain_two = own_order(mlp_gain, m, 0)
    _, unit_one, scale_one = norm_rows(inputs, gain_one)

    def head_blocks(v):
        return [
            lax.dynamic_slice_in_dim(v, (j ^ m) * head, head, 2).transpose(1, 0, 2).reshape(block, span)
            for j in range(4)
        ]

    proj_mine, proj_far = head_blocks(w_proj), head_blocks(proj_got)
    proj_low = jnp.concatenate([pair(proj_mine, 0, 2, 1), other(pair(proj_mine, 1, 3, 1), "mp", 1)], axis=0)
    proj_high = jnp.concatenate([pair(proj_far, 0, 2, 1), other(pair(proj_far, 1, 3, 1), "mp", 1)], axis=0)
    beta_both = jnp.concatenate([beta_mine, after(beta_got, proj_got)], axis=1)
    beta_all = own_order(jnp.concatenate([beta_both, other(beta_both, "mp", 1)], axis=1), m, 0)
    beta_all = pair([beta_all[0:1], beta_all[2:3]], 0, 1, 0)
    full_beta = jnp.concatenate([beta_all[:, p * block:(p + 1) * block] for p in (0, 2, 1, 3)], axis=1)
    logits = matmul(full_beta, normed, ((1,), (1,))).astype(bf16)
    normed_low, normed_high = normed[:, :near_blocks], normed[:, near_blocks:]
    far_out = (matmul(normed_low, proj_low[:, span:]) + matmul(normed_high, proj_high[:, span:])).astype(bf16)
    count = far_out.shape[0]
    logit_rows = count // span
    far_sent = jnp.concatenate([far_out, jnp.pad(logits[1].reshape(logit_rows, span), ((0, HALO - logit_rows), (0, 0)))], 0)
    units = w_down.shape[0]
    half = LANES * ((units // LANES + 1) // 2)
    ours = lambda v, axis: lax.dynamic_slice_in_dim(v, core * (units - half), half, axis)
    theirs = lambda v, axis: lax.dynamic_slice_in_dim(v, (1 - core) * (units - half), half, axis)
    cot_own = own_order(cotangent, m, 1)
    early = after((theirs(w_down, 0), theirs(w_in, 2), cot_own), far_sent)
    down_core, in_core, cot_core = [other(v, "mp", 1) for v in early]
    full_proj = jnp.concatenate(after((proj_low, proj_high), far_sent), axis=0)
    far = after(other(far_sent, "mp", 2), down_core, in_core, cot_core, full_proj)
    near_low, near_high = after((normed_low, normed_high), far_sent)
    near = (matmul(near_low, proj_low[:, :span]) + matmul(near_high, proj_high[:, :span])).astype(bf16)
    chunk_rows = (-1, LANES)
    logit = jnp.concatenate(
        [logits[0].reshape(chunk_rows), far[count:count + logit_rows].reshape(chunk_rows)], axis=0
    ).astype(f32)

    live = (lax.broadcasted_iota(jnp.int32, (1, half), 1) >= core * (2 * half - units)).astype(f32)
    out_blocks = lambda v: [lax.dynamic_slice_in_dim(v, (j ^ m) * head, head, 0) for j in range(4)]
    rows_sent = after(jnp.concatenate([w_out, w_down], axis=0), far)
    rows_got = other(rows_sent, "mp", 2)
    cot_pieces = gather_tensor(after(cot_own, far), tree=False)

    taps = conv_weight.reshape(3, conv_weight.shape[1], head)
    info = jnp.stack([lengths[0], place]).astype(jnp.int32)
    head_args = (near, far, logit, taps, out_gain[None], starts[0], info)
    mixed, norm_total, kept = head_forward(*head_args)
    mixed = after(mixed, rows_got, *cot_pieces)
    mixed_far = other(mixed[count:], "mp", 2)
    out_mine, out_far = out_blocks(w_out), out_blocks(rows_got[: w_out.shape[0]])
    out_sent = jnp.concatenate([pair(out_mine, 1, 3, 0), pair(out_far, 1, 3, 0)], axis=1)
    out_core = other(after(out_sent, mixed), "mp", 1)
    full_out = jnp.concatenate(
        [pair(out_mine, 0, 2, 0), out_core[:, :block], pair(out_far, 0, 2, 0), out_core[:, block:]], axis=1
    )
    mixed_tok = jnp.concatenate([mixed[:count], mixed_far], axis=1)
    branch_parts = partials(count, lambda a, b: matmul(mixed_tok[a:b], full_out))
    gate_first = other(after(w_in[0, : block // 2], mixed_far), "mp", 2)
    gate_second = other(after(w_in[0, block // 2:], mixed_far), "mp", 2)
    branch_own, branch_got, branch_sent = collect_pieces(branch_parts, before=(gate_first,))
    branch = added(branch_own, branch_got)
    up_far = other(after(w_in[1], branch_sent), "mp", 2)

    middle = inputs + branch
    scaled_two, unit_two, scale_two = norm_rows(middle, gain_two)
    low_two = after(scaled_two.astype(bf16), gate_second)
    down_far = after(rows_got, low_two)[w_out.shape[0]:]
    down_across = other(theirs(down_far, 0), "mp", 1)
    cot_across = other(after(jnp.concatenate(cot_pieces[1:], axis=0), low_two), "mp", 1)
    piece = cot_own.shape[0]
    theirs_cot = [cot_core] + [cot_across[s * piece:(s + 1) * piece] for s in range(len(cot_pieces) - 1)]
    cot_all = with_core(cot_pieces, theirs_cot)
    full_down = jnp.concatenate([ours(w_down, 0), down_core, ours(down_far, 0), down_across], axis=1)
    d_hidden = matmul(cot_all, full_down, ((1,), (1,)))
    two_pieces = gather_tensor(low_two, before=(up_far,))
    normed_two = after(with_core(two_pieces), d_hidden)
    gate_far = jnp.concatenate([after(gate_first, low_two), after(gate_second, low_two)], axis=0)
    in_far = [gate_far, after(up_far, two_pieces[2])]
    full_in = [
        after(
            jnp.concatenate([ours(w_in[i], 1), in_core[i], ours(v, 1), other(theirs(v, 1), "mp", 1)], axis=0), d_hidden
        )
        for i, v in enumerate(in_far)
    ]

    gate = matmul(normed_two, full_in[0])
    up = matmul(normed_two, full_in[1])
    sigma = jax.nn.sigmoid(gate)
    activated = gate * sigma
    hidden = (activated * up * live).astype(bf16)
    d_hidden = d_hidden * live
    d_gate = (d_hidden * up * sigma * (1.0 + gate * (1.0 - sigma))).astype(bf16)
    d_up = (d_hidden * activated).astype(bf16)
    two_parts = partials(
        count,
        lambda a, b: matmul(d_gate[a:b], full_in[0], ((1,), (1,))) + matmul(d_up[a:b], full_in[1], ((1,), (1,))),
    )
    two_own, two_got, two_sent = collect_pieces(two_parts)
    d_normed_two = added(two_own, two_got)
    hidden, d_gate, d_up = after((hidden, d_gate, d_up), two_sent)
    tn = ((0,), (0,))
    grad_dot = lambda a, b: matmul(a, b, tn)

    def joined_units(mine, theirs, axis):
        gap = units - half
        low = jnp.where(core == 0, mine, theirs)
        high = jnp.where(core == 0, theirs, mine)
        zero = jnp.zeros_like(lax.slice_in_dim(low, 0, gap, axis=axis))
        return jnp.concatenate([low, zero], axis) + jnp.concatenate([zero, high], axis)

    def units_joined(product, axis):
        cut = lambda v, p: lax.slice_in_dim(v, p * block, (p + 1) * block, axis=axis)
        two = lambda i, j: jnp.concatenate([cut(product, i), cut(product, j)], axis)
        joined = joined_units(two(0, 2), other(two(1, 3), "mp", 1), 1 - axis)
        return cut(joined, 0), cut(joined, 1)

    down_product = grad_dot(hidden, cot_all).astype(bf16)
    gate_product = grad_dot(normed_two, after(d_gate, down_product)).astype(bf16)
    down_held, down_sent = units_joined(down_product, 1)
    up_product = grad_dot(normed_two, after(d_up, gate_product, down_sent)).astype(bf16)
    gate_held, gate_sent = units_joined(gate_product, 0)
    up_held, up_sent = units_joined(up_product, 0)
    down_got = other(down_sent, "mp", 2)

    d_mid_norm, g_mlp = norm_back(d_normed_two, unit_two, scale_two, gain_two)
    d_middle = cot_own.astype(f32) + d_mid_norm
    d_mid_low = after(d_middle.astype(bf16), down_sent, gate_sent)
    d_mid_pieces = gather_tensor(d_mid_low)
    gate_got = other(after(gate_sent, d_mid_pieces[2]), "mp", 2)
    down_sums = over_dp_pieces(summed(down_held, after(down_got, d_mid_pieces[2])))
    feed_parts = partials(count, lambda a, b: matmul(hidden[a:b], full_down))
    feed_theirs = other(after(feed_parts[0], d_mid_pieces[2]), "mp", 1)
    feed_joined = feed_parts[1] + neighbour_order(feed_theirs, 1, 1).astype(f32)
    piece_rows = feed_joined.shape[0] // lax.axis_size("tensor")
    feed_sent = [
        feed_joined[p * piece_rows:(p + 1) * piece_rows].astype(bf16) for p in range(1, lax.axis_size("tensor"))
    ]
    d_mid_all = after(with_core(d_mid_pieces), down_got, feed_sent)
    d_mixed = matmul(d_mid_all, full_out, ((1,), (1,))).astype(bf16)
    d_far = other(d_mixed[:, head:], "mp", 2)
    gate_sums = over_dp_pieces(summed(gate_held, after(gate_got, down_sums[1], d_mixed)))
    feed_got = [other(after(v, d_mid_all), "tensor", p + 1) for p, v in enumerate(feed_sent)]
    feed_own = feed_joined[:piece_rows]
    output = own_order((middle + added(feed_own, feed_got)).astype(bf16), m, 1)

    out_grad = grad_dot(mixed_tok, d_mid_all)
    out_sent = out_grad[:, near_blocks:].astype(bf16)
    late_sent = jnp.concatenate(
        [up_sent, jnp.concatenate([out_sent[:, :block], out_sent[:, block:]], axis=0)], axis=1
    )
    late_got = other(after(late_sent, d_far), "mp", 2)
    d_near = after(d_mixed[:, :head], gate_got, down_sums[1])
    d_heads, d_logit, d_taps, g_head_gain = head_backward(d_near, d_far, *head_args, kept)
    d_heads, d_logit = after((d_heads, d_logit), late_got, gate_sums[1], *feed_got)
    d_own = d_heads[:count]
    d_logit = d_logit.astype(bf16)
    half_chunks = d_logit.shape[0] // 2
    d_sent = jnp.concatenate(
        [
            d_heads[count:],
            jnp.pad(d_logit[half_chunks:].reshape(logit_rows, span), ((0, HALO - logit_rows), (0, 0))),
        ],
        axis=0,
    )
    d_got = other(d_sent, "mp", 2)
    d_proj = jnp.concatenate([d_own, d_got[:count]], axis=1)
    d_logits = jnp.concatenate(
        [d_logit[:half_chunks].reshape(1, count), d_got[count:count + logit_rows].reshape(1, count)], axis=0
    )
    late_got = after(late_got, d_sent)
    out_got = jnp.concatenate([late_got[: 2 * head, units:], late_got[2 * head:, units:]], axis=1)
    out_two = (out_grad[:, :near_blocks] + neighbour_order(out_got, 0, 1, 2).astype(f32)).astype(bf16)
    out_theirs = other(out_two[:, block:], "mp", 1)
    out_mine = out_two[:, :block]
    out_rows = jnp.concatenate([out_mine[:head], out_theirs[:head], out_mine[head:], out_theirs[head:]], axis=0)
    up_two = summed(up_held, late_got[:, :units]).astype(bf16)
    late_sums = over_dp_pieces(jnp.concatenate([up_two, out_rows], axis=1))
    normed_parts = partials(
        count,
        lambda a, b: matmul(d_proj[a:b], full_proj, ((1,), (1,))) + matmul(d_logits[:, a:b], full_beta, tn),
    )
    normed_own, normed_got, normed_sent = collect_pieces(normed_parts)
    d_normed = added(normed_own, normed_got)
    own_grad = grad_dot(normed, after(d_own, d_sent))
    far_grad = grad_dot(normed, after(d_got, normed_parts)[:count])
    own_back = other(own_grad[near_blocks:].astype(bf16), "mp", 2)
    far_back = other(after(far_grad[near_blocks:].astype(bf16), normed_sent), "mp", 2)

    def proj_part(held, back):
        two = (held[:near_blocks] + back.astype(f32)).astype(bf16)
        return jnp.concatenate([two[:block], other(two[block:], "mp", 1)], axis=1)

    far_part = after(proj_part(far_grad, after(own_back, normed_sent)), late_sums[1])
    far_sums = over_dp_pieces(far_part)
    own_part = proj_part(own_grad, after(far_back, normed_got))
    own_sums = over_dp_pieces(own_part)
    part_far, part_own = summed(*far_sums), summed(*own_sums)
    g_heads = [part_own[:, :span], part_own[:, span:], part_far[:, :span], part_far[:, span:]]
    g_proj = own_order(
        jnp.concatenate([v.reshape(block, pieces, head).transpose(1, 0, 2) for v in g_heads], axis=2), m, 2
    )
    beta_part = after(matmul(after(d_logits, far_part), normed), far_sums[1], own_part)
    beta_back = neighbour_order(neighbour_order(other(beta_part, "mp", 2), 0, 1, 2), 1, 1, 2)
    beta_two = beta_part + beta_back
    beta_theirs = other(beta_two[:, block:near_blocks], "mp", 1)
    g_beta = own_order(
        jnp.concatenate([beta_two[:1, :block], beta_theirs[:1], beta_two[1:, :block], beta_theirs[1:]], axis=0), m, 0
    )
    small = jnp.concatenate([g_beta.reshape(-1, LANES), d_taps.reshape(-1, LANES)], axis=0)
    bit = 1
    while bit < lax.axis_size("dp"):
        small = small + other(small, "dp", bit)
        bit *= 2
    cut = g_beta.size // LANES
    g_beta = small[:cut].reshape(g_beta.shape)
    d_taps = small[cut:]
    normed_again, partial_rows = after((normed, normed_parts), far_part)
    g_norm = (
        jnp.sum(normed_again[: count // 2].astype(f32) * partial_rows[1], axis=0)
        + jnp.sum(normed_again[count // 2:].astype(f32) * partial_rows[0].astype(f32), axis=0)
    ) / gain_one
    row = lambda v: v.reshape(-1, LANES)
    rows_all = [own_order(row(g_norm), m, 0), own_order(row(g_mlp), m, 0), g_head_gain[:1]]
    rows_all.append(jnp.full((1, LANES), norm_total))
    sums = over_all(after(jnp.concatenate(rows_all, axis=0), far_sums[1], own_part))
    d_in_norm, _ = norm_back(d_normed, unit_one, scale_one, gain_one)
    d_tokens = own_order(d_middle + d_in_norm, m, 1)
    down_sums, gate_sums = after((down_sums, gate_sums), far_part)
    g_down = summed(*down_sums)
    g_late = summed(*after(late_sums, far_part))
    g_in = jnp.stack([summed(*gate_sums), g_late[:, :units]])
    g_out = own_order(g_late[:, units:], m, 0)
    lines = g_norm.shape[0] // LANES
    ways = lax.axis_size("mp") * lax.axis_size("tensor")
    state_norm = sums[2 * lines + 1, 0] / (ways * lax.axis_size("dp") * (2 * count // BLOCK))
    return (
        output,
        d_tokens,
        sums[:lines].reshape(-1),
        g_proj,
        g_beta.T,
        d_taps.reshape(conv_weight.shape),
        sums[2 * lines],
        g_out,
        sums[lines:2 * lines].reshape(-1),
        g_in,
        g_down,
        state_norm,
    )


def solution(mesh):
    placed = (
        P(("dp", "mp", "tensor"), None),
        P(),
        P(None, "mp", "tensor"),
        P("mp", "tensor"),
        P(None, None, "tensor", "mp", None),
        P(),
        P("tensor", "mp"),
        P(),
        P(None, "mp", "tensor"),
        P("tensor", "mp"),
        P(("dp", "mp", "tensor"), None),
        P("dp", None),
        P("dp"),
    )
    return jax.shard_map(
        shards,
        mesh=mesh,
        in_specs=placed,
        out_specs=(
            P(("dp", "mp", "tensor"), None),
            P(("dp", "mp", "tensor"), None),
            P(),
            P(None, "mp", "tensor"),
            P("mp", "tensor"),
            P(None, None, "tensor", "mp", None),
            P(),
            P("tensor", "mp"),
            P(),
            P(None, "mp", "tensor"),
            P("tensor", "mp"),
            P(),
        ),
        check_vma=False,
    )
```

```python
import jax
import jax.numpy as jnp
from jax import lax
from jax.experimental import pallas as pl
from jax.experimental.pallas import tpu as pltpu
from jax.sharding import PartitionSpec as P

BLOCK = 64
PAIR = 2 * BLOCK
LANES = 128
f32 = jnp.float32
bf16 = jnp.bfloat16


def halves(a):
    hi = a.astype(bf16)
    return hi, (a - hi.astype(f32)).astype(bf16)


def product(a, b, dims):
    return lax.dot_general(a, b, (dims, ((), ())), preferred_element_type=f32)


def close_dot(a, b, dims=((1,), (0,))):
    a_hi, a_lo = a if isinstance(a, tuple) else halves(a)
    b_hi, b_lo = b if isinstance(b, tuple) else halves(b)
    return product(a_hi, b_hi, dims) + (product(a_hi, b_lo, dims) + product(a_lo, b_hi, dims))


def low_dot(a, b, dims=((1,), (0,))):
    return product(a.astype(bf16), b.astype(bf16), dims)


NN = ((1,), (0,))
NT = ((1,), (1,))
TN = ((0,), (0,))


def doc_start(places, starts_ref):
    found = jnp.zeros_like(places)
    for j in range(1, starts_ref.shape[0]):
        begin = starts_ref[j]
        found = jnp.where(places >= begin, begin, found)
    return found


def place_rows(base, rows, width=LANES):
    return base + lax.broadcasted_iota(jnp.int32, (rows, width), 0)


def pair_masks(base, begins):
    rows = lax.broadcasted_iota(jnp.int32, (PAIR, PAIR), 0)
    cols = lax.broadcasted_iota(jnp.int32, (PAIR, PAIR), 1)
    heads = (rows // BLOCK) * BLOCK
    lower = jnp.maximum(begins - base, heads)
    upto = (cols >= lower) & (cols <= rows)
    strict = (cols >= lower) & (cols < rows)
    keep = begins < base + heads
    return upto, strict, keep, (rows == cols).astype(f32)


HALO = 16


def place_of(chunk, info_ref):
    return chunk ^ info_ref[1]


def in_order(step, count, info_ref, refs, target_ref, first):
    local = place_of(step * count, info_ref)
    near = local < pl.num_programs(0) * count // 2
    for n in range(count):
        inside = (local ^ n) % count

        @pl.when(near)
        def _():
            target_ref[first + n * PAIR:first + (n + 1) * PAIR, :] = refs[0][
                pl.ds(pl.multiple_of(inside * PAIR, PAIR), PAIR), :]

        @pl.when(jnp.logical_not(near))
        def _():
            target_ref[first + n * PAIR:first + (n + 1) * PAIR, :] = refs[1][
                pl.ds(pl.multiple_of(inside * PAIR, PAIR), PAIR), :]


def out_of_order(step, count, info_ref, value, target_ref, width):
    local = place_of(step * count, info_ref)
    for n in range(count):
        inside = pl.multiple_of(((local ^ n) % count) * PAIR, PAIR)
        target_ref[pl.ds(inside, PAIR), width] = value[n * PAIR:(n + 1) * PAIR]


def column(row):
    eye = lax.broadcasted_iota(jnp.int32, (PAIR, PAIR), 0) == lax.broadcasted_iota(jnp.int32, (PAIR, PAIR), 1)
    return jnp.sum(jnp.where(eye, row, 0.0), axis=1, keepdims=True)


def columns(step, count, info_ref, ref):
    return jnp.concatenate(
        [column(ref[pl.ds(place_of(step * count + n, info_ref), 1), :]) for n in range(count)], axis=0)


def forward_body(starts_ref, info_ref, near_ref, far_ref, before_near_ref, before_far_ref, logit_ref, taps_ref,
                 gain_ref, mixed_ref, norm_ref, conv_ref, wu_ref, t_ref, a_ref, c_ref, m_ref, s_ref, o_ref,
                 state_ref, square_ref, x_ref):
    step = pl.program_id(0)
    rows = near_ref.shape[0]
    base = step * rows
    count = rows // PAIR
    half_chunks = pl.num_programs(0) * count // 2
    before = place_of(jnp.maximum(step * count - 1, 0), info_ref)

    @pl.when(before < half_chunks)
    def _():
        x_ref[:HALO, :] = before_near_ref[...]

    @pl.when(before >= half_chunks)
    def _():
        x_ref[:HALO, :] = before_far_ref[...]

    in_order(step, count, info_ref, (near_ref, far_ref), x_ref, HALO)

    @pl.when(step == 0)
    def _():
        state_ref[...] = jnp.zeros_like(state_ref)

    places = place_rows(base, rows)
    begins = doc_start(places, starts_ref)
    since = places - begins
    valid = (places < info_ref[0]).astype(f32)
    parts = []
    for p in range(3):
        tall = x_ref[:, p * LANES:(p + 1) * LANES].astype(f32)
        now = tall[HALO:]
        summed = now * taps_ref[p, 3:4, :]
        for j in range(1, 4):
            moved = pltpu.roll(tall, j, 0)[HALO:]
            summed = summed + jnp.where(since >= j, moved, 0.0) * taps_ref[p, 3 - j:4 - j, :]
        conv_ref[p] = summed
        act = summed * jax.nn.sigmoid(summed)
        if p < 2:
            act = act * lax.rsqrt(jnp.sum(act * act, axis=1, keepdims=True) + 1e-06)
        parts.append(act)
    beta = jax.nn.sigmoid(columns(step, count, info_ref, logit_ref)) * valid
    gates = x_ref[HALO:, 3 * LANES:].astype(f32)
    gates = gates * jax.nn.sigmoid(gates) * valid * gain_ref[...]
    pairs = rows // PAIR
    blocks = []
    for g in range(pairs):
        at = slice(g * PAIR, (g + 1) * PAIR)
        start = base + g * PAIR
        q, k, v, b = parts[0][at], parts[1][at], parts[2][at], beta[at]
        upto, strict, keep, eye = pair_masks(start, begins[at])
        kb = b * k
        k_two = halves(k)
        neg = jnp.where(strict, -close_dot(kb, k_two, NT), 0.0)
        inverse = eye + neg
        power = neg
        for _ in range(BLOCK.bit_length() - 2):
            power_two = halves(power)
            power = close_dot(power_two, power_two)
            inverse = inverse + close_dot(inverse, power)
        wu = close_dot(inverse, jnp.concatenate([jnp.where(keep, kb, 0.0), b * v], axis=1))
        wu_two = halves(wu)
        scores = jnp.where(upto, product(q.astype(bf16), k_two[0], NT), 0.0).astype(bf16)
        cd = product(scores, wu_two[0], NN)
        c = jnp.where(keep, q, 0.0) - cd[:, :LANES]
        wu_ref[at] = wu
        t_ref[at] = inverse.astype(bf16)
        a_ref[at] = scores
        c = c.astype(bf16)
        c_ref[at] = c
        for h in range(2):
            inner = slice(h * BLOCK, (h + 1) * BLOCK)
            first = start + h * BLOCK
            final = doc_start(first + BLOCK - 1, starts_ref)
            tail = place_rows(first, BLOCK) >= final
            k_last = jnp.where(tail, k[inner], 0.0)
            mb = close_dot(k_last, (wu_two[0][inner], wu_two[1][inner]), TN)
            kept = jnp.where(final < first, 1.0, 0.0)
            m = kept * eye - mb[:, :LANES]
            m_ref[g * 2 + h] = m
            blocks.append((halves(m), mb[:, LANES:], c[inner], cd[inner, LANES:]))
    state = state_ref[...]
    results = []
    for n, (m_two, addend, c, d) in enumerate(blocks):
        s_two = halves(state)
        s_ref[n] = s_two[0]
        results.append(product(c, s_two[0], NN) + d)
        state = close_dot(m_two, s_two) + addend
        square_ref[pl.ds(step * len(blocks) + n, 1), :] = jnp.sum(state * state, axis=0, keepdims=True)
    state_ref[...] = state
    result = jnp.concatenate(results, axis=0)
    o_ref[...] = result
    unit = result * lax.rsqrt(jnp.mean(result * result, axis=1, keepdims=True) + 1e-05)
    out_of_order(step, count, info_ref, (unit * gates).astype(bf16), mixed_ref, slice(None))

    @pl.when(step == pl.num_programs(0) - 1)
    def _():
        sizes = jnp.sqrt(jnp.sum(square_ref[...], axis=1, keepdims=True) + 1e-12)
        norm_ref[...] = jnp.broadcast_to(jnp.sum(sizes, axis=0, keepdims=True), norm_ref.shape)


def backward_body(starts_ref, info_ref, near_ref, far_ref, logit_ref, taps_ref, gain_ref, grad_near_ref,
                  grad_far_ref, conv_ref, wu_ref, t_ref, a_ref, c_ref, m_ref, s_ref, o_ref,
                  dx_ref, dlogit_ref, dtaps_ref, dgain_ref, dstate_ref, after_ref, x_ref, grad_ref):
    step = pl.num_programs(0) - 1 - pl.program_id(0)
    rows = near_ref.shape[0]
    base = step * rows
    count = rows // PAIR
    in_order(step, count, info_ref, (near_ref, far_ref), x_ref, 0)
    in_order(step, count, info_ref, (grad_near_ref, grad_far_ref), grad_ref, 0)

    @pl.when(pl.program_id(0) == 0)
    def _():
        dstate_ref[...] = jnp.zeros_like(dstate_ref)
        after_ref[...] = jnp.zeros_like(after_ref)
        dtaps_ref[...] = jnp.zeros_like(dtaps_ref)
        dgain_ref[...] = jnp.zeros_like(dgain_ref)

    lead = after_ref.shape[1]
    places_tall = place_rows(base, rows + lead)
    begins_tall = doc_start(places_tall, starts_ref)
    since_tall = places_tall - begins_tall
    places, begins = places_tall[:rows], begins_tall[:rows]
    valid = (places < info_ref[0]).astype(f32)
    gain = gain_ref[...]
    gate = x_ref[:, 3 * LANES:].astype(f32)
    gate_sig = jax.nn.sigmoid(gate)
    gate_act = gate * gate_sig
    o = o_ref[...]
    r = lax.rsqrt(jnp.mean(o * o, axis=1, keepdims=True) + 1e-05)
    unit = o * r
    grad = grad_ref[...].astype(f32) * valid
    gu = grad * unit
    dgain_ref[0:1, :] += jnp.sum(gu * gate_act, axis=0, keepdims=True)
    dgate = (gu * gain * (gate_sig * (1.0 + gate * (1.0 - gate_sig)))).astype(bf16)
    out_of_order(step, count, info_ref, dgate, dx_ref, slice(3 * LANES, 4 * LANES))
    dunit = grad * gain * gate_act
    d_o = r * (dunit - unit * jnp.mean(dunit * unit, axis=1, keepdims=True))
    convs, sigs, acts, scales, units = [], [], [], [], []
    for p in range(3):
        conv = conv_ref[p]
        sig = jax.nn.sigmoid(conv)
        act = conv * sig
        convs.append(conv)
        sigs.append(sig)
        if p < 2:
            scale = lax.rsqrt(jnp.sum(act * act, axis=1, keepdims=True) + 1e-06)
            scales.append(scale)
            units.append(act * scale)
        else:
            units.append(act)
    logit_sig = jax.nn.sigmoid(columns(step, count, info_ref, logit_ref))
    beta = logit_sig * valid
    pairs = rows // PAIR
    do_low = d_o.astype(bf16)
    pieces = [None] * (2 * pairs)
    for n in range(2 * pairs):
        inner = slice(n * BLOCK, (n + 1) * BLOCK)
        pieces[n] = product(c_ref[inner, :], do_low[inner], TN)
    dstate = dstate_ref[...]
    dstates = [None] * (2 * pairs)
    for n in reversed(range(2 * pairs)):
        d_two = halves(dstate)
        dstates[n] = d_two[0]
        dstate = close_dot(m_ref[n], d_two, TN) + pieces[n]
    dstate_ref[...] = dstate
    grads = [[], [], []]
    dbetas = []
    for g in range(pairs):
        at = slice(g * PAIR, (g + 1) * PAIR)
        start = base + g * PAIR
        q, k, v, b = units[0][at], units[1][at], units[2][at], beta[at]
        upto, strict, keep, eye = pair_masks(start, begins[at])
        wu = wu_ref[at, :]
        wu_low = wu.astype(bf16)
        k_low = k.astype(bf16)
        do_pair = do_low[at]
        p_rows, dp_rows, dq_rows, dk_rows, dw_rows = [], [], [], [], []
        later = product(a_ref[at, :], do_pair, TN)
        for h in range(2):
            n = g * 2 + h
            inner = slice(h * BLOCK, (h + 1) * BLOCK)
            first = start + h * BLOCK
            final = doc_start(first + BLOCK - 1, starts_ref)
            tail = place_rows(first, BLOCK) >= final
            s_low = s_ref[n]
            ds_low = dstates[n]
            p = (wu[inner, LANES:] - product(wu_low[inner, :LANES], s_low, NN)).astype(bf16)
            k_last = jnp.where(tail, k[inner], 0.0)
            dp = later[inner] + low_dot(k_last, ds_low)
            p_rows.append(p)
            dp_rows.append(dp)
            dq_rows.append(product(do_pair[inner], s_low, NT))
            dk_rows.append(jnp.where(tail, product(p, ds_low, NT), 0.0))
            dw_rows.append(-low_dot(dp, s_low, NT))
        dp = jnp.concatenate(dp_rows, axis=0)
        da = jnp.where(upto, product(do_pair, jnp.concatenate(p_rows, axis=0), NT), 0.0).astype(bf16)
        dq = jnp.where(keep, jnp.concatenate(dq_rows, axis=0), 0.0) + product(da, k_low, NN)
        dk = jnp.concatenate(dk_rows, axis=0) + low_dot(da, q, TN)
        dwu = jnp.concatenate([jnp.concatenate(dw_rows, axis=0), dp], axis=1)
        dbkv = low_dot(t_ref[at, :], dwu, TN)
        dl = jnp.where(strict, -low_dot(dbkv, wu_low, NT), 0.0).astype(bf16)
        dkb = product(dl, k_low, NN) + jnp.where(keep, dbkv[:, :LANES], 0.0)
        dbv = dbkv[:, LANES:]
        dk = dk + b * dkb + low_dot(dl, b * k, TN)
        grads[0].append(dq)
        grads[1].append(dk)
        grads[2].append(b * dbv)
        dbetas.append(jnp.sum(k * dkb + v * dbv, axis=1, keepdims=True))
    dbeta = jnp.concatenate(dbetas, axis=0)
    dlogit = dbeta * (beta * (1.0 - logit_sig))
    eye = lax.broadcasted_iota(jnp.int32, (PAIR, PAIR), 0) == lax.broadcasted_iota(jnp.int32, (PAIR, PAIR), 1)
    for n in range(count):
        row = jnp.sum(jnp.where(eye, dlogit[n * PAIR:(n + 1) * PAIR], 0.0), axis=0, keepdims=True)
        dlogit_ref[pl.ds(place_of(step * count + n, info_ref), 1), :] = row
    for p in range(3):
        dact = jnp.concatenate(grads[p], axis=0)
        if p < 2:
            dact = scales[p] * (dact - units[p] * jnp.sum(dact * units[p], axis=1, keepdims=True))
        dconv = dact * (sigs[p] * (1.0 + convs[p] * (1.0 - sigs[p])))
        tall = jnp.concatenate([dconv, after_ref[p]], axis=0)
        after_ref[p] = dconv[:lead]
        x = x_ref[:, p * LANES:(p + 1) * LANES].astype(f32)
        dx = dconv * taps_ref[p, 3:4, :]
        dtaps_ref[p, 3:4, :] += jnp.sum(dconv * x, axis=0, keepdims=True)
        for j in range(1, 4):
            moved = pltpu.roll(jnp.where(since_tall >= j, tall, 0.0), rows + lead - j, 0)[:rows]
            dx = dx + moved * taps_ref[p, 3 - j:4 - j, :]
            dtaps_ref[p, 3 - j:4 - j, :] += jnp.sum(moved * x, axis=0, keepdims=True)
        out_of_order(step, count, info_ref, dx.astype(bf16), dx_ref, slice(p * LANES, (p + 1) * LANES))


def half_specs(rows, width, steps, order):
    count = rows // PAIR

    def pair(i, info):
        return place_of(order(i) * count, info) // count

    return [
        pl.BlockSpec((rows, width), lambda i, _, info: (jnp.minimum(pair(i, info), steps // 2 - 1), 0)),
        pl.BlockSpec((rows, width), lambda i, _, info: (jnp.maximum(pair(i, info) - steps // 2, 0), 0)),
    ]


def whole_spec(shape):
    return pl.BlockSpec(shape, lambda i, *_: (0,) * len(shape))


def head_forward(near, far, logit, taps, gain, starts, info, rows=256):
    total = 2 * near.shape[0]
    steps = total // rows
    count = rows // PAIR
    per = rows // BLOCK
    chunks = total // PAIR
    flat = lambda width: pl.BlockSpec((rows, width), lambda i, *_: (i, 0))
    square = pl.BlockSpec((per, LANES, LANES), lambda i, *_: (i, 0, 0))
    fine = PAIR // HALO

    def before(i, info):
        return place_of(jnp.maximum(i * count - 1, 0), info)

    s = jax.ShapeDtypeStruct
    outs = pl.pallas_call(
        forward_body,
        grid_spec=pltpu.PrefetchScalarGridSpec(
            num_scalar_prefetch=2,
            grid=(steps,),
            in_specs=[
                *half_specs(rows, 4 * LANES, steps, lambda i: i),
                pl.BlockSpec((HALO, 4 * LANES), lambda i, _, info: (
                    jnp.minimum(before(i, info), chunks // 2 - 1) * fine + fine - 1, 0)),
                pl.BlockSpec((HALO, 4 * LANES), lambda i, _, info: (
                    jnp.maximum(before(i, info) - chunks // 2, 0) * fine + fine - 1, 0)),
                whole_spec(logit.shape),
                whole_spec(taps.shape),
                whole_spec(gain.shape),
            ],
            out_specs=[
                pl.BlockSpec((rows, LANES), lambda i, _, info: (place_of(i * count, info) // count, 0)),
                whole_spec((8, LANES)),
                pl.BlockSpec((3, rows, LANES), lambda i, *_: (0, i, 0)),
                flat(2 * LANES), flat(PAIR), flat(PAIR), flat(LANES),
                square, square, flat(LANES),
            ],
            scratch_shapes=[
                pltpu.VMEM((LANES, LANES), f32), pltpu.VMEM((total // BLOCK, LANES), f32),
                pltpu.VMEM((rows + HALO, 4 * LANES), bf16),
            ],
        ),
        out_shape=[
            s((total, LANES), bf16), s((8, LANES), f32), s((3, total, LANES), f32),
            s((total, 2 * LANES), f32), s((total, PAIR), bf16), s((total, PAIR), bf16), s((total, LANES), bf16),
            s((total // BLOCK, LANES, LANES), f32), s((total // BLOCK, LANES, LANES), bf16),
            s((total, LANES), f32),
        ],
        name="head_forward",
        cost_estimate=pl.CostEstimate(flops=total * 20_000_000, transcendentals=0, bytes_accessed=total * 10_000),
    )(starts, info, near, far, near, far, logit, taps, gain)
    return outs[0], outs[1][0, 0], tuple(outs[2:])


def head_backward(grad_near, grad_far, near, far, logit, taps, gain, starts, info, kept, rows=256):
    total = 2 * near.shape[0]
    steps = total // rows
    count = rows // PAIR
    per = rows // BLOCK
    back = lambda i: steps - 1 - i
    flat = lambda width: pl.BlockSpec((rows, width), lambda i, *_: (back(i), 0))
    square = pl.BlockSpec((per, LANES, LANES), lambda i, *_: (back(i), 0, 0))
    s = jax.ShapeDtypeStruct
    return pl.pallas_call(
        backward_body,
        grid_spec=pltpu.PrefetchScalarGridSpec(
            num_scalar_prefetch=2,
            grid=(steps,),
            in_specs=[
                *half_specs(rows, 4 * LANES, steps, back),
                whole_spec(logit.shape), whole_spec(taps.shape), whole_spec(gain.shape),
                *half_specs(rows, LANES, steps, back),
                pl.BlockSpec((3, rows, LANES), lambda i, *_: (0, back(i), 0)),
                flat(2 * LANES), flat(PAIR), flat(PAIR), flat(LANES), square, square, flat(LANES),
            ],
            out_specs=[
                pl.BlockSpec((rows, 4 * LANES), lambda i, _, info: (place_of(back(i) * count, info) // count, 0)),
                whole_spec(logit.shape), whole_spec(taps.shape), whole_spec((8, LANES)),
            ],
            scratch_shapes=[
                pltpu.VMEM((LANES, LANES), f32), pltpu.VMEM((3, 8, LANES), f32),
                pltpu.VMEM((rows, 4 * LANES), bf16), pltpu.VMEM((rows, LANES), bf16),
            ],
        ),
        out_shape=[s((total, 4 * LANES), bf16), s(logit.shape, f32), s(taps.shape, f32), s((8, LANES), f32)],
        name="head_backward",
        cost_estimate=pl.CostEstimate(flops=total * 12_000_000, transcendentals=0, bytes_accessed=total * 10_000),
    )(starts, info, near, far, logit, taps, gain, grad_near, grad_far, *kept)


def other(value, axis, bit):
    size = lax.axis_size(axis)
    return lax.ppermute(value, axis, [(i, i ^ bit) for i in range(size)])


def after(value, *done):
    return lax.optimization_barrier((value, *done))[0]


def own_order(value, index, axis, parts=4):
    size = value.shape[axis] // parts
    return jnp.concatenate(
        [lax.dynamic_slice_in_dim(value, (p ^ index) * size, size, axis) for p in range(parts)], axis
    )


def neighbour_order(value, axis, bit, parts=4):
    size = value.shape[axis] // parts
    return jnp.concatenate(
        [lax.slice_in_dim(value, (p ^ bit) * size, ((p ^ bit) + 1) * size, axis=axis) for p in range(parts)], axis
    )


def matmul(a, b, dims=((1,), (0,))):
    return lax.dot_general(a, b, (dims, ((), ())), preferred_element_type=f32)


def norm_rows(values, gain):
    scale = lax.rsqrt(jnp.mean(values * values, axis=-1, keepdims=True) + 1e-05)
    unit = values * scale
    return unit * gain, unit, scale


def norm_back(grad, unit, scale, gain):
    pulled = grad * gain
    inner = jnp.mean(pulled * unit, axis=-1, keepdims=True)
    return scale * (pulled - unit * inner), jnp.sum(grad * unit, axis=0)


def tensor_tree():
    return lax.axis_size("tensor") == 4


def inner_place():
    index = lax.axis_index("tensor")
    return (index == 1) | (index == 2)


def along_tensor(value, pairs):
    return lax.ppermute(value, "tensor", pairs)


def gather_tensor(value, tree=True, before=()):
    if not tree or not tensor_tree():
        return [value] + [other(value, "tensor", s) for s in range(1, lax.axis_size("tensor"))]
    two = after(other(value, "tensor", 2), *before)
    one = other(value, "tensor", 1)
    passed = along_tensor(two, [(2, 3), (1, 0)])
    middle = along_tensor(after(value, one), [(1, 2), (2, 1)])
    return [value, one, two, jnp.where(inner_place(), middle, passed)]


def with_core(mine, theirs=()):
    came = list(theirs) + [other(v, "mp", 1) for v in mine[len(theirs):]]
    return jnp.concatenate(mine + [neighbour_order(v, 1, 1) for v in came], axis=0)


def spread(values):
    return with_core(gather_tensor(values))


def partials(rows, body):
    return body(rows // 2, rows).astype(bf16), body(0, rows // 2)


def collect_pieces(parts, before=()):
    theirs, mine = parts
    ways = lax.axis_size("tensor")
    piece = mine.shape[0] // ways
    if not tensor_tree():
        joined = mine + neighbour_order(other(theirs, "mp", 1), 1, 1).astype(f32)
        sent = [joined[s * piece:(s + 1) * piece].astype(bf16) for s in range(1, ways)]
        return joined[:piece], [other(v, "tensor", s + 1) for s, v in enumerate(sent)], sent
    last = (ways - 1) * piece
    tail = mine[last:] + neighbour_order(other(theirs[last:], "mp", 1), 1, 1).astype(f32)
    rest = mine[:last] + neighbour_order(other(theirs[:last], "mp", 1), 1, 1).astype(f32)
    low = tail.astype(bf16)
    passed = along_tensor(low, [(3, 2), (0, 1)])
    middle = along_tensor(low, [(1, 2), (2, 1)])
    sent = [(rest[2 * piece:] + passed.astype(f32)).astype(bf16), rest[piece:2 * piece].astype(bf16)]
    sent = list(after(sent, middle, *before))
    return rest[:piece], [middle, other(sent[0], "tensor", 2), other(sent[1], "tensor", 1)], sent


def added(own, received):
    for v in received:
        own = own + v.astype(f32)
    return own


def over_dp_pieces(value):
    bit = 1
    low = value.astype(bf16)
    came = other(low, "dp", bit)
    while 2 * bit < lax.axis_size("dp"):
        bit *= 2
        low = (low.astype(f32) + came.astype(f32)).astype(bf16)
        came = other(low, "dp", bit)
    return low, came


def summed(low, came):
    return low.astype(f32) + came.astype(f32)


def over_all(value):
    for axis in ("mp", "tensor"):
        if lax.axis_size(axis) == 4:
            one, two, three = [other(value, axis, bit) for bit in (1, 2, 3)]
            value = (value + one) + (two + three)
        else:
            bit = 1
            while bit < lax.axis_size(axis):
                value = value + other(value, axis, bit)
                bit *= 2
    bit = 1
    while bit < lax.axis_size("dp"):
        value = value + other(value, "dp", bit)
        bit *= 2
    return value


def shards(
    tokens,
    norm_gain,
    w_proj,
    w_beta,
    conv_weight,
    out_gain,
    w_out,
    mlp_gain,
    w_in,
    w_down,
    cotangent,
    starts,
    lengths,
):
    assert lax.axis_size("mp") == 4 and starts.shape[0] == 1
    m = lax.axis_index("mp")
    core = m & 1
    place = m * lax.axis_size("tensor") + lax.axis_index("tensor")
    block = w_proj.shape[1]
    near_blocks = 2 * block

    pieces, _, wide = w_proj.shape
    head = wide // 4
    span = pieces * head
    pair = lambda values, i, j, axis: jnp.concatenate([values[i], values[j]], axis)
    proj_got = other(w_proj, "mp", 2)
    beta_mine = w_beta.T
    beta_got = other(beta_mine, "mp", 2)
    scaled = own_order(norm_rows(tokens.astype(f32), norm_gain)[0].astype(bf16), m, 1)
    normed = spread(scaled)
    inputs = own_order(after(tokens, normed), m, 1).astype(f32)
    gain_one = own_order(norm_gain, m, 0)
    gain_two = own_order(mlp_gain, m, 0)
    _, unit_one, scale_one = norm_rows(inputs, gain_one)

    def head_blocks(v):
        return [
            lax.dynamic_slice_in_dim(v, (j ^ m) * head, head, 2).transpose(1, 0, 2).reshape(block, span)
            for j in range(4)
        ]

    proj_mine, proj_far = head_blocks(w_proj), head_blocks(proj_got)
    proj_low = jnp.concatenate([pair(proj_mine, 0, 2, 1), other(pair(proj_mine, 1, 3, 1), "mp", 1)], axis=0)
    proj_high = jnp.concatenate([pair(proj_far, 0, 2, 1), other(pair(proj_far, 1, 3, 1), "mp", 1)], axis=0)
    beta_both = jnp.concatenate([beta_mine, after(beta_got, proj_got)], axis=1)
    beta_all = own_order(jnp.concatenate([beta_both, other(beta_both, "mp", 1)], axis=1), m, 0)
    beta_all = pair([beta_all[0:1], beta_all[2:3]], 0, 1, 0)
    full_beta = jnp.concatenate([beta_all[:, p * block:(p + 1) * block] for p in (0, 2, 1, 3)], axis=1)
    logits = matmul(full_beta, normed, ((1,), (1,))).astype(bf16)
    normed_low, normed_high = normed[:, :near_blocks], normed[:, near_blocks:]
    far_out = (matmul(normed_low, proj_low[:, span:]) + matmul(normed_high, proj_high[:, span:])).astype(bf16)
    count = far_out.shape[0]
    logit_rows = count // span
    far_sent = jnp.concatenate([far_out, jnp.pad(logits[1].reshape(logit_rows, span), ((0, HALO - logit_rows), (0, 0)))], 0)
    units = w_down.shape[0]
    half = LANES * ((units // LANES + 1) // 2)
    ours = lambda v, axis: lax.dynamic_slice_in_dim(v, core * (units - half), half, axis)
    theirs = lambda v, axis: lax.dynamic_slice_in_dim(v, (1 - core) * (units - half), half, axis)
    cot_own = own_order(cotangent, m, 1)
    early = after((theirs(w_down, 0), theirs(w_in, 2), cot_own), far_sent)
    down_core, in_core, cot_core = [other(v, "mp", 1) for v in early]
    full_proj = jnp.concatenate(after((proj_low, proj_high), far_sent), axis=0)
    far = after(other(far_sent, "mp", 2), down_core, in_core, cot_core, full_proj)
    near_low, near_high = after((normed_low, normed_high), far_sent)
    near = (matmul(near_low, proj_low[:, :span]) + matmul(near_high, proj_high[:, :span])).astype(bf16)
    chunk_rows = (-1, LANES)
    logit = jnp.concatenate(
        [logits[0].reshape(chunk_rows), far[count:count + logit_rows].reshape(chunk_rows)], axis=0
    ).astype(f32)

    live = (lax.broadcasted_iota(jnp.int32, (1, half), 1) >= core * (2 * half - units)).astype(f32)
    out_blocks = lambda v: [lax.dynamic_slice_in_dim(v, (j ^ m) * head, head, 0) for j in range(4)]
    rows_sent = after(jnp.concatenate([w_out, w_down], axis=0), far)
    rows_got = other(rows_sent, "mp", 2)
    cot_pieces = gather_tensor(after(cot_own, far), tree=False)

    taps = conv_weight.reshape(3, conv_weight.shape[1], head)
    info = jnp.stack([lengths[0], place]).astype(jnp.int32)
    head_args = (near, far, logit, taps, out_gain[None], starts[0], info)
    mixed, norm_total, kept = head_forward(*head_args)
    mixed = after(mixed, rows_got, *cot_pieces)
    mixed_far = other(mixed[count:], "mp", 2)
    out_mine, out_far = out_blocks(w_out), out_blocks(rows_got[: w_out.shape[0]])
    out_sent = jnp.concatenate([pair(out_mine, 1, 3, 0), pair(out_far, 1, 3, 0)], axis=1)
    out_core = other(after(out_sent, mixed), "mp", 1)
    full_out = jnp.concatenate(
        [pair(out_mine, 0, 2, 0), out_core[:, :block], pair(out_far, 0, 2, 0), out_core[:, block:]], axis=1
    )
    mixed_tok = jnp.concatenate([mixed[:count], mixed_far], axis=1)
    branch_parts = partials(count, lambda a, b: matmul(mixed_tok[a:b], full_out))
    gate_first = other(after(w_in[0, : block // 2], mixed_far), "mp", 2)
    gate_second = other(after(w_in[0, block // 2:], mixed_far), "mp", 2)
    branch_own, branch_got, branch_sent = collect_pieces(branch_parts, before=(gate_first,))
    branch = added(branch_own, branch_got)
    up_far = other(after(w_in[1], branch_sent), "mp", 2)

    middle = inputs + branch
    scaled_two, unit_two, scale_two = norm_rows(middle, gain_two)
    low_two = after(scaled_two.astype(bf16), gate_second)
    down_far = after(rows_got, low_two)[w_out.shape[0]:]
    down_across = other(theirs(down_far, 0), "mp", 1)
    cot_across = other(after(jnp.concatenate(cot_pieces[1:], axis=0), low_two), "mp", 1)
    piece = cot_own.shape[0]
    theirs_cot = [cot_core] + [cot_across[s * piece:(s + 1) * piece] for s in range(len(cot_pieces) - 1)]
    cot_all = with_core(cot_pieces, theirs_cot)
    full_down = jnp.concatenate([ours(w_down, 0), down_core, ours(down_far, 0), down_across], axis=1)
    d_hidden = matmul(cot_all, full_down, ((1,), (1,)))
    two_pieces = gather_tensor(low_two, before=(up_far,))
    normed_two = after(with_core(two_pieces), d_hidden)
    gate_far = jnp.concatenate([after(gate_first, low_two), after(gate_second, low_two)], axis=0)
    in_far = [gate_far, after(up_far, two_pieces[2])]
    full_in = [
        after(
            jnp.concatenate([ours(w_in[i], 1), in_core[i], ours(v, 1), other(theirs(v, 1), "mp", 1)], axis=0), d_hidden
        )
        for i, v in enumerate(in_far)
    ]

    gate = matmul(normed_two, full_in[0])
    up = matmul(normed_two, full_in[1])
    sigma = jax.nn.sigmoid(gate)
    activated = gate * sigma
    hidden = (activated * up * live).astype(bf16)
    d_hidden = d_hidden * live
    d_gate = (d_hidden * up * sigma * (1.0 + gate * (1.0 - sigma))).astype(bf16)
    d_up = (d_hidden * activated).astype(bf16)
    two_parts = partials(
        count,
        lambda a, b: matmul(d_gate[a:b], full_in[0], ((1,), (1,))) + matmul(d_up[a:b], full_in[1], ((1,), (1,))),
    )
    two_own, two_got, two_sent = collect_pieces(two_parts)
    hidden, d_gate, d_up = after((hidden, d_gate, d_up), two_sent)
    tn = ((0,), (0,))
    grad_dot = lambda a, b: matmul(a, b, tn)

    def joined_units(mine, theirs, axis):
        gap = units - half
        low = jnp.where(core == 0, mine, theirs)
        high = jnp.where(core == 0, theirs, mine)
        zero = jnp.zeros_like(lax.slice_in_dim(low, 0, gap, axis=axis))
        return jnp.concatenate([low, zero], axis) + jnp.concatenate([zero, high], axis)

    def units_joined(product, axis):
        cut = lambda v, p: lax.slice_in_dim(v, p * block, (p + 1) * block, axis=axis)
        two = lambda i, j: jnp.concatenate([cut(product, i), cut(product, j)], axis)
        joined = joined_units(two(0, 2), other(two(1, 3), "mp", 1), 1 - axis)
        return cut(joined, 0), cut(joined, 1)

    down_product = grad_dot(hidden, cot_all).astype(bf16)
    gate_product = grad_dot(normed_two, after(d_gate, down_product)).astype(bf16)
    down_held, down_sent = units_joined(down_product, 1)
    up_product = grad_dot(normed_two, after(d_up, gate_product, down_sent)).astype(bf16)
    gate_held, gate_sent = units_joined(gate_product, 0)
    up_held, up_sent = units_joined(up_product, 0)
    down_got = other(down_sent, "mp", 2)

    d_normed_two = added(after(two_own, down_sent), two_got)
    d_mid_norm, g_mlp = norm_back(d_normed_two, unit_two, scale_two, gain_two)
    d_middle = cot_own.astype(f32) + d_mid_norm
    d_mid_low = after(d_middle.astype(bf16), down_sent, gate_sent)
    d_mid_pieces = gather_tensor(d_mid_low)
    gate_got = other(after(gate_sent, d_mid_pieces[2]), "mp", 2)
    down_sums = over_dp_pieces(summed(down_held, after(down_got, d_mid_pieces[2])))
    feed_parts = partials(count, lambda a, b: matmul(hidden[a:b], full_down))
    feed_theirs = other(after(feed_parts[0], d_mid_pieces[2]), "mp", 1)
    feed_joined = feed_parts[1] + neighbour_order(feed_theirs, 1, 1).astype(f32)
    piece_rows = feed_joined.shape[0] // lax.axis_size("tensor")
    feed_sent = [
        feed_joined[p * piece_rows:(p + 1) * piece_rows].astype(bf16) for p in range(1, lax.axis_size("tensor"))
    ]
    d_mid_all = after(with_core(d_mid_pieces), down_got, feed_sent)
    d_mixed = matmul(d_mid_all, full_out, ((1,), (1,))).astype(bf16)
    d_far = other(d_mixed[:, head:], "mp", 2)
    gate_sums = over_dp_pieces(summed(gate_held, after(gate_got, down_sums[1], d_far)))
    feed_got = [other(after(v, d_mid_all), "tensor", p + 1) for p, v in enumerate(feed_sent)]
    feed_own = feed_joined[:piece_rows]
    output = own_order((middle + added(feed_own, feed_got)).astype(bf16), m, 1)

    out_grad = grad_dot(mixed_tok, d_mid_all)
    out_sent = out_grad[:, near_blocks:].astype(bf16)
    up_got = other(after(up_sent, d_far), "mp", 2)
    d_near = after(d_mixed[:, :head], gate_got, down_sums[1])
    d_heads, d_logit, d_taps, g_head_gain = head_backward(d_near, d_far, *head_args, kept)
    d_heads, d_logit = after((d_heads, d_logit), up_got, gate_sums[1], *feed_got)
    d_own = d_heads[:count]
    d_logit = d_logit.astype(bf16)
    half_chunks = d_logit.shape[0] // 2
    d_sent = jnp.concatenate(
        [
            d_heads[count:],
            jnp.pad(d_logit[half_chunks:].reshape(logit_rows, span), ((0, HALO - logit_rows), (0, 0))),
        ],
        axis=0,
    )
    d_got = other(d_sent, "mp", 2)
    d_proj = jnp.concatenate([d_own, d_got[:count]], axis=1)
    d_logits = jnp.concatenate(
        [d_logit[:half_chunks].reshape(1, count), d_got[count:count + logit_rows].reshape(1, count)], axis=0
    )
    up_sums = over_dp_pieces(summed(up_held, after(up_got, d_sent)))
    out_got = other(after(out_sent, d_sent), "mp", 2)
    normed_parts = partials(
        count,
        lambda a, b: matmul(d_proj[a:b], full_proj, ((1,), (1,))) + matmul(d_logits[:, a:b], full_beta, tn),
    )
    normed_own, normed_got, normed_sent = collect_pieces(normed_parts)
    out_got = after(out_got, normed_parts)
    out_two = (out_grad[:, :near_blocks] + neighbour_order(out_got, 0, 1, 2).astype(f32)).astype(bf16)
    out_theirs = other(out_two[:, block:], "mp", 1)
    out_mine = out_two[:, :block]
    out_rows = jnp.concatenate([out_mine[:head], out_theirs[:head], out_mine[head:], out_theirs[head:]], axis=0)
    out_sums = over_dp_pieces(out_rows)
    own_grad = grad_dot(normed, after(d_own, d_sent))
    far_grad = grad_dot(normed, after(d_got, normed_parts)[:count])
    own_back = other(own_grad[near_blocks:].astype(bf16), "mp", 2)
    far_back = other(after(far_grad[near_blocks:].astype(bf16), normed_sent), "mp", 2)

    def proj_part(held, back):
        two = (held[:near_blocks] + back.astype(f32)).astype(bf16)
        return jnp.concatenate([two[:block], other(two[block:], "mp", 1)], axis=1)

    far_part = after(proj_part(far_grad, after(own_back, normed_sent)), up_sums[1], out_sums[1])
    far_sums = over_dp_pieces(far_part)
    down_sums, gate_sums = after((down_sums, gate_sums), far_part)
    g_down = summed(*down_sums)
    up_sums, out_sums = after((up_sums, out_sums), far_part)
    g_in = jnp.stack([summed(*gate_sums), summed(*up_sums)])
    g_out = own_order(summed(*out_sums), m, 0)
    normed_again, partial_rows = after((normed, normed_parts), far_part)
    g_norm = (
        jnp.sum(normed_again[: count // 2].astype(f32) * partial_rows[1], axis=0)
        + jnp.sum(normed_again[count // 2:].astype(f32) * partial_rows[0].astype(f32), axis=0)
    ) / gain_one
    row = lambda v: v.reshape(-1, LANES)
    rows_all = [own_order(row(g_norm), m, 0), own_order(row(g_mlp), m, 0), g_head_gain[:1]]
    rows_all.append(jnp.full((1, LANES), norm_total))
    rows_here = jnp.concatenate(rows_all, axis=0)
    beta_here = matmul(after(d_logits, far_part), normed)
    d_normed = added(after(normed_own, g_down, g_in, g_out, rows_here, beta_here), normed_got)
    own_part = proj_part(own_grad, after(far_back, normed_got))
    own_sums = over_dp_pieces(own_part)
    part_far, part_own = summed(*far_sums), summed(*own_sums)
    g_heads = [part_own[:, :span], part_own[:, span:], part_far[:, :span], part_far[:, span:]]
    g_proj = own_order(
        jnp.concatenate([v.reshape(block, pieces, head).transpose(1, 0, 2) for v in g_heads], axis=2), m, 2
    )
    beta_part = after(beta_here, far_sums[1], own_part)
    beta_back = neighbour_order(neighbour_order(other(beta_part, "mp", 2), 0, 1, 2), 1, 1, 2)
    beta_two = beta_part + beta_back
    beta_theirs = other(beta_two[:, block:near_blocks], "mp", 1)
    g_beta = own_order(
        jnp.concatenate([beta_two[:1, :block], beta_theirs[:1], beta_two[1:, :block], beta_theirs[1:]], axis=0), m, 0
    )
    small = jnp.concatenate([g_beta.reshape(-1, LANES), d_taps.reshape(-1, LANES)], axis=0)
    bit = 1
    while bit < lax.axis_size("dp"):
        small = small + other(small, "dp", bit)
        bit *= 2
    cut = g_beta.size // LANES
    g_beta = small[:cut].reshape(g_beta.shape)
    d_taps = small[cut:]
    sums = over_all(after(rows_here, far_sums[1], own_part))
    d_in_norm, _ = norm_back(d_normed, unit_one, scale_one, gain_one)
    d_tokens = own_order(d_middle + d_in_norm, m, 1)
    lines = g_norm.shape[0] // LANES
    ways = lax.axis_size("mp") * lax.axis_size("tensor")
    state_norm = sums[2 * lines + 1, 0] / (ways * lax.axis_size("dp") * (2 * count // BLOCK))
    return (
        output,
        d_tokens,
        sums[:lines].reshape(-1),
        g_proj,
        g_beta.T,
        d_taps.reshape(conv_weight.shape),
        sums[2 * lines],
        g_out,
        sums[lines:2 * lines].reshape(-1),
        g_in,
        g_down,
        state_norm,
    )


def solution(mesh):
    placed = (
        P(("dp", "mp", "tensor"), None),
        P(),
        P(None, "mp", "tensor"),
        P("mp", "tensor"),
        P(None, None, "tensor", "mp", None),
        P(),
        P("tensor", "mp"),
        P(),
        P(None, "mp", "tensor"),
        P("tensor", "mp"),
        P(("dp", "mp", "tensor"), None),
        P("dp", None),
        P("dp"),
    )
    return jax.shard_map(
        shards,
        mesh=mesh,
        in_specs=placed,
        out_specs=(
            P(("dp", "mp", "tensor"), None),
            P(("dp", "mp", "tensor"), None),
            P(),
            P(None, "mp", "tensor"),
            P("mp", "tensor"),
            P(None, None, "tensor", "mp", None),
            P(),
            P("tensor", "mp"),
            P(),
            P(None, "mp", "tensor"),
            P("tensor", "mp"),
            P(),
        ),
        check_vma=False,
    )
```

```python
import jax
import jax.numpy as jnp
from jax import lax
from jax.experimental import pallas as pl
from jax.experimental.pallas import tpu as pltpu
from jax.sharding import PartitionSpec as P

BLOCK = 64
PAIR = 2 * BLOCK
LANES = 128
f32 = jnp.float32
bf16 = jnp.bfloat16


def halves(a):
    hi = a.astype(bf16)
    return hi, (a - hi.astype(f32)).astype(bf16)


def product(a, b, dims):
    return lax.dot_general(a, b, (dims, ((), ())), preferred_element_type=f32)


def close_dot(a, b, dims=((1,), (0,))):
    a_hi, a_lo = a if isinstance(a, tuple) else halves(a)
    b_hi, b_lo = b if isinstance(b, tuple) else halves(b)
    return product(a_hi, b_hi, dims) + (product(a_hi, b_lo, dims) + product(a_lo, b_hi, dims))


def low_dot(a, b, dims=((1,), (0,))):
    return product(a.astype(bf16), b.astype(bf16), dims)


NN = ((1,), (0,))
NT = ((1,), (1,))
TN = ((0,), (0,))


def doc_start(places, starts_ref):
    found = jnp.zeros_like(places)
    for j in range(1, starts_ref.shape[0]):
        begin = starts_ref[j]
        found = jnp.where(places >= begin, begin, found)
    return found


def place_rows(base, rows, width=LANES):
    return base + lax.broadcasted_iota(jnp.int32, (rows, width), 0)


def pair_masks(base, begins):
    rows = lax.broadcasted_iota(jnp.int32, (PAIR, PAIR), 0)
    cols = lax.broadcasted_iota(jnp.int32, (PAIR, PAIR), 1)
    heads = (rows // BLOCK) * BLOCK
    lower = jnp.maximum(begins - base, heads)
    upto = (cols >= lower) & (cols <= rows)
    strict = (cols >= lower) & (cols < rows)
    keep = begins < base + heads
    return upto, strict, keep, (rows == cols).astype(f32)


HALO = 16


def place_of(chunk, info_ref):
    return chunk ^ info_ref[1]


def in_order(step, count, info_ref, refs, target_ref, first):
    local = place_of(step * count, info_ref)
    near = local < pl.num_programs(0) * count // 2
    for n in range(count):
        inside = (local ^ n) % count

        @pl.when(near)
        def _():
            target_ref[first + n * PAIR:first + (n + 1) * PAIR, :] = refs[0][
                pl.ds(pl.multiple_of(inside * PAIR, PAIR), PAIR), :]

        @pl.when(jnp.logical_not(near))
        def _():
            target_ref[first + n * PAIR:first + (n + 1) * PAIR, :] = refs[1][
                pl.ds(pl.multiple_of(inside * PAIR, PAIR), PAIR), :]


def out_of_order(step, count, info_ref, value, target_ref, width):
    local = place_of(step * count, info_ref)
    for n in range(count):
        inside = pl.multiple_of(((local ^ n) % count) * PAIR, PAIR)
        target_ref[pl.ds(inside, PAIR), width] = value[n * PAIR:(n + 1) * PAIR]


def column(row):
    eye = lax.broadcasted_iota(jnp.int32, (PAIR, PAIR), 0) == lax.broadcasted_iota(jnp.int32, (PAIR, PAIR), 1)
    return jnp.sum(jnp.where(eye, row, 0.0), axis=1, keepdims=True)


def columns(step, count, info_ref, ref):
    return jnp.concatenate(
        [column(ref[pl.ds(place_of(step * count + n, info_ref), 1), :]) for n in range(count)], axis=0)


def forward_body(starts_ref, info_ref, near_ref, far_ref, before_near_ref, before_far_ref, logit_ref, taps_ref,
                 gain_ref, mixed_ref, norm_ref, conv_ref, wu_ref, t_ref, a_ref, c_ref, m_ref, s_ref, o_ref,
                 state_ref, square_ref, x_ref):
    step = pl.program_id(0)
    rows = near_ref.shape[0]
    base = step * rows
    count = rows // PAIR
    half_chunks = pl.num_programs(0) * count // 2
    before = place_of(jnp.maximum(step * count - 1, 0), info_ref)

    @pl.when(before < half_chunks)
    def _():
        x_ref[:HALO, :] = before_near_ref[...]

    @pl.when(before >= half_chunks)
    def _():
        x_ref[:HALO, :] = before_far_ref[...]

    in_order(step, count, info_ref, (near_ref, far_ref), x_ref, HALO)

    @pl.when(step == 0)
    def _():
        state_ref[...] = jnp.zeros_like(state_ref)

    places = place_rows(base, rows)
    begins = doc_start(places, starts_ref)
    since = places - begins
    valid = (places < info_ref[0]).astype(f32)
    parts = []
    for p in range(3):
        tall = x_ref[:, p * LANES:(p + 1) * LANES].astype(f32)
        now = tall[HALO:]
        summed = now * taps_ref[p, 3:4, :]
        for j in range(1, 4):
            moved = pltpu.roll(tall, j, 0)[HALO:]
            summed = summed + jnp.where(since >= j, moved, 0.0) * taps_ref[p, 3 - j:4 - j, :]
        conv_ref[p] = summed
        act = summed * jax.nn.sigmoid(summed)
        if p < 2:
            act = act * lax.rsqrt(jnp.sum(act * act, axis=1, keepdims=True) + 1e-06)
        parts.append(act)
    beta = jax.nn.sigmoid(columns(step, count, info_ref, logit_ref)) * valid
    gates = x_ref[HALO:, 3 * LANES:].astype(f32)
    gates = gates * jax.nn.sigmoid(gates) * valid * gain_ref[...]
    pairs = rows // PAIR
    blocks = []
    for g in range(pairs):
        at = slice(g * PAIR, (g + 1) * PAIR)
        start = base + g * PAIR
        q, k, v, b = parts[0][at], parts[1][at], parts[2][at], beta[at]
        upto, strict, keep, eye = pair_masks(start, begins[at])
        kb = b * k
        k_two = halves(k)
        neg = jnp.where(strict, -close_dot(kb, k_two, NT), 0.0)
        inverse = eye + neg
        power = neg
        for _ in range(BLOCK.bit_length() - 2):
            power_two = halves(power)
            power = close_dot(power_two, power_two)
            inverse = inverse + close_dot(inverse, power)
        wu = close_dot(inverse, jnp.concatenate([jnp.where(keep, kb, 0.0), b * v], axis=1))
        wu_two = halves(wu)
        scores = jnp.where(upto, product(q.astype(bf16), k_two[0], NT), 0.0).astype(bf16)
        cd = product(scores, wu_two[0], NN)
        c = jnp.where(keep, q, 0.0) - cd[:, :LANES]
        wu_ref[at] = wu
        t_ref[at] = inverse.astype(bf16)
        a_ref[at] = scores
        c = c.astype(bf16)
        c_ref[at] = c
        for h in range(2):
            inner = slice(h * BLOCK, (h + 1) * BLOCK)
            first = start + h * BLOCK
            final = doc_start(first + BLOCK - 1, starts_ref)
            tail = place_rows(first, BLOCK) >= final
            k_last = jnp.where(tail, k[inner], 0.0)
            mb = close_dot(k_last, (wu_two[0][inner], wu_two[1][inner]), TN)
            kept = jnp.where(final < first, 1.0, 0.0)
            m = kept * eye - mb[:, :LANES]
            m_ref[g * 2 + h] = m
            blocks.append((halves(m), mb[:, LANES:], c[inner], cd[inner, LANES:]))
    state = state_ref[...]
    results = []
    for n, (m_two, addend, c, d) in enumerate(blocks):
        s_two = halves(state)
        s_ref[n] = s_two[0]
        results.append(product(c, s_two[0], NN) + d)
        state = close_dot(m_two, s_two) + addend
        square_ref[pl.ds(step * len(blocks) + n, 1), :] = jnp.sum(state * state, axis=0, keepdims=True)
    state_ref[...] = state
    result = jnp.concatenate(results, axis=0)
    o_ref[...] = result
    unit = result * lax.rsqrt(jnp.mean(result * result, axis=1, keepdims=True) + 1e-05)
    out_of_order(step, count, info_ref, (unit * gates).astype(bf16), mixed_ref, slice(None))

    @pl.when(step == pl.num_programs(0) - 1)
    def _():
        sizes = jnp.sqrt(jnp.sum(square_ref[...], axis=1, keepdims=True) + 1e-12)
        norm_ref[...] = jnp.broadcast_to(jnp.sum(sizes, axis=0, keepdims=True), norm_ref.shape)


def backward_body(starts_ref, info_ref, near_ref, far_ref, logit_ref, taps_ref, gain_ref, grad_near_ref,
                  grad_far_ref, conv_ref, wu_ref, t_ref, a_ref, c_ref, m_ref, s_ref, o_ref,
                  dx_ref, dlogit_ref, dtaps_ref, dgain_ref, dstate_ref, after_ref, x_ref, grad_ref):
    step = pl.num_programs(0) - 1 - pl.program_id(0)
    rows = near_ref.shape[0]
    base = step * rows
    count = rows // PAIR
    in_order(step, count, info_ref, (near_ref, far_ref), x_ref, 0)
    in_order(step, count, info_ref, (grad_near_ref, grad_far_ref), grad_ref, 0)

    @pl.when(pl.program_id(0) == 0)
    def _():
        dstate_ref[...] = jnp.zeros_like(dstate_ref)
        after_ref[...] = jnp.zeros_like(after_ref)
        dtaps_ref[...] = jnp.zeros_like(dtaps_ref)
        dgain_ref[...] = jnp.zeros_like(dgain_ref)

    lead = after_ref.shape[1]
    places_tall = place_rows(base, rows + lead)
    begins_tall = doc_start(places_tall, starts_ref)
    since_tall = places_tall - begins_tall
    places, begins = places_tall[:rows], begins_tall[:rows]
    valid = (places < info_ref[0]).astype(f32)
    gain = gain_ref[...]
    gate = x_ref[:, 3 * LANES:].astype(f32)
    gate_sig = jax.nn.sigmoid(gate)
    gate_act = gate * gate_sig
    o = o_ref[...]
    r = lax.rsqrt(jnp.mean(o * o, axis=1, keepdims=True) + 1e-05)
    unit = o * r
    grad = grad_ref[...].astype(f32) * valid
    gu = grad * unit
    dgain_ref[0:1, :] += jnp.sum(gu * gate_act, axis=0, keepdims=True)
    dgate = (gu * gain * (gate_sig * (1.0 + gate * (1.0 - gate_sig)))).astype(bf16)
    out_of_order(step, count, info_ref, dgate, dx_ref, slice(3 * LANES, 4 * LANES))
    dunit = grad * gain * gate_act
    d_o = r * (dunit - unit * jnp.mean(dunit * unit, axis=1, keepdims=True))
    convs, sigs, acts, scales, units = [], [], [], [], []
    for p in range(3):
        conv = conv_ref[p]
        sig = jax.nn.sigmoid(conv)
        act = conv * sig
        convs.append(conv)
        sigs.append(sig)
        if p < 2:
            scale = lax.rsqrt(jnp.sum(act * act, axis=1, keepdims=True) + 1e-06)
            scales.append(scale)
            units.append(act * scale)
        else:
            units.append(act)
    logit_sig = jax.nn.sigmoid(columns(step, count, info_ref, logit_ref))
    beta = logit_sig * valid
    pairs = rows // PAIR
    do_low = d_o.astype(bf16)
    pieces = [None] * (2 * pairs)
    for n in range(2 * pairs):
        inner = slice(n * BLOCK, (n + 1) * BLOCK)
        pieces[n] = product(c_ref[inner, :], do_low[inner], TN)
    dstate = dstate_ref[...]
    dstates = [None] * (2 * pairs)
    for n in reversed(range(2 * pairs)):
        d_two = halves(dstate)
        dstates[n] = d_two[0]
        dstate = close_dot(m_ref[n], d_two, TN) + pieces[n]
    dstate_ref[...] = dstate
    grads = [[], [], []]
    dbetas = []
    for g in range(pairs):
        at = slice(g * PAIR, (g + 1) * PAIR)
        start = base + g * PAIR
        q, k, v, b = units[0][at], units[1][at], units[2][at], beta[at]
        upto, strict, keep, eye = pair_masks(start, begins[at])
        wu = wu_ref[at, :]
        wu_low = wu.astype(bf16)
        k_low = k.astype(bf16)
        do_pair = do_low[at]
        p_rows, dp_rows, dq_rows, dk_rows, dw_rows = [], [], [], [], []
        later = product(a_ref[at, :], do_pair, TN)
        for h in range(2):
            n = g * 2 + h
            inner = slice(h * BLOCK, (h + 1) * BLOCK)
            first = start + h * BLOCK
            final = doc_start(first + BLOCK - 1, starts_ref)
            tail = place_rows(first, BLOCK) >= final
            s_low = s_ref[n]
            ds_low = dstates[n]
            p = (wu[inner, LANES:] - product(wu_low[inner, :LANES], s_low, NN)).astype(bf16)
            k_last = jnp.where(tail, k[inner], 0.0)
            dp = later[inner] + low_dot(k_last, ds_low)
            p_rows.append(p)
            dp_rows.append(dp)
            dq_rows.append(product(do_pair[inner], s_low, NT))
            dk_rows.append(jnp.where(tail, product(p, ds_low, NT), 0.0))
            dw_rows.append(-low_dot(dp, s_low, NT))
        dp = jnp.concatenate(dp_rows, axis=0)
        da = jnp.where(upto, product(do_pair, jnp.concatenate(p_rows, axis=0), NT), 0.0).astype(bf16)
        dq = jnp.where(keep, jnp.concatenate(dq_rows, axis=0), 0.0) + product(da, k_low, NN)
        dk = jnp.concatenate(dk_rows, axis=0) + low_dot(da, q, TN)
        dwu = jnp.concatenate([jnp.concatenate(dw_rows, axis=0), dp], axis=1)
        dbkv = low_dot(t_ref[at, :], dwu, TN)
        dl = jnp.where(strict, -low_dot(dbkv, wu_low, NT), 0.0).astype(bf16)
        dkb = product(dl, k_low, NN) + jnp.where(keep, dbkv[:, :LANES], 0.0)
        dbv = dbkv[:, LANES:]
        dk = dk + b * dkb + low_dot(dl, b * k, TN)
        grads[0].append(dq)
        grads[1].append(dk)
        grads[2].append(b * dbv)
        dbetas.append(jnp.sum(k * dkb + v * dbv, axis=1, keepdims=True))
    dbeta = jnp.concatenate(dbetas, axis=0)
    dlogit = dbeta * (beta * (1.0 - logit_sig))
    eye = lax.broadcasted_iota(jnp.int32, (PAIR, PAIR), 0) == lax.broadcasted_iota(jnp.int32, (PAIR, PAIR), 1)
    for n in range(count):
        row = jnp.sum(jnp.where(eye, dlogit[n * PAIR:(n + 1) * PAIR], 0.0), axis=0, keepdims=True)
        dlogit_ref[pl.ds(place_of(step * count + n, info_ref), 1), :] = row
    for p in range(3):
        dact = jnp.concatenate(grads[p], axis=0)
        if p < 2:
            dact = scales[p] * (dact - units[p] * jnp.sum(dact * units[p], axis=1, keepdims=True))
        dconv = dact * (sigs[p] * (1.0 + convs[p] * (1.0 - sigs[p])))
        tall = jnp.concatenate([dconv, after_ref[p]], axis=0)
        after_ref[p] = dconv[:lead]
        x = x_ref[:, p * LANES:(p + 1) * LANES].astype(f32)
        dx = dconv * taps_ref[p, 3:4, :]
        dtaps_ref[p, 3:4, :] += jnp.sum(dconv * x, axis=0, keepdims=True)
        for j in range(1, 4):
            moved = pltpu.roll(jnp.where(since_tall >= j, tall, 0.0), rows + lead - j, 0)[:rows]
            dx = dx + moved * taps_ref[p, 3 - j:4 - j, :]
            dtaps_ref[p, 3 - j:4 - j, :] += jnp.sum(moved * x, axis=0, keepdims=True)
        out_of_order(step, count, info_ref, dx.astype(bf16), dx_ref, slice(p * LANES, (p + 1) * LANES))


def half_specs(rows, width, steps, order):
    count = rows // PAIR

    def pair(i, info):
        return place_of(order(i) * count, info) // count

    return [
        pl.BlockSpec((rows, width), lambda i, _, info: (jnp.minimum(pair(i, info), steps // 2 - 1), 0)),
        pl.BlockSpec((rows, width), lambda i, _, info: (jnp.maximum(pair(i, info) - steps // 2, 0), 0)),
    ]


def whole_spec(shape):
    return pl.BlockSpec(shape, lambda i, *_: (0,) * len(shape))


def head_forward(near, far, logit, taps, gain, starts, info, rows=512):
    total = 2 * near.shape[0]
    steps = total // rows
    count = rows // PAIR
    per = rows // BLOCK
    chunks = total // PAIR
    flat = lambda width: pl.BlockSpec((rows, width), lambda i, *_: (i, 0))
    square = pl.BlockSpec((per, LANES, LANES), lambda i, *_: (i, 0, 0))
    fine = PAIR // HALO

    def before(i, info):
        return place_of(jnp.maximum(i * count - 1, 0), info)

    s = jax.ShapeDtypeStruct
    outs = pl.pallas_call(
        forward_body,
        grid_spec=pltpu.PrefetchScalarGridSpec(
            num_scalar_prefetch=2,
            grid=(steps,),
            in_specs=[
                *half_specs(rows, 4 * LANES, steps, lambda i: i),
                pl.BlockSpec((HALO, 4 * LANES), lambda i, _, info: (
                    jnp.minimum(before(i, info), chunks // 2 - 1) * fine + fine - 1, 0)),
                pl.BlockSpec((HALO, 4 * LANES), lambda i, _, info: (
                    jnp.maximum(before(i, info) - chunks // 2, 0) * fine + fine - 1, 0)),
                whole_spec(logit.shape),
                whole_spec(taps.shape),
                whole_spec(gain.shape),
            ],
            out_specs=[
                pl.BlockSpec((rows, LANES), lambda i, _, info: (place_of(i * count, info) // count, 0)),
                whole_spec((8, LANES)),
                pl.BlockSpec((3, rows, LANES), lambda i, *_: (0, i, 0)),
                flat(2 * LANES), flat(PAIR), flat(PAIR), flat(LANES),
                square, square, flat(LANES),
            ],
            scratch_shapes=[
                pltpu.VMEM((LANES, LANES), f32), pltpu.VMEM((total // BLOCK, LANES), f32),
                pltpu.VMEM((rows + HALO, 4 * LANES), bf16),
            ],
        ),
        out_shape=[
            s((total, LANES), bf16), s((8, LANES), f32), s((3, total, LANES), f32),
            s((total, 2 * LANES), f32), s((total, PAIR), bf16), s((total, PAIR), bf16), s((total, LANES), bf16),
            s((total // BLOCK, LANES, LANES), f32), s((total // BLOCK, LANES, LANES), bf16),
            s((total, LANES), f32),
        ],
        name="head_forward",
        cost_estimate=pl.CostEstimate(flops=total * 20_000_000, transcendentals=0, bytes_accessed=total * 10_000),
    )(starts, info, near, far, near, far, logit, taps, gain)
    return outs[0], outs[1][0, 0], tuple(outs[2:])


def head_backward(grad_near, grad_far, near, far, logit, taps, gain, starts, info, kept, rows=512):
    total = 2 * near.shape[0]
    steps = total // rows
    count = rows // PAIR
    per = rows // BLOCK
    back = lambda i: steps - 1 - i
    flat = lambda width: pl.BlockSpec((rows, width), lambda i, *_: (back(i), 0))
    square = pl.BlockSpec((per, LANES, LANES), lambda i, *_: (back(i), 0, 0))
    s = jax.ShapeDtypeStruct
    return pl.pallas_call(
        backward_body,
        grid_spec=pltpu.PrefetchScalarGridSpec(
            num_scalar_prefetch=2,
            grid=(steps,),
            in_specs=[
                *half_specs(rows, 4 * LANES, steps, back),
                whole_spec(logit.shape), whole_spec(taps.shape), whole_spec(gain.shape),
                *half_specs(rows, LANES, steps, back),
                pl.BlockSpec((3, rows, LANES), lambda i, *_: (0, back(i), 0)),
                flat(2 * LANES), flat(PAIR), flat(PAIR), flat(LANES), square, square, flat(LANES),
            ],
            out_specs=[
                pl.BlockSpec((rows, 4 * LANES), lambda i, _, info: (place_of(back(i) * count, info) // count, 0)),
                whole_spec(logit.shape), whole_spec(taps.shape), whole_spec((8, LANES)),
            ],
            scratch_shapes=[
                pltpu.VMEM((LANES, LANES), f32), pltpu.VMEM((3, 8, LANES), f32),
                pltpu.VMEM((rows, 4 * LANES), bf16), pltpu.VMEM((rows, LANES), bf16),
            ],
        ),
        out_shape=[s((total, 4 * LANES), bf16), s(logit.shape, f32), s(taps.shape, f32), s((8, LANES), f32)],
        name="head_backward",
        cost_estimate=pl.CostEstimate(flops=total * 12_000_000, transcendentals=0, bytes_accessed=total * 10_000),
    )(starts, info, near, far, logit, taps, gain, grad_near, grad_far, *kept)


def other(value, axis, bit):
    size = lax.axis_size(axis)
    return lax.ppermute(value, axis, [(i, i ^ bit) for i in range(size)])


def after(value, *done):
    return lax.optimization_barrier((value, *done))[0]


def own_order(value, index, axis, parts=4):
    size = value.shape[axis] // parts
    return jnp.concatenate(
        [lax.dynamic_slice_in_dim(value, (p ^ index) * size, size, axis) for p in range(parts)], axis
    )


def neighbour_order(value, axis, bit, parts=4):
    size = value.shape[axis] // parts
    return jnp.concatenate(
        [lax.slice_in_dim(value, (p ^ bit) * size, ((p ^ bit) + 1) * size, axis=axis) for p in range(parts)], axis
    )


def matmul(a, b, dims=((1,), (0,))):
    return lax.dot_general(a, b, (dims, ((), ())), preferred_element_type=f32)


def norm_rows(values, gain):
    scale = lax.rsqrt(jnp.mean(values * values, axis=-1, keepdims=True) + 1e-05)
    unit = values * scale
    return unit * gain, unit, scale


def norm_back(grad, unit, scale, gain):
    pulled = grad * gain
    inner = jnp.mean(pulled * unit, axis=-1, keepdims=True)
    return scale * (pulled - unit * inner), jnp.sum(grad * unit, axis=0)


def tensor_tree():
    return lax.axis_size("tensor") == 4


def inner_place():
    index = lax.axis_index("tensor")
    return (index == 1) | (index == 2)


def along_tensor(value, pairs):
    return lax.ppermute(value, "tensor", pairs)


def gather_tensor(value, tree=True, before=()):
    if not tree or not tensor_tree():
        return [value] + [other(value, "tensor", s) for s in range(1, lax.axis_size("tensor"))]
    two = after(other(value, "tensor", 2), *before)
    one = other(value, "tensor", 1)
    passed = along_tensor(two, [(2, 3), (1, 0)])
    middle = along_tensor(after(value, one), [(1, 2), (2, 1)])
    return [value, one, two, jnp.where(inner_place(), middle, passed)]


def with_core(mine, theirs=()):
    came = list(theirs) + [other(v, "mp", 1) for v in mine[len(theirs):]]
    return jnp.concatenate(mine + [neighbour_order(v, 1, 1) for v in came], axis=0)


def spread(values):
    return with_core(gather_tensor(values))


def partials(rows, body):
    return body(rows // 2, rows).astype(bf16), body(0, rows // 2)


def collect_pieces(parts, before=()):
    theirs, mine = parts
    ways = lax.axis_size("tensor")
    piece = mine.shape[0] // ways
    if not tensor_tree():
        joined = mine + neighbour_order(other(theirs, "mp", 1), 1, 1).astype(f32)
        sent = [joined[s * piece:(s + 1) * piece].astype(bf16) for s in range(1, ways)]
        return joined[:piece], [other(v, "tensor", s + 1) for s, v in enumerate(sent)], sent
    last = (ways - 1) * piece
    tail = mine[last:] + neighbour_order(other(theirs[last:], "mp", 1), 1, 1).astype(f32)
    rest = mine[:last] + neighbour_order(other(theirs[:last], "mp", 1), 1, 1).astype(f32)
    low = tail.astype(bf16)
    passed = along_tensor(low, [(3, 2), (0, 1)])
    middle = along_tensor(low, [(1, 2), (2, 1)])
    sent = [(rest[2 * piece:] + passed.astype(f32)).astype(bf16), rest[piece:2 * piece].astype(bf16)]
    sent = list(after(sent, middle, *before))
    return rest[:piece], [middle, other(sent[0], "tensor", 2), other(sent[1], "tensor", 1)], sent


def added(own, received):
    for v in received:
        own = own + v.astype(f32)
    return own


def over_dp_pieces(value):
    bit = 1
    low = value.astype(bf16)
    came = other(low, "dp", bit)
    while 2 * bit < lax.axis_size("dp"):
        bit *= 2
        low = (low.astype(f32) + came.astype(f32)).astype(bf16)
        came = other(low, "dp", bit)
    return low, came


def summed(low, came):
    return low.astype(f32) + came.astype(f32)


def over_all(value):
    for axis in ("mp", "tensor"):
        if lax.axis_size(axis) == 4:
            one, two, three = [other(value, axis, bit) for bit in (1, 2, 3)]
            value = (value + one) + (two + three)
        else:
            bit = 1
            while bit < lax.axis_size(axis):
                value = value + other(value, axis, bit)
                bit *= 2
    bit = 1
    while bit < lax.axis_size("dp"):
        value = value + other(value, "dp", bit)
        bit *= 2
    return value


def shards(
    tokens,
    norm_gain,
    w_proj,
    w_beta,
    conv_weight,
    out_gain,
    w_out,
    mlp_gain,
    w_in,
    w_down,
    cotangent,
    starts,
    lengths,
):
    assert lax.axis_size("mp") == 4 and starts.shape[0] == 1
    m = lax.axis_index("mp")
    core = m & 1
    place = m * lax.axis_size("tensor") + lax.axis_index("tensor")
    block = w_proj.shape[1]
    near_blocks = 2 * block

    pieces, _, wide = w_proj.shape
    head = wide // 4
    span = pieces * head
    pair = lambda values, i, j, axis: jnp.concatenate([values[i], values[j]], axis)
    proj_got = other(w_proj, "mp", 2)
    beta_mine = w_beta.T
    beta_got = other(beta_mine, "mp", 2)
    scaled = own_order(norm_rows(tokens.astype(f32), norm_gain)[0].astype(bf16), m, 1)
    normed = spread(scaled)
    inputs = own_order(after(tokens, normed), m, 1).astype(f32)
    gain_one = own_order(norm_gain, m, 0)
    gain_two = own_order(mlp_gain, m, 0)
    _, unit_one, scale_one = norm_rows(inputs, gain_one)

    def head_blocks(v):
        return [
            lax.dynamic_slice_in_dim(v, (j ^ m) * head, head, 2).transpose(1, 0, 2).reshape(block, span)
            for j in range(4)
        ]

    proj_mine, proj_far = head_blocks(w_proj), head_blocks(proj_got)
    proj_low = jnp.concatenate([pair(proj_mine, 0, 2, 1), other(pair(proj_mine, 1, 3, 1), "mp", 1)], axis=0)
    proj_high = jnp.concatenate([pair(proj_far, 0, 2, 1), other(pair(proj_far, 1, 3, 1), "mp", 1)], axis=0)
    beta_both = jnp.concatenate([beta_mine, after(beta_got, proj_got)], axis=1)
    beta_all = own_order(jnp.concatenate([beta_both, other(beta_both, "mp", 1)], axis=1), m, 0)
    beta_all = pair([beta_all[0:1], beta_all[2:3]], 0, 1, 0)
    full_beta = jnp.concatenate([beta_all[:, p * block:(p + 1) * block] for p in (0, 2, 1, 3)], axis=1)
    logits = matmul(full_beta, normed, ((1,), (1,))).astype(bf16)
    normed_low, normed_high = normed[:, :near_blocks], normed[:, near_blocks:]
    far_out = (matmul(normed_low, proj_low[:, span:]) + matmul(normed_high, proj_high[:, span:])).astype(bf16)
    count = far_out.shape[0]
    logit_rows = count // span
    far_sent = jnp.concatenate([far_out, jnp.pad(logits[1].reshape(logit_rows, span), ((0, HALO - logit_rows), (0, 0)))], 0)
    units = w_down.shape[0]
    half = LANES * ((units // LANES + 1) // 2)
    ours = lambda v, axis: lax.dynamic_slice_in_dim(v, core * (units - half), half, axis)
    theirs = lambda v, axis: lax.dynamic_slice_in_dim(v, (1 - core) * (units - half), half, axis)
    cot_own = own_order(cotangent, m, 1)
    early = after((theirs(w_down, 0), theirs(w_in, 2), cot_own), far_sent)
    down_core, in_core, cot_core = [other(v, "mp", 1) for v in early]
    full_proj = jnp.concatenate(after((proj_low, proj_high), far_sent), axis=0)
    far = after(other(far_sent, "mp", 2), down_core, in_core, cot_core, full_proj)
    near_low, near_high = after((normed_low, normed_high), far_sent)
    near = (matmul(near_low, proj_low[:, :span]) + matmul(near_high, proj_high[:, :span])).astype(bf16)
    chunk_rows = (-1, LANES)
    logit = jnp.concatenate(
        [logits[0].reshape(chunk_rows), far[count:count + logit_rows].reshape(chunk_rows)], axis=0
    ).astype(f32)

    live = (lax.broadcasted_iota(jnp.int32, (1, half), 1) >= core * (2 * half - units)).astype(f32)
    out_blocks = lambda v: [lax.dynamic_slice_in_dim(v, (j ^ m) * head, head, 0) for j in range(4)]
    rows_sent = after(jnp.concatenate([w_out, w_down], axis=0), far)
    rows_got = other(rows_sent, "mp", 2)
    cot_pieces = gather_tensor(after(cot_own, far), tree=False)

    taps = conv_weight.reshape(3, conv_weight.shape[1], head)
    info = jnp.stack([lengths[0], place]).astype(jnp.int32)
    head_args = (near, far, logit, taps, out_gain[None], starts[0], info)
    mixed, norm_total, kept = head_forward(*head_args)
    mixed = after(mixed, rows_got, *cot_pieces)
    mixed_far = other(mixed[count:], "mp", 2)
    out_mine, out_far = out_blocks(w_out), out_blocks(rows_got[: w_out.shape[0]])
    out_sent = jnp.concatenate([pair(out_mine, 1, 3, 0), pair(out_far, 1, 3, 0)], axis=1)
    out_core = other(after(out_sent, mixed), "mp", 1)
    full_out = jnp.concatenate(
        [pair(out_mine, 0, 2, 0), out_core[:, :block], pair(out_far, 0, 2, 0), out_core[:, block:]], axis=1
    )
    mixed_tok = jnp.concatenate([mixed[:count], mixed_far], axis=1)
    branch_parts = partials(count, lambda a, b: matmul(mixed_tok[a:b], full_out))
    gate_first = other(after(w_in[0, : block // 2], mixed_far), "mp", 2)
    gate_second = other(after(w_in[0, block // 2:], mixed_far), "mp", 2)
    branch_own, branch_got, branch_sent = collect_pieces(branch_parts, before=(gate_first,))
    branch = added(branch_own, branch_got)
    up_far = other(after(w_in[1], branch_sent), "mp", 2)

    middle = inputs + branch
    scaled_two, unit_two, scale_two = norm_rows(middle, gain_two)
    low_two = after(scaled_two.astype(bf16), gate_second)
    down_far = after(rows_got, low_two)[w_out.shape[0]:]
    down_across = other(theirs(down_far, 0), "mp", 1)
    cot_across = other(after(jnp.concatenate(cot_pieces[1:], axis=0), low_two), "mp", 1)
    piece = cot_own.shape[0]
    theirs_cot = [cot_core] + [cot_across[s * piece:(s + 1) * piece] for s in range(len(cot_pieces) - 1)]
    cot_all = with_core(cot_pieces, theirs_cot)
    full_down = jnp.concatenate([ours(w_down, 0), down_core, ours(down_far, 0), down_across], axis=1)
    d_hidden = matmul(cot_all, full_down, ((1,), (1,)))
    two_pieces = gather_tensor(low_two, before=(up_far,))
    normed_two = after(with_core(two_pieces), d_hidden)
    gate_far = jnp.concatenate([after(gate_first, low_two), after(gate_second, low_two)], axis=0)
    in_far = [gate_far, after(up_far, two_pieces[2])]
    full_in = [
        after(
            jnp.concatenate([ours(w_in[i], 1), in_core[i], ours(v, 1), other(theirs(v, 1), "mp", 1)], axis=0), d_hidden
        )
        for i, v in enumerate(in_far)
    ]

    gate = matmul(normed_two, full_in[0])
    up = matmul(normed_two, full_in[1])
    sigma = jax.nn.sigmoid(gate)
    activated = gate * sigma
    hidden = (activated * up * live).astype(bf16)
    d_hidden = d_hidden * live
    d_gate = (d_hidden * up * sigma * (1.0 + gate * (1.0 - sigma))).astype(bf16)
    d_up = (d_hidden * activated).astype(bf16)
    two_parts = partials(
        count,
        lambda a, b: matmul(d_gate[a:b], full_in[0], ((1,), (1,))) + matmul(d_up[a:b], full_in[1], ((1,), (1,))),
    )
    two_own, two_got, two_sent = collect_pieces(two_parts)
    hidden, d_gate, d_up = after((hidden, d_gate, d_up), two_sent)
    tn = ((0,), (0,))
    grad_dot = lambda a, b: matmul(a, b, tn)

    def joined_units(mine, theirs, axis):
        gap = units - half
        low = jnp.where(core == 0, mine, theirs)
        high = jnp.where(core == 0, theirs, mine)
        zero = jnp.zeros_like(lax.slice_in_dim(low, 0, gap, axis=axis))
        return jnp.concatenate([low, zero], axis) + jnp.concatenate([zero, high], axis)

    def units_joined(product, axis):
        cut = lambda v, p: lax.slice_in_dim(v, p * block, (p + 1) * block, axis=axis)
        two = lambda i, j: jnp.concatenate([cut(product, i), cut(product, j)], axis)
        joined = joined_units(two(0, 2), other(two(1, 3), "mp", 1), 1 - axis)
        return cut(joined, 0), cut(joined, 1)

    down_product = grad_dot(hidden, cot_all).astype(bf16)
    gate_product = grad_dot(normed_two, after(d_gate, down_product)).astype(bf16)
    down_held, down_sent = units_joined(down_product, 1)
    up_product = grad_dot(normed_two, after(d_up, gate_product, down_sent)).astype(bf16)
    gate_held, gate_sent = units_joined(gate_product, 0)
    up_held, up_sent = units_joined(up_product, 0)
    down_got = other(down_sent, "mp", 2)

    d_normed_two = added(after(two_own, down_sent), two_got)
    d_mid_norm, g_mlp = norm_back(d_normed_two, unit_two, scale_two, gain_two)
    d_middle = cot_own.astype(f32) + d_mid_norm
    d_mid_low = after(d_middle.astype(bf16), down_sent, gate_sent)
    d_mid_pieces = gather_tensor(d_mid_low)
    gate_got = other(after(gate_sent, d_mid_pieces[2]), "mp", 2)
    down_sums = over_dp_pieces(summed(down_held, after(down_got, d_mid_pieces[2])))
    feed_parts = partials(count, lambda a, b: matmul(hidden[a:b], full_down))
    feed_theirs = other(after(feed_parts[0], d_mid_pieces[2]), "mp", 1)
    feed_joined = feed_parts[1] + neighbour_order(feed_theirs, 1, 1).astype(f32)
    piece_rows = feed_joined.shape[0] // lax.axis_size("tensor")
    feed_sent = [
        feed_joined[p * piece_rows:(p + 1) * piece_rows].astype(bf16) for p in range(1, lax.axis_size("tensor"))
    ]
    d_mid_all = after(with_core(d_mid_pieces), down_got, feed_sent)
    d_mixed = matmul(d_mid_all, full_out, ((1,), (1,))).astype(bf16)
    d_far = other(d_mixed[:, head:], "mp", 2)
    gate_sums = over_dp_pieces(summed(gate_held, after(gate_got, down_sums[1], d_far)))
    feed_got = [other(after(v, d_mid_all), "tensor", p + 1) for p, v in enumerate(feed_sent)]
    feed_own = feed_joined[:piece_rows]
    output = own_order((middle + added(feed_own, feed_got)).astype(bf16), m, 1)

    out_grad = grad_dot(mixed_tok, d_mid_all)
    out_sent = out_grad[:, near_blocks:].astype(bf16)
    up_got = other(after(up_sent, d_far), "mp", 2)
    d_near = after(d_mixed[:, :head], gate_got, down_sums[1])
    d_heads, d_logit, d_taps, g_head_gain = head_backward(d_near, d_far, *head_args, kept)
    d_heads, d_logit = after((d_heads, d_logit), up_got, gate_sums[1], *feed_got)
    d_own = d_heads[:count]
    d_logit = d_logit.astype(bf16)
    half_chunks = d_logit.shape[0] // 2
    d_sent = jnp.concatenate(
        [
            d_heads[count:],
            jnp.pad(d_logit[half_chunks:].reshape(logit_rows, span), ((0, HALO - logit_rows), (0, 0))),
        ],
        axis=0,
    )
    d_got = other(d_sent, "mp", 2)
    d_proj = jnp.concatenate([d_own, d_got[:count]], axis=1)
    d_logits = jnp.concatenate(
        [d_logit[:half_chunks].reshape(1, count), d_got[count:count + logit_rows].reshape(1, count)], axis=0
    )
    up_sums = over_dp_pieces(summed(up_held, after(up_got, d_sent)))
    out_got = other(after(out_sent, d_sent), "mp", 2)
    normed_parts = partials(
        count,
        lambda a, b: matmul(d_proj[a:b], full_proj, ((1,), (1,))) + matmul(d_logits[:, a:b], full_beta, tn),
    )
    normed_own, normed_got, normed_sent = collect_pieces(normed_parts)
    out_got = after(out_got, normed_parts)
    out_two = (out_grad[:, :near_blocks] + neighbour_order(out_got, 0, 1, 2).astype(f32)).astype(bf16)
    out_theirs = other(out_two[:, block:], "mp", 1)
    out_mine = out_two[:, :block]
    out_rows = jnp.concatenate([out_mine[:head], out_theirs[:head], out_mine[head:], out_theirs[head:]], axis=0)
    out_sums = over_dp_pieces(out_rows)
    own_grad = grad_dot(normed, after(d_own, d_sent))
    far_grad = grad_dot(normed, after(d_got, normed_parts)[:count])
    own_back = other(own_grad[near_blocks:].astype(bf16), "mp", 2)
    far_back = other(after(far_grad[near_blocks:].astype(bf16), normed_sent), "mp", 2)

    def proj_part(held, back):
        two = (held[:near_blocks] + back.astype(f32)).astype(bf16)
        return jnp.concatenate([two[:block], other(two[block:], "mp", 1)], axis=1)

    far_part = after(proj_part(far_grad, after(own_back, normed_sent)), up_sums[1], out_sums[1])
    far_sums = over_dp_pieces(far_part)
    down_sums, gate_sums = after((down_sums, gate_sums), far_part)
    g_down = summed(*down_sums)
    up_sums, out_sums = after((up_sums, out_sums), far_part)
    g_in = jnp.stack([summed(*gate_sums), summed(*up_sums)])
    g_out = own_order(summed(*out_sums), m, 0)
    normed_again, partial_rows = after((normed, normed_parts), far_part)
    g_norm = (
        jnp.sum(normed_again[: count // 2].astype(f32) * partial_rows[1], axis=0)
        + jnp.sum(normed_again[count // 2:].astype(f32) * partial_rows[0].astype(f32), axis=0)
    ) / gain_one
    row = lambda v: v.reshape(-1, LANES)
    rows_all = [own_order(row(g_norm), m, 0), own_order(row(g_mlp), m, 0), g_head_gain[:1]]
    rows_all.append(jnp.full((1, LANES), norm_total))
    rows_here = jnp.concatenate(rows_all, axis=0)
    beta_here = matmul(after(d_logits, far_part), normed)
    d_normed = added(after(normed_own, g_down, g_in, g_out, rows_here, beta_here), normed_got)
    own_part = proj_part(own_grad, after(far_back, normed_got))
    own_sums = over_dp_pieces(own_part)
    part_far, part_own = summed(*far_sums), summed(*own_sums)
    g_heads = [part_own[:, :span], part_own[:, span:], part_far[:, :span], part_far[:, span:]]
    g_proj = own_order(
        jnp.concatenate([v.reshape(block, pieces, head).transpose(1, 0, 2) for v in g_heads], axis=2), m, 2
    )
    beta_part = after(beta_here, far_sums[1], own_part)
    beta_back = neighbour_order(neighbour_order(other(beta_part, "mp", 2), 0, 1, 2), 1, 1, 2)
    beta_two = beta_part + beta_back
    beta_theirs = other(beta_two[:, block:near_blocks], "mp", 1)
    g_beta = own_order(
        jnp.concatenate([beta_two[:1, :block], beta_theirs[:1], beta_two[1:, :block], beta_theirs[1:]], axis=0), m, 0
    )
    small = jnp.concatenate([g_beta.reshape(-1, LANES), d_taps.reshape(-1, LANES)], axis=0)
    bit = 1
    while bit < lax.axis_size("dp"):
        small = small + other(small, "dp", bit)
        bit *= 2
    cut = g_beta.size // LANES
    g_beta = small[:cut].reshape(g_beta.shape)
    d_taps = small[cut:]
    sums = over_all(after(rows_here, far_sums[1], own_part))
    d_in_norm, _ = norm_back(d_normed, unit_one, scale_one, gain_one)
    d_tokens = own_order(d_middle + d_in_norm, m, 1)
    lines = g_norm.shape[0] // LANES
    ways = lax.axis_size("mp") * lax.axis_size("tensor")
    state_norm = sums[2 * lines + 1, 0] / (ways * lax.axis_size("dp") * (2 * count // BLOCK))
    return (
        output,
        d_tokens,
        sums[:lines].reshape(-1),
        g_proj,
        g_beta.T,
        d_taps.reshape(conv_weight.shape),
        sums[2 * lines],
        g_out,
        sums[lines:2 * lines].reshape(-1),
        g_in,
        g_down,
        state_norm,
    )


def solution(mesh):
    placed = (
        P(("dp", "mp", "tensor"), None),
        P(),
        P(None, "mp", "tensor"),
        P("mp", "tensor"),
        P(None, None, "tensor", "mp", None),
        P(),
        P("tensor", "mp"),
        P(),
        P(None, "mp", "tensor"),
        P("tensor", "mp"),
        P(("dp", "mp", "tensor"), None),
        P("dp", None),
        P("dp"),
    )
    return jax.shard_map(
        shards,
        mesh=mesh,
        in_specs=placed,
        out_specs=(
            P(("dp", "mp", "tensor"), None),
            P(("dp", "mp", "tensor"), None),
            P(),
            P(None, "mp", "tensor"),
            P("mp", "tensor"),
            P(None, None, "tensor", "mp", None),
            P(),
            P("tensor", "mp"),
            P(),
            P(None, "mp", "tensor"),
            P("tensor", "mp"),
            P(),
        ),
        check_vma=False,
    )
```
